32 devices in a mesh: dp: 4 (over y, x), ctx: 4 (over z), head: 2 (over core).
Axes of the slice: x: 2, y: 2, z: 4, core: 2. Of those that a mesh axis runs over, the one named last changes fastest.
Arguments:
- inputs: bfloat16 [4, 512, 2048], P('dp', 'ctx', 'head'), may hold values from -1.5 to 1.5
- dt_raw: float32 [4, 512, 32], P('dp', 'ctx', 'head'), may hold values from -4 to 4
- dt_bias: float32 [32], P('head'), may hold values from -1 to 1
- a_log: float32 [32], P('head'), may hold values from -30 to -2.8
- b_in: bfloat16 [4, 512, 128], P('dp', 'ctx'), may hold values from -0.13183594 to 0.13183594
- c_in: bfloat16 [4, 512, 128], P('dp', 'ctx'), may hold values from -0.13183594 to 0.13183594
- skip_gain: float32 [32], P('head'), may hold values from 0.5 to 1.5
- grad_out: bfloat16 [4, 512, 2048], P('dp', 'ctx', 'head'), may hold values from -1.5 to 1.5
- doc_lengths: int32 [4, 4], P('dp'), may hold values from 1 to 256, 512 in all within a row
Outputs:
- grad_inputs: bfloat16 [4, 512, 2048], P('dp', 'ctx', 'head')
- grad_dt_raw: float32 [4, 512, 32], P('dp', 'ctx', 'head')
- grad_b: float32 [4, 512, 128], P('dp', 'ctx')
- grad_c: float32 [4, 512, 128], P('dp', 'ctx')
- grad_a_log: float32 [32], P('head')
- grad_dt_bias: float32 [32], P('head')
- grad_skip: float32 [32], P('head')
The draws below stay inside these ranges and needn't reach their ends.
Inputs may be any that keep to these rules, and one draw needn't show every extreme that they name: `doc_lengths`: each row lists 4 document lengths laid end to end from the sequence's first position; they sum to 512, and the longest is exactly half of 512.
All inputs are finite; a program needn't handle non-finite values.
Results may differ from the reference program's by a relative error of at most 0.007.
Values sent between devices are 32-bit elements; how exact they have to be, the bound alone decides.
No kernel may reach another device: no remote copies, remote signals or barrier semaphores. Data moves between devices by JAX's collectives and lax.ppermute only.
A program may use at most 64 MiB of HBM per device.

```python
import math
import jax
import jax.numpy as jnp
import numpy as np
from jax import lax

HEADS = 32
HEAD_P = 64
STATE = 128
SPAN = 128
DOCS = 4
LENGTH = 512
SEQS = 4


def draw_a_log(key, part):
    pick_key = jax.random.fold_in(key, 11)
    fast_key = jax.random.fold_in(key, 23)
    slow_key = jax.random.fold_in(key, 37)
    pick = jax.random.uniform(pick_key, (HEADS,), jnp.float32)
    fast_rate = jnp.exp(jax.random.uniform(fast_key, (HEADS,), jnp.float32, jnp.log(0.02), jnp.log(0.06)))
    slow_rate = jnp.exp(jax.random.uniform(slow_key, (HEADS,), jnp.float32, jnp.log(0.25), jnp.log(2.0))) / LENGTH
    share = 0.5
    chosen = jnp.where(pick < share, fast_rate, slow_rate)
    return jnp.log(chosen).astype(jnp.float32)


def draw_dt_raw(key, part):
    base_key = jax.random.fold_in(key, 41)
    block_key = jax.random.fold_in(key, 53)
    block_count = LENGTH // SPAN
    offset = jax.random.uniform(block_key, (SEQS, block_count, 1, HEADS), jnp.float32, -1.5, 1.5)
    base = jax.random.normal(base_key, (SEQS, block_count, SPAN, HEADS), jnp.float32)
    values = jnp.clip(base + offset, -4.0, 4.0)
    return values.reshape(SEQS, LENGTH, HEADS).astype(jnp.float32)


def steps_of(stream_key, extent, shards, least, largest):
    def one(position, blocks):
        draws = jax.random.uniform(jax.random.fold_in(jax.random.fold_in(stream_key, 6), position), (blocks,), jnp.float32, least / len(shards), largest / len(shards))
        return jnp.repeat(jnp.exp(draws), extent[position] // blocks).reshape((-1,) + (1,) * (len(extent) - position - 1))

    level = one(*shards[0])
    for cut in shards[1:]:
        level = level * one(*cut)
    return level


def profile(count, total, bound, skew):
    weights = [(1 << 20) // math.isqrt(grade ** skew) + 1 for grade in range(2, count + 1)]
    rest, holding = total - bound - (count - 1), [1] * (count - 1)
    while rest > 0:
        candidates = [i for i in range(count - 1) if holding[i] < bound]
        whole, remaining = sum([weights[i] for i in candidates]), rest
        for i in candidates:
            more = min(bound - holding[i], max(1, remaining * weights[i] // whole), rest)
            holding[i] = holding[i] + more
            rest = rest - more
    return np.array([bound] + holding)


def ragged(stream_key, amount, total, bound, skew):
    if amount == 2:
        one = jax.random.randint(stream_key, (), max(1, total - bound), min(bound, total - 1) + 1)
        return jnp.stack([one, total - one])
    lengths = jnp.asarray(profile(amount, total, bound, skew), jnp.int32)
    couples = (amount - 1) // 2
    source_of, receiver = lengths[1:1 + 2 * couples:2], lengths[2:2 + 2 * couples:2]
    slack = jnp.minimum(source_of - 1, bound - receiver)
    moved = jax.random.randint(jax.random.fold_in(stream_key, 1), (couples,), 0, 1 << 20) % (slack + 1)
    lengths = lengths.at[1:1 + 2 * couples:2].set(source_of - moved).at[2:2 + 2 * couples:2].set(receiver + moved)
    return lengths[jax.random.permutation(jax.random.fold_in(stream_key, 2), amount)]


def gaussian(key, dims, width, reach, cuts=(), kind=jnp.bfloat16):
    gain = steps_of(key, dims, cuts, -0.22, 0.18) if cuts else 1.0
    result = jax.random.normal(key, dims, jnp.float32) * width * gain
    return jnp.minimum(jnp.maximum(result, -reach), reach).astype(kind)


def setup_inputs(seed: int = 0) -> dict:
    key_of = jax.random.split(jax.random.key(seed), 10)
    inputs = gaussian(key_of[0], (SEQS, LENGTH, HEADS * HEAD_P), 0.25, 1.5, ((0, 4), (1, 4), (2, 2)))
    dt_raw = draw_dt_raw(jax.random.fold_in(key_of[9], 71), 0)
    dt_bias = jnp.clip(jax.random.uniform(key_of[2], (HEADS,), jnp.float32, -1.0, 1.0) * steps_of(key_of[2], (HEADS,), ((0, 2),), -0.4, 0.0), -1.0, 1.0)
    a_log = draw_a_log(jax.random.fold_in(key_of[9], 71), 0)
    b_in = gaussian(key_of[4], (SEQS, LENGTH, STATE), (0.25 * STATE ** -0.5), 0.13183594, ((0, 4), (1, 4)))
    c_in = gaussian(key_of[5], (SEQS, LENGTH, STATE), (0.25 * STATE ** -0.5), 0.13183594, ((0, 4), (1, 4)))
    skip_gain = jnp.clip(0.5 + 1.0 * jax.random.uniform(key_of[6], (HEADS,), jnp.float32) ** steps_of(key_of[6], (HEADS,), ((0, 2),), -0.2, 0.2), 0.5, 1.5)
    grad_out = gaussian(key_of[7], (SEQS, LENGTH, HEADS * HEAD_P), 0.25, 1.5, ((0, 4), (1, 4), (2, 2)))
    doc_lengths = jax.vmap(lambda own: ragged(own, DOCS, LENGTH, LENGTH // 2, 2))(jax.random.split(key_of[8], SEQS)).reshape((SEQS, DOCS)).astype(jnp.int32)
    return {"inputs": inputs, "dt_raw": dt_raw, "dt_bias": dt_bias, "a_log": a_log, "b_in": b_in, "c_in": c_in, "skip_gain": skip_gain, "grad_out": grad_out, "doc_lengths": doc_lengths}


def reverse_cumsum(values, along_axis):
    return jnp.flip(jnp.cumsum(jnp.flip(values, along_axis), axis=along_axis), along_axis)


def vector_factors(decay_block, segment_block, previous_block):
    cumulative = jnp.cumsum(decay_block, axis=0)
    last_segment = segment_block[-1]
    mask_in = (segment_block == previous_block).astype(jnp.float32)
    mask_out = (segment_block == last_segment).astype(jnp.float32)
    factor_in = mask_in[:, None] * jnp.exp(cumulative)
    factor_out = mask_out[:, None] * jnp.exp(cumulative[-1][None, :] - cumulative)
    span_total = (last_segment == previous_block).astype(jnp.float32) * jnp.exp(cumulative[-1])
    return cumulative, mask_in, mask_out, factor_in, factor_out, span_total


def pair_factor(cumulative, segment_block):
    local_pos = jnp.arange(segment_block.shape[0], dtype=jnp.int32)
    allowed = (local_pos[:, None] >= local_pos[None, :]) & (segment_block[:, None] == segment_block[None, :])
    spread = cumulative.T[:, :, None] - cumulative.T[:, None, :]
    return jnp.where(allowed[None], jnp.exp(jnp.where(allowed[None], spread, 0.0)), 0.0)


def state_terms(inputs_block, grads_block, b_block, c_block, step_block, factor_in, factor_out):
    scaled_in = (inputs_block.astype(jnp.float32) * (factor_out * step_block)[:, :, None]).astype(jnp.bfloat16)
    scaled_grad = (grads_block.astype(jnp.float32) * factor_in[:, :, None]).astype(jnp.bfloat16)
    state_part = jnp.einsum("shp,sn->hpn", scaled_in.astype(jnp.float32), b_block.astype(jnp.float32))
    grad_part = jnp.einsum("uhp,un->hpn", scaled_grad.astype(jnp.float32), c_block.astype(jnp.float32))
    return state_part, grad_part


def first_pass(pieces):
    inputs_block, grads_block, b_block, c_block, step_block, decay_block, segment_block, previous_block, preact_block = pieces
    cumulative, mask_in, mask_out, factor_in, factor_out, span_total = vector_factors(decay_block, segment_block, previous_block)
    state_part, grad_part = state_terms(inputs_block, grads_block, b_block, c_block, step_block, factor_in, factor_out)
    return span_total, state_part, grad_part


def span_grads(inputs_block, grads_block, b_block, c_block, step_block, decay_block, segment_block, previous_block, preact_block, state_in, state_grad, decay_rate, skip_gain):
    cumulative, mask_in, mask_out, factor_in, factor_out, span_total = vector_factors(decay_block, segment_block, previous_block)
    pair_decay = pair_factor(cumulative, segment_block)
    inputs_wide = inputs_block.astype(jnp.float32)
    grads_wide = grads_block.astype(jnp.float32)
    b_wide = b_block.astype(jnp.float32)
    c_wide = c_block.astype(jnp.float32)
    scores = jnp.einsum("un,sn->us", c_wide, b_wide)
    cross_term = jnp.einsum("uhp,shp->hus", grads_wide, inputs_wide)
    masked = (pair_decay * scores[None]).astype(jnp.bfloat16)
    weighted = pair_decay * cross_term * step_block.T[:, None, :]
    summed = jnp.sum(weighted, axis=0).astype(jnp.bfloat16)
    products = weighted * scores[None]
    change = jnp.sum(products, axis=2) - jnp.sum(products, axis=1)
    first_term = reverse_cumsum(change, 1).T
    h_low = state_in.astype(jnp.bfloat16).astype(jnp.float32)
    e_low = state_grad.astype(jnp.bfloat16).astype(jnp.float32)
    along_b = jnp.einsum("tn,hpn->thp", b_wide, e_low)
    grad_b_prod = jnp.einsum("hut,uhp->thp", masked.astype(jnp.float32), grads_wide) + factor_out[:, :, None] * along_b
    grad_x = (step_block[:, :, None] * grad_b_prod + skip_gain[None, :, None] * grads_wide).astype(jnp.bfloat16)
    x_state = jnp.einsum("thp,hpn->thn", inputs_wide, e_low)
    y_state = jnp.einsum("uhp,hpn->uhn", grads_wide, h_low)
    summed_wide = summed.astype(jnp.float32)
    grad_b = jnp.einsum("us,un->sn", summed_wide, c_wide) + jnp.sum((step_block * factor_out)[:, :, None] * x_state, axis=1)
    grad_c = jnp.einsum("us,sn->un", summed_wide, b_wide) + jnp.sum(factor_in[:, :, None] * y_state, axis=1)
    z_term = jnp.sum(y_state * c_wide[:, None, :], axis=2)
    w_term = step_block * jnp.sum(x_state * b_wide[:, None, :], axis=2)
    second_term = mask_in[:, None] * reverse_cumsum(factor_in * z_term, 0)
    carried = factor_out * w_term
    third_term = mask_out[:, None] * (jnp.cumsum(carried, axis=0) - carried)
    fourth_term = factor_out * factor_in * jnp.sum(state_grad * state_in, axis=(1, 2))[None, :]
    decay_grad = first_term + second_term + third_term + fourth_term
    x_dot_g = jnp.sum(inputs_wide * grad_b_prod, axis=2)
    grad_dt = (x_dot_g + decay_rate[None, :] * decay_grad) * jax.nn.sigmoid(preact_block)
    grad_alog = jnp.sum(decay_grad * step_block, axis=0) * decay_rate
    grad_bias = jnp.sum(grad_dt, axis=0)
    grad_skip = jnp.einsum("thp,thp->h", grads_wide, inputs_wide)
    return grad_x, grad_dt, grad_b, grad_c, grad_alog, grad_bias, grad_skip


def chain_link(running, pieces):
    span_total, span_part = pieces
    return span_total[:, None, None] * running + span_part, running


def sequence_grads(inputs, dt_raw, b_in, c_in, grad_out, doc_lengths, dt_bias, a_log, skip_gain):
    span_count = LENGTH // SPAN
    preact = dt_raw + dt_bias[None, :]
    step_size = jax.nn.softplus(preact)
    decay_rate = -jnp.exp(a_log)
    log_decay = step_size * decay_rate[None, :]
    starts = jnp.cumsum(doc_lengths) - doc_lengths
    positions = jnp.arange(LENGTH, dtype=jnp.int32)
    segment = jnp.sum((starts[None, :] <= positions[:, None]).astype(jnp.int32), axis=1)
    previous = jnp.concatenate([jnp.zeros((1,), jnp.int32), segment[:-1]])[::SPAN]
    shaped = (inputs.reshape(span_count, SPAN, HEADS, HEAD_P),
              grad_out.reshape(span_count, SPAN, HEADS, HEAD_P),
              b_in.reshape(span_count, SPAN, STATE),
              c_in.reshape(span_count, SPAN, STATE),
              step_size.reshape(span_count, SPAN, HEADS),
              log_decay.reshape(span_count, SPAN, HEADS),
              segment.reshape(span_count, SPAN),
              previous,
              preact.reshape(span_count, SPAN, HEADS))
    totals, state_parts, grad_parts = lax.map(first_pass, shaped)
    zero_state = jnp.zeros((HEADS, HEAD_P, STATE), jnp.float32)
    final_state, entering = lax.scan(chain_link, zero_state, (totals, state_parts))
    final_grad, leaving = lax.scan(chain_link, zero_state, (totals, grad_parts), reverse=True)

    def finish(pieces):
        return span_grads(*pieces, a_log_rate, skip_gain)

    a_log_rate = decay_rate
    grad_x, grad_dt, grad_b, grad_c, grad_alog, grad_bias, grad_skip = lax.map(finish, shaped + (entering, leaving))
    return (grad_x.reshape(LENGTH, HEADS * HEAD_P), grad_dt.reshape(LENGTH, HEADS),
            grad_b.reshape(LENGTH, STATE), grad_c.reshape(LENGTH, STATE),
            jnp.sum(grad_alog, axis=0), jnp.sum(grad_bias, axis=0), jnp.sum(grad_skip, axis=0))


def reference(inputs, dt_raw, dt_bias, a_log, b_in, c_in, skip_gain, grad_out, doc_lengths):
    def per_sequence(pieces):
        return sequence_grads(*pieces, dt_bias, a_log, skip_gain)

    grad_x, grad_dt, grad_b, grad_c, grad_alog, grad_bias, grad_skip = lax.map(per_sequence, (inputs, dt_raw, b_in, c_in, grad_out, doc_lengths))
    return (grad_x, grad_dt, grad_b, grad_c, jnp.sum(grad_alog, axis=0), jnp.sum(grad_bias, axis=0), jnp.sum(grad_skip, axis=0))
```

```python
import functools

import jax
import jax.numpy as jnp
from jax import lax
from jax.experimental import pallas as pl
from jax.experimental.pallas import tpu as pltpu
from jax.sharding import PartitionSpec as P

SPAN = 128
LANES = 128
F32 = jnp.float32
BF16 = jnp.bfloat16
EXACT = lax.Precision.HIGHEST


def from_behind(array, axis, by):
    count = lax.axis_size(axis)
    pairs = [(i, i + by) for i in range(count) if 0 <= i + by < count]
    return lax.ppermute(array, axis, pairs)


def reverse_cumsum(values, along_axis):
    return jnp.flip(jnp.cumsum(jnp.flip(values, along_axis), axis=along_axis), along_axis)


def doc_index(positions, starts):
    return jnp.sum((starts[None, :] <= positions[:, None]).astype(jnp.int32), axis=1)


def vector_factors(decay_block, segment_block, previous_block):
    cumulative = jnp.cumsum(decay_block, axis=0)
    last_segment = segment_block[-1]
    mask_in = (segment_block == previous_block).astype(jnp.float32)
    mask_out = (segment_block == last_segment).astype(jnp.float32)
    factor_in = mask_in[:, None] * jnp.exp(cumulative)
    factor_out = mask_out[:, None] * jnp.exp(cumulative[-1][None, :] - cumulative)
    span_total = (last_segment == previous_block).astype(jnp.float32) * jnp.exp(cumulative[-1])
    return (cumulative, mask_in, mask_out, factor_in, factor_out, span_total)


def pair_factor(cumulative, segment_block):
    local_pos = jnp.arange(segment_block.shape[0], dtype=jnp.int32)
    allowed = (local_pos[:, None] >= local_pos[None, :]) & (
        segment_block[:, None] == segment_block[None, :]
    )
    spread = cumulative.T[:, :, None] - cumulative.T[:, None, :]
    return jnp.where(allowed[None], jnp.exp(jnp.where(allowed[None], spread, 0.0)), 0.0)


def first_pass(
    inputs_block,
    grads_block,
    b_block,
    c_block,
    step_block,
    decay_block,
    segment_block,
    previous_block,
):
    cumulative, mask_in, mask_out, factor_in, factor_out, span_total = vector_factors(
        decay_block, segment_block, previous_block
    )
    scaled_in = (inputs_block * (factor_out * step_block)[:, :, None]).astype(jnp.bfloat16)
    scaled_grad = (grads_block * factor_in[:, :, None]).astype(jnp.bfloat16)
    state_part = jnp.einsum("shp,sn->hpn", scaled_in, b_block, preferred_element_type=jnp.float32)
    grad_part = jnp.einsum("uhp,un->hpn", scaled_grad, c_block, preferred_element_type=jnp.float32)
    return (span_total, state_part, grad_part)


def span_grads(
    inputs_block,
    grads_block,
    b_block,
    c_block,
    step_block,
    decay_block,
    segment_block,
    previous_block,
    preact_block,
    state_in,
    state_grad,
    decay_rate,
    skip_gain,
):
    cumulative, mask_in, mask_out, factor_in, factor_out, span_total = vector_factors(
        decay_block, segment_block, previous_block
    )
    pair_decay = pair_factor(cumulative, segment_block)
    scores = jnp.einsum("un,sn->us", c_block, b_block, preferred_element_type=jnp.float32)
    cross_term = jnp.einsum(
        "uhp,shp->hus", grads_block, inputs_block, preferred_element_type=jnp.float32
    )
    masked = (pair_decay * scores[None]).astype(jnp.bfloat16)
    weighted = pair_decay * cross_term * step_block.T[:, None, :]
    summed = jnp.sum(weighted, axis=0).astype(jnp.bfloat16)
    products = weighted * scores[None]
    change = jnp.sum(products, axis=2) - jnp.sum(products, axis=1)
    first_term = reverse_cumsum(change, 1).T
    h_low = state_in.astype(jnp.bfloat16)
    e_low = state_grad.astype(jnp.bfloat16)
    along_b = jnp.einsum("tn,hpn->thp", b_block, e_low, preferred_element_type=jnp.float32)
    grad_b_prod = (
        jnp.einsum("hut,uhp->thp", masked, grads_block, preferred_element_type=jnp.float32)
        + factor_out[:, :, None] * along_b
    )
    grad_x = (step_block[:, :, None] * grad_b_prod + skip_gain[None, :, None] * grads_block).astype(
        jnp.bfloat16
    )
    x_state = jnp.einsum("thp,hpn->thn", inputs_block, e_low, preferred_element_type=jnp.float32)
    y_state = jnp.einsum("uhp,hpn->uhn", grads_block, h_low, preferred_element_type=jnp.float32)
    grad_b = jnp.einsum("us,un->sn", summed, c_block, preferred_element_type=jnp.float32) + jnp.sum(
        (step_block * factor_out)[:, :, None] * x_state, axis=1
    )
    grad_c = jnp.einsum("us,sn->un", summed, b_block, preferred_element_type=jnp.float32) + jnp.sum(
        factor_in[:, :, None] * y_state, axis=1
    )
    z_term = jnp.sum(y_state * c_block[:, None, :], axis=2)
    w_term = step_block * jnp.sum(x_state * b_block[:, None, :], axis=2)
    second_term = mask_in[:, None] * reverse_cumsum(factor_in * z_term, 0)
    carried = factor_out * w_term
    third_term = mask_out[:, None] * (jnp.cumsum(carried, axis=0) - carried)
    fourth_term = factor_out * factor_in * jnp.sum(state_grad * state_in, axis=(1, 2))[None, :]
    decay_grad = first_term + second_term + third_term + fourth_term
    x_dot_g = jnp.sum(inputs_block * grad_b_prod, axis=2)
    grad_dt = (x_dot_g + decay_rate[None, :] * decay_grad) * jax.nn.sigmoid(preact_block)
    grad_alog = jnp.sum(decay_grad * step_block, axis=0) * decay_rate
    grad_bias = jnp.sum(grad_dt, axis=0)
    grad_skip = jnp.einsum(
        "thp,thp->h", grads_block, inputs_block, preferred_element_type=jnp.float32
    )
    return (grad_x, grad_dt, grad_b, grad_c, grad_alog, grad_bias, grad_skip)


def local_link(running, pieces):
    decay_gain, held_state = running
    span_total, span_part = pieces
    return ((decay_gain * span_total, span_total[:, None, None] * held_state + span_part), running)


def link_maps(earlier, later):
    return (earlier[0] * later[0], later[0][:, None, None] * earlier[1] + later[1])


def doubling(element, reverse):
    axis_count = lax.axis_size("ctx")
    own_index = lax.axis_index("ctx")
    distances = [1] + [2**power for power in range((axis_count - 1).bit_length())]
    running = element
    for section_num, distance in enumerate(distances):
        shift_by = -distance if reverse else distance
        received = from_behind((running[0], running[1]), "ctx", shift_by)
        source = own_index - shift_by
        present = (source >= 0) & (source < axis_count)
        fixed = (jnp.where(present, received[0], 1.0), received[1])
        if section_num == 0:
            running = fixed
        else:
            running = link_maps(fixed, running)
    return running


def general_local(inputs, dt_raw, dt_bias, a_log, b_in, c_in, skip_gain, grad_out, doc_lengths):
    token_count = inputs.shape[1]
    head_count = dt_bias.shape[0]
    head_width = inputs.shape[2] // head_count
    state_size = b_in.shape[2]
    span_count = token_count // SPAN
    preact = dt_raw[0] + dt_bias[None, :]
    step_size = jax.nn.softplus(preact)
    decay_rate = -jnp.exp(a_log)
    log_decay = step_size * decay_rate[None, :]
    lengths = doc_lengths[0]
    starts = jnp.cumsum(lengths) - lengths
    positions = lax.axis_index("ctx") * token_count + jnp.arange(token_count, dtype=jnp.int32)
    segment = doc_index(positions, starts)
    previous = doc_index(positions[::SPAN] - 1, starts)
    shaped = (
        inputs[0].reshape(span_count, SPAN, head_count, head_width),
        grad_out[0].reshape(span_count, SPAN, head_count, head_width),
        b_in[0].reshape(span_count, SPAN, state_size),
        c_in[0].reshape(span_count, SPAN, state_size),
        step_size.reshape(span_count, SPAN, head_count),
        log_decay.reshape(span_count, SPAN, head_count),
        segment.reshape(span_count, SPAN),
        previous,
    )
    totals, state_parts, grad_parts = jax.vmap(first_pass)(*shaped)
    start_maps = (
        jnp.ones((head_count,), jnp.float32),
        jnp.zeros((head_count, head_width, state_size), jnp.float32),
    )
    forward_map, (gain_before, local_entry) = lax.scan(
        local_link, start_maps, (totals, state_parts)
    )
    backward_map, (gain_after, local_leave) = lax.scan(
        local_link, start_maps, (totals, grad_parts), reverse=True
    )
    entry_state = doubling(forward_map, False)[1]
    leave_state = doubling(backward_map, True)[1]
    entering = gain_before[:, :, None, None] * entry_state[None] + local_entry
    leaving = gain_after[:, :, None, None] * leave_state[None] + local_leave
    mapped = jax.vmap(span_grads, in_axes=(0, 0, 0, 0, 0, 0, 0, 0, 0, 0, 0, None, None))
    grad_x, grad_dt, grad_b, grad_c, grad_alog, grad_bias, grad_skip = mapped(
        *shaped,
        preact.reshape(span_count, SPAN, head_count),
        entering,
        leaving,
        decay_rate,
        skip_gain
    )
    b_total, c_total = lax.psum(
        (grad_b.reshape(token_count, state_size), grad_c.reshape(token_count, state_size)), "head"
    )
    alog_total, bias_total, skip_total = lax.psum(
        (jnp.sum(grad_alog, axis=0), jnp.sum(grad_bias, axis=0), jnp.sum(grad_skip, axis=0)),
        ("dp", "ctx"),
    )
    return (
        grad_x.reshape(1, token_count, head_count * head_width),
        grad_dt,
        b_total[None],
        c_total[None],
        alog_total,
        bias_total,
        skip_total,
    )


def nn(left, right, precision=None):
    return lax.dot_general(
        left, right, (((1,), (0,)), ((), ())), precision=precision, preferred_element_type=F32
    )


def nt(left, right, precision=None):
    return lax.dot_general(
        left, right, (((1,), (1,)), ((), ())), precision=precision, preferred_element_type=F32
    )


def iota(shape, axis):
    return lax.broadcasted_iota(jnp.int32, shape, axis)


def eye(size):
    return (iota((size, size), 0) == iota((size, size), 1)).astype(F32)


def head_rows(heads, features):
    width = features // heads
    start = iota((heads, features), 0) * width
    feature = iota((heads, features), 1)
    return ((feature >= start) & (feature < start + width)).astype(BF16)


def head_columns(features, heads):
    width = features // heads
    start = iota((features, heads), 1) * width
    feature = iota((features, heads), 0)
    return ((feature >= start) & (feature < start + width)).astype(BF16)


def spread(factor, rows):
    high = factor.astype(BF16)
    rest = factor - high.astype(F32)
    middle = rest.astype(BF16)
    low = (rest - middle.astype(F32)).astype(BF16)
    return nn(high, rows) + nn(middle, rows) + nn(low, rows)


def head_sum(values, columns):
    high = values.astype(BF16)
    low = (values - high.astype(F32)).astype(BF16)
    return nn(high, columns) + nn(low, columns)


def doc_of(lens_ref, positions):
    count = jnp.zeros(positions.shape, jnp.int32)
    start = jnp.int32(0)
    for index in range(lens_ref.shape[1]):
        count = count + (start <= positions).astype(jnp.int32)
        start = start + lens_ref[0, index]
    return count


def doc_scalar(lens_ref, position):
    count = jnp.int32(0)
    start = jnp.int32(0)
    for index in range(lens_ref.shape[1]):
        count = count + jnp.where(start <= position, 1, 0)
        start = start + lens_ref[0, index]
    return count


def masks(lens_ref, span):
    base = lax.axis_index("ctx") * span
    doc = doc_of(lens_ref, base + iota((span, 1), 0))
    before = doc_scalar(lens_ref, base - 1)
    last = doc_scalar(lens_ref, base + span - 1)
    inward = (doc == before).astype(F32)
    outward = (doc == last).astype(F32)
    whole = jnp.where(last == before, 1.0, 0.0)
    return inward, outward, whole


AUX = ("dt", "gate", "cum", "din", "dout", "alpha_s", "beta_s", "alpha_u", "beta_u", "tot", "rate")


def aux_get(aux_ref, name, heads):
    slot = AUX.index(name) * heads
    return aux_ref[:, slot : slot + heads]


def prep_kernel(
    lens_ref, x_ref, g_ref, raw_ref, bias_ref, alog_ref, b_ref, c_ref,
    pay_even_ref, pay_odd_ref, aux_ref, xs_ref, gs_ref,
):
    span, features = x_ref.shape[1:]
    heads = raw_ref.shape[2]
    inward, outward, whole = masks(lens_ref, span)
    preact = raw_ref[0] + bias_ref[...]
    dt = jnp.maximum(preact, 0.0) + jnp.log1p(jnp.exp(-jnp.abs(preact)))
    gate = 1.0 / (1.0 + jnp.exp(-preact))
    rate = -jnp.exp(alog_ref[...])
    row, column = iota((span, span), 0), iota((span, span), 1)
    upto = (row >= column).astype(F32)
    beyond = (row < column).astype(F32)
    cum = nn(upto, dt * rate, EXACT)
    cum_last = cum[span - 1 : span, :]
    din = inward * jnp.exp(cum)
    dout = outward * jnp.exp(cum_last - cum)
    tot = jnp.broadcast_to(whole * jnp.exp(cum_last), cum.shape)
    pair = jnp.concatenate([dt, gate], axis=1)
    seen = nn(upto, pair * inward, EXACT)
    left = nn(beyond, pair * outward, EXACT)
    alpha_s = rate * left[:, :heads]
    beta_s = rate * left[:, heads:] + gate / dt
    alpha_u = rate * seen[:, :heads]
    beta_u = rate * seen[:, heads:]
    values = (dt, gate, cum, din, dout, alpha_s, beta_s, alpha_u, beta_u, tot,
              jnp.broadcast_to(rate, cum.shape))
    for slot, value in enumerate(values):
        aux_ref[:, slot * heads : (slot + 1) * heads] = value
    rows = head_rows(heads, features)
    xs = (x_ref[0].astype(F32) * spread(dout * dt, rows)).astype(BF16)
    gs = (g_ref[0].astype(F32) * spread(din, rows)).astype(BF16)
    xs_ref[...] = xs
    gs_ref[...] = gs
    turn = eye(heads)
    ahead_small = [nt(turn, alpha_s, EXACT), nt(turn, beta_s, EXACT)]
    behind_small = [nt(turn, alpha_u, EXACT), nt(turn, beta_u, EXACT)]

    def fill(ref, scaled, wide, small):
        blocks = features // LANES
        for block in range(blocks):
            ref[block * span : (block + 1) * span, :] = scaled[
                :, block * LANES : (block + 1) * LANES
            ].astype(F32)
        base = blocks * span
        ref[base : base + span, :] = wide.astype(F32)
        base = base + span
        for part in small:
            ref[base : base + heads, :] = part
            base = base + heads

    even = lax.rem(lax.axis_index("ctx"), 2) == 0

    @pl.when(even)
    def _():
        fill(pay_even_ref, xs, b_ref[0], ahead_small)
        fill(pay_odd_ref, gs, c_ref[0], behind_small)

    @pl.when(jnp.logical_not(even))
    def _():
        fill(pay_even_ref, gs, c_ref[0], behind_small)
        fill(pay_odd_ref, xs, b_ref[0], ahead_small)


def local_kernel(lens_ref, x_ref, g_ref, aux_ref, b_ref, c_ref, gb_ref, small_ref, grads_ref):
    span, features = x_ref.shape[1:]
    heads = small_ref.shape[1] // 8
    width = features // heads
    base = lax.axis_index("ctx") * span
    doc_s = doc_of(lens_ref, base + iota((span, 1), 0))
    doc_u = doc_of(lens_ref, base + iota((1, span), 1))
    row, column = iota((span, span), 0), iota((span, span), 1)
    closed = jnp.where((column >= row) & (doc_s == doc_u), 0.0, -1e30)
    dt = aux_get(aux_ref, "dt", heads)
    gate = aux_get(aux_ref, "gate", heads)
    cum = aux_get(aux_ref, "cum", heads)
    rate = aux_get(aux_ref, "rate", heads)
    cum_rows = nt(eye(heads), cum, EXACT)
    scores = nt(b_ref[0], c_ref[0])
    summed = jnp.zeros((span, span), F32)
    lane = iota((span, heads), 1)
    from_s = jnp.zeros((span, heads), F32)
    to_u = []
    for pair in range(0, heads, 2):
        outs = []
        for head in (pair, pair + 1):
            part = slice(head * width, (head + 1) * width)
            g_head, x_head = g_ref[0, :, part], x_ref[0, :, part]
            cross = nt(x_head, g_head)
            decay = jnp.exp(cum_rows[head : head + 1, :] - cum[:, head : head + 1] + closed)
            masked = decay * scores
            weighted = decay * cross * dt[:, head : head + 1]
            summed = summed + weighted
            product = weighted * scores
            from_s = jnp.where(lane == head, jnp.sum(product, axis=1, keepdims=True), from_s)
            to_u.append(jnp.sum(product, axis=0, keepdims=True))
            outs.append(nn(masked.astype(BF16), g_head))
        gb_ref[:, pair * width : (pair + 2) * width] = jnp.concatenate(outs, axis=1)
    onward = (row <= column).astype(F32)
    first = nt(onward, jnp.concatenate(to_u, axis=0), EXACT) - nn(onward, from_s, EXACT)
    columns = head_columns(features, heads)
    x_wide = x_ref[0].astype(F32)
    x_gb = head_sum(x_wide * gb_ref[...], columns)
    skip = head_sum(x_wide * g_ref[0].astype(F32), columns)
    values = (first, x_gb, rate * dt * first, gate * (x_gb + rate * first), skip)
    for slot, value in enumerate(values):
        small_ref[:, slot * heads : (slot + 1) * heads] = value
    grads_ref[:span, :] = nn(summed.astype(BF16), c_ref[0])
    grads_ref[span:, :] = nn(jnp.transpose(summed).astype(BF16), b_ref[0])


def relay_kernel(
    got_even_ref, got_odd_ref, xs_ref, gs_ref, aux_ref, b_ref, c_ref, small_ref, grads_ref,
    hop_even_ref, hop_odd_ref, red_ref, zw_ref, gb_ref, sums_ref,
):
    span, features = xs_ref.shape
    heads = small_ref.shape[1] // 8
    blocks = features // LANES
    even = lax.rem(lax.axis_index("ctx"), 2) == 0

    def behind(part):
        return jnp.where(even, got_odd_ref[part, :], got_even_ref[part, :])

    def ahead(part):
        return jnp.where(even, got_even_ref[part, :], got_odd_ref[part, :])

    def wide(get):
        return jnp.concatenate(
            [get(slice(k * span, (k + 1) * span)).astype(BF16) for k in range(blocks)], axis=1
        )

    base = blocks * span
    xp, bp = wide(behind), behind(slice(base, base + span)).astype(BF16)
    gn, cn = wide(ahead), ahead(slice(base, base + span)).astype(BF16)
    base = base + span
    alpha_p = behind(slice(base, base + heads))
    beta_p = behind(slice(base + heads, base + 2 * heads))
    alpha_n = ahead(slice(base, base + heads))
    beta_n = ahead(slice(base + heads, base + 2 * heads))
    xs, gs, b, c = xs_ref[...], gs_ref[...], b_ref[0], c_ref[0]
    columns = head_columns(features, heads)
    rows = head_rows(heads, features)
    tot = aux_get(aux_ref, "tot", heads)
    gn_tot = (gn.astype(F32) * spread(tot, rows)).astype(BF16)

    pull = nn(nt(c, bp).astype(BF16), xp)
    z_own = head_sum(gs.astype(F32) * pull, columns)
    push = nn(nt(b, cn).astype(BF16), gn)
    w_own = head_sum(xs.astype(F32) * push, columns)
    gb_ref[...] = push
    far_pull = nn(nt(cn, bp).astype(BF16), xp)
    z_far = head_sum(gn_tot.astype(F32) * far_pull, columns)
    far_push = nn(nt(bp, cn).astype(BF16), gn_tot)
    w_far = head_sum(xp.astype(F32) * far_push, columns)

    turn = eye(heads)
    z_far_rows = nt(turn, z_far, EXACT)
    w_far_rows = nt(turn, w_far, EXACT)
    carried = jnp.sum(z_far, axis=0, keepdims=True)
    dt, gate, rate = (aux_get(aux_ref, name, heads) for name in ("dt", "gate", "rate"))
    values = small_ref[:, 2 * heads : 5 * heads]
    alog_own = (
        z_own * aux_get(aux_ref, "alpha_u", heads)
        + w_own * aux_get(aux_ref, "alpha_s", heads)
        + carried * rate * dt
        + values[:, :heads]
    )
    bias_own = (
        z_own * aux_get(aux_ref, "beta_u", heads)
        + w_own * aux_get(aux_ref, "beta_s", heads)
        + carried * rate * gate
        + values[:, heads : 2 * heads]
    )
    ones = jnp.ones((8, span), F32)
    alog = nn(ones, alog_own, EXACT) + nt(ones, z_far_rows * alpha_n + w_far_rows * alpha_p, EXACT)
    bias = nn(ones, bias_own, EXACT) + nt(ones, z_far_rows * beta_n + w_far_rows * beta_p, EXACT)
    skip = nn(ones, values[:, 2 * heads :], EXACT)
    red_ref[...] = jnp.zeros(red_ref.shape, F32)
    red_ref[:, :heads] = alog
    red_ref[:, heads : 2 * heads] = bias
    red_ref[:, 2 * heads : 3 * heads] = skip
    zw_ref[:, :heads] = z_own
    zw_ref[:, heads : 2 * heads] = w_own
    zw_ref[:, 2 * heads : 3 * heads] = jnp.broadcast_to(carried, z_own.shape)

    sums_ref[:span, :] = grads_ref[:span, :] + nn(nt(xs, gn).astype(BF16), cn)
    sums_ref[span:, :] = grads_ref[span:, :] + nn(nt(gs, xp).astype(BF16), bp)
    grad_b_far = nn(nt(xp, gn_tot).astype(BF16), cn)
    grad_c_far = nn(nt(gn_tot, xp).astype(BF16), bp)

    base = blocks * span

    def fill(ref, grad, small, heavy):
        if heavy:
            for block in range(blocks):
                ref[block * span : (block + 1) * span, :] = far_push[
                    :, block * LANES : (block + 1) * LANES
                ]
        ref[base : base + span, :] = grad
        ref[base + span : base + span + heads, :] = small

    @pl.when(even)
    def _():
        fill(hop_even_ref, grad_c_far, z_far_rows, True)
        fill(hop_odd_ref, grad_b_far, w_far_rows, True)

    @pl.when(jnp.logical_not(even))
    def _():
        fill(hop_even_ref, grad_b_far, w_far_rows, True)
        fill(hop_odd_ref, grad_c_far, z_far_rows, True)


def final_kernel(
    lens_ref, far_even_ref, far_odd_ref, g_ref, aux_ref, skip_ref, gbl_ref, gbn_ref, small_ref,
    zw_ref, sums_ref, gx_ref, gdt_ref, half_ref,
):
    span, features = g_ref.shape[1:]
    heads = small_ref.shape[1] // 8
    blocks = features // LANES
    even = lax.rem(lax.axis_index("ctx"), 2) == 0

    def behind(part):
        return jnp.where(even, far_odd_ref[part, :], far_even_ref[part, :])

    def ahead(part):
        return jnp.where(even, far_even_ref[part, :], far_odd_ref[part, :])

    base = blocks * span
    push = gbn_ref[...] + jnp.concatenate(
        [ahead(slice(k * span, (k + 1) * span)) for k in range(blocks)], axis=1
    )
    rows = head_rows(heads, features)
    dt = aux_get(aux_ref, "dt", heads)
    dout = aux_get(aux_ref, "dout", heads)
    gate = aux_get(aux_ref, "gate", heads)
    rate = aux_get(aux_ref, "rate", heads)
    skip = jnp.broadcast_to(skip_ref[...], dt.shape)
    gx_ref[0] = (
        spread(dt, rows) * gbl_ref[...]
        + spread(dt * dout, rows) * push
        + spread(skip, rows) * g_ref[0].astype(F32)
    ).astype(BF16)
    inward, outward, _ = masks(lens_ref, span)
    flip = eye(span)
    z = zw_ref[:, :heads] + nt(flip, behind(slice(base + span, base + span + heads)), EXACT)
    w = zw_ref[:, heads : 2 * heads] + nt(
        flip, ahead(slice(base + span, base + span + heads)), EXACT
    )
    row, column = iota((span, span), 0), iota((span, span), 1)
    onward = (row <= column).astype(F32)
    past = (row > column).astype(F32)
    decay_grad = (
        small_ref[:, :heads]
        + inward * nn(onward, z, EXACT)
        + outward * nn(past, w, EXACT)
        + zw_ref[:, 2 * heads : 3 * heads]
    )
    x_gb = small_ref[:, heads : 2 * heads] + w / dt
    gdt_ref[0] = (x_gb + rate * decay_grad) * gate
    half_ref[:span, :] = sums_ref[:span, :] + ahead(slice(base, base + span))
    half_ref[span:, :] = sums_ref[span:, :] + behind(slice(base, base + span))


def call(kernel, shapes, operands, scalars=0, flops=0):
    specs = [pl.BlockSpec(memory_space=pltpu.SMEM)] * scalars + [
        pl.BlockSpec(memory_space=pltpu.VMEM)
    ] * (len(operands) - scalars)
    moved = sum(item.size * item.dtype.itemsize for item in operands) + sum(
        item.size * jnp.dtype(item.dtype).itemsize for item in shapes
    )
    return pl.pallas_call(
        kernel,
        out_shape=shapes,
        in_specs=specs,
        out_specs=[pl.BlockSpec(memory_space=pltpu.VMEM)] * len(shapes),
        cost_estimate=pl.CostEstimate(flops=flops, bytes_accessed=moved, transcendentals=0),
    )(*operands)


def near_local(inputs, dt_raw, dt_bias, a_log, b_in, c_in, skip_gain, grad_out, doc_lengths):
    _, span, features = inputs.shape
    heads = dt_bias.shape[0]
    state = b_in.shape[2]
    count = lax.axis_size("ctx")
    struct = jax.ShapeDtypeStruct
    bias, alog, skip = (item.reshape(1, heads) for item in (dt_bias, a_log, skip_gain))
    pay_rows = features // LANES * span + span + 2 * heads
    pay = struct((pay_rows, LANES), F32)
    pay_even, pay_odd, aux, xs, gs = call(
        prep_kernel,
        (pay, pay, struct((span, 2 * LANES), F32), struct((span, features), BF16),
         struct((span, features), BF16)),
        (doc_lengths, inputs, grad_out, dt_raw, bias, alog, b_in, c_in),
        scalars=1,
        flops=10**8,
    )
    even_pairs = [(i, i ^ 1) for i in range(count) if i ^ 1 < count]
    odd_pairs = [(i, j) for i in range(count) for j in [((i + 1) ^ 1) - 1] if 0 <= j < count]
    got_odd = lax.ppermute(pay_odd, "ctx", odd_pairs)
    got_even = lax.ppermute(pay_even, "ctx", even_pairs)
    gb_local, small, grads = call(
        local_kernel,
        (struct((span, features), F32), struct((span, 8 * heads), F32),
         struct((2 * span, state), F32)),
        (doc_lengths, inputs, grad_out, aux, b_in, c_in),
        scalars=1,
        flops=10**8,
    )
    hop_rows = features // LANES * span + span + heads
    hop = struct((hop_rows, LANES), F32)
    hop_even, hop_odd, red, zw, gb_next, sums = call(
        relay_kernel,
        (hop, hop, struct((8, LANES), F32), struct((span, LANES), F32),
         struct((span, features), F32), struct((2 * span, state), F32)),
        (got_even, got_odd, xs, gs, aux, b_in, c_in, small, grads),
        flops=3 * 10**8,
    )
    inner = range(1, count - 1)
    far_even = lax.ppermute(hop_even, "ctx", [p for p in even_pairs if p[0] in inner])
    far_odd = lax.ppermute(hop_odd, "ctx", [p for p in odd_pairs if p[0] in inner])
    for axis in ("dp", "ctx"):
        size = lax.axis_size(axis)
        bit = 1
        while bit < size:
            red = red + lax.ppermute(red, axis, [(i, i ^ bit) for i in range(size)])
            bit *= 2
    grad_x, grad_dt, half = call(
        final_kernel,
        (struct((1, span, features), BF16), struct((1, span, heads), F32),
         struct((2 * span, state), F32)),
        (doc_lengths, far_even, far_odd, grad_out, aux, skip, gb_local, gb_next, small, zw, sums),
        scalars=1,
        flops=10**8,
    )
    lanes = lax.axis_size("head")
    total = half
    for step in range(1, lanes):
        total = total + lax.ppermute(half, "head", [(i, (i + step) % lanes) for i in range(lanes)])
    alog_total, bias_total, skip_total = (
        red[0, i * heads : (i + 1) * heads] for i in range(3)
    )
    return (grad_x, grad_dt, total[None, :span], total[None, span:], alog_total, bias_total, skip_total)


def local(inputs, dt_raw, dt_bias, a_log, b_in, c_in, skip_gain, grad_out, doc_lengths):
    args = (inputs, dt_raw, dt_bias, a_log, b_in, c_in, skip_gain, grad_out, doc_lengths)
    heads = dt_bias.shape[0]
    shards = [lax.axis_size(axis) for axis in ("dp", "ctx")]
    near = (
        inputs.shape[1] == SPAN
        and shards[1] in (2, 4)
        and shards[0] & (shards[0] - 1) == 0
        and b_in.shape[2] == LANES
        and inputs.shape[2] % LANES == 0
        and heads * len(AUX) <= 2 * LANES
        and heads * 8 == LANES
    )
    return near_local(*args) if near else general_local(*args)


def solution(mesh):
    placed = (
        P("dp", "ctx", "head"),
        P("dp", "ctx", "head"),
        P("head"),
        P("head"),
        P("dp", "ctx", None),
        P("dp", "ctx", None),
        P("head"),
        P("dp", "ctx", "head"),
        P("dp", None),
    )
    return jax.shard_map(
        local,
        mesh=mesh,
        in_specs=placed,
        out_specs=(
            P("dp", "ctx", "head"),
            P("dp", "ctx", "head"),
            P("dp", "ctx", None),
            P("dp", "ctx", None),
            P("head"),
            P("head"),
            P("head"),
        ),
        check_vma=False,
    )
```

```python
import jax
import jax.numpy as jnp
from jax import lax
from jax.experimental import pallas as pl
from jax.experimental.pallas import tpu as pltpu
from jax.sharding import PartitionSpec as P


SPAN = 128
LANES = 128
VMEM_GRANT = 16 << 20
F32 = jnp.float32
BF16 = jnp.bfloat16
EXACT = lax.Precision.HIGHEST


def from_behind(array, axis, by):
    count = lax.axis_size(axis)
    pairs = [(i, i + by) for i in range(count) if 0 <= i + by < count]
    return lax.ppermute(array, axis, pairs)


def reverse_cumsum(values, along_axis):
    return jnp.flip(jnp.cumsum(jnp.flip(values, along_axis), axis=along_axis), along_axis)


def doc_index(positions, starts):
    return jnp.sum((starts[None, :] <= positions[:, None]).astype(jnp.int32), axis=1)


def vector_factors(decay_block, segment_block, previous_block):
    cumulative = jnp.cumsum(decay_block, axis=0)
    last_segment = segment_block[-1]
    mask_in = (segment_block == previous_block).astype(jnp.float32)
    mask_out = (segment_block == last_segment).astype(jnp.float32)
    factor_in = mask_in[:, None] * jnp.exp(cumulative)
    factor_out = mask_out[:, None] * jnp.exp(cumulative[-1][None, :] - cumulative)
    span_total = (last_segment == previous_block).astype(jnp.float32) * jnp.exp(cumulative[-1])
    return (cumulative, mask_in, mask_out, factor_in, factor_out, span_total)


def pair_factor(cumulative, segment_block):
    local_pos = jnp.arange(segment_block.shape[0], dtype=jnp.int32)
    allowed = (local_pos[:, None] >= local_pos[None, :]) & (
        segment_block[:, None] == segment_block[None, :]
    )
    spread = cumulative.T[:, :, None] - cumulative.T[:, None, :]
    return jnp.where(allowed[None], jnp.exp(jnp.where(allowed[None], spread, 0.0)), 0.0)


def first_pass(
    inputs_block,
    grads_block,
    b_block,
    c_block,
    step_block,
    decay_block,
    segment_block,
    previous_block,
):
    _, _, _, factor_in, factor_out, span_total = vector_factors(
        decay_block, segment_block, previous_block
    )
    scaled_in = (inputs_block * (factor_out * step_block)[:, :, None]).astype(jnp.bfloat16)
    scaled_grad = (grads_block * factor_in[:, :, None]).astype(jnp.bfloat16)
    state_part = jnp.einsum("shp,sn->hpn", scaled_in, b_block, preferred_element_type=jnp.float32)
    grad_part = jnp.einsum("uhp,un->hpn", scaled_grad, c_block, preferred_element_type=jnp.float32)
    return (span_total, state_part, grad_part)


def span_grads(
    inputs_block,
    grads_block,
    b_block,
    c_block,
    step_block,
    decay_block,
    segment_block,
    previous_block,
    preact_block,
    state_in,
    state_grad,
    decay_rate,
    skip_gain,
):
    cumulative, mask_in, mask_out, factor_in, factor_out, _ = vector_factors(
        decay_block, segment_block, previous_block
    )
    pair_decay = pair_factor(cumulative, segment_block)
    scores = jnp.einsum("un,sn->us", c_block, b_block, preferred_element_type=jnp.float32)
    cross_term = jnp.einsum(
        "uhp,shp->hus", grads_block, inputs_block, preferred_element_type=jnp.float32
    )
    masked = (pair_decay * scores[None]).astype(jnp.bfloat16)
    weighted = pair_decay * cross_term * step_block.T[:, None, :]
    summed = jnp.sum(weighted, axis=0).astype(jnp.bfloat16)
    products = weighted * scores[None]
    change = jnp.sum(products, axis=2) - jnp.sum(products, axis=1)
    first_term = reverse_cumsum(change, 1).T
    h_low = state_in.astype(jnp.bfloat16)
    e_low = state_grad.astype(jnp.bfloat16)
    along_b = jnp.einsum("tn,hpn->thp", b_block, e_low, preferred_element_type=jnp.float32)
    grad_b_prod = (
        jnp.einsum("hut,uhp->thp", masked, grads_block, preferred_element_type=jnp.float32)
        + factor_out[:, :, None] * along_b
    )
    grad_x = (step_block[:, :, None] * grad_b_prod + skip_gain[None, :, None] * grads_block).astype(
        jnp.bfloat16
    )
    x_state = jnp.einsum("thp,hpn->thn", inputs_block, e_low, preferred_element_type=jnp.float32)
    y_state = jnp.einsum("uhp,hpn->uhn", grads_block, h_low, preferred_element_type=jnp.float32)
    grad_b = jnp.einsum("us,un->sn", summed, c_block, preferred_element_type=jnp.float32) + jnp.sum(
        (step_block * factor_out)[:, :, None] * x_state, axis=1
    )
    grad_c = jnp.einsum("us,sn->un", summed, b_block, preferred_element_type=jnp.float32) + jnp.sum(
        factor_in[:, :, None] * y_state, axis=1
    )
    z_term = jnp.sum(y_state * c_block[:, None, :], axis=2)
    w_term = step_block * jnp.sum(x_state * b_block[:, None, :], axis=2)
    second_term = mask_in[:, None] * reverse_cumsum(factor_in * z_term, 0)
    carried = factor_out * w_term
    third_term = mask_out[:, None] * (jnp.cumsum(carried, axis=0) - carried)
    fourth_term = factor_out * factor_in * jnp.sum(state_grad * state_in, axis=(1, 2))[None, :]
    decay_grad = first_term + second_term + third_term + fourth_term
    x_dot_g = jnp.sum(inputs_block * grad_b_prod, axis=2)
    grad_dt = (x_dot_g + decay_rate[None, :] * decay_grad) * jax.nn.sigmoid(preact_block)
    grad_alog = jnp.sum(decay_grad * step_block, axis=0) * decay_rate
    grad_bias = jnp.sum(grad_dt, axis=0)
    grad_skip = jnp.einsum(
        "thp,thp->h", grads_block, inputs_block, preferred_element_type=jnp.float32
    )
    return (grad_x, grad_dt, grad_b, grad_c, grad_alog, grad_bias, grad_skip)


def local_link(running, pieces):
    decay_gain, held_state = running
    span_total, span_part = pieces
    return ((decay_gain * span_total, span_total[:, None, None] * held_state + span_part), running)


def link_maps(earlier, later):
    return (earlier[0] * later[0], later[0][:, None, None] * earlier[1] + later[1])


def doubling(element, reverse):
    axis_count = lax.axis_size("ctx")
    own_index = lax.axis_index("ctx")
    distances = [1] + [2**power for power in range((axis_count - 1).bit_length())]
    running = element
    for section_num, distance in enumerate(distances):
        shift_by = -distance if reverse else distance
        received = from_behind((running[0], running[1]), "ctx", shift_by)
        source = own_index - shift_by
        present = (source >= 0) & (source < axis_count)
        fixed = (jnp.where(present, received[0], 1.0), received[1])
        if section_num == 0:
            running = fixed
        else:
            running = link_maps(fixed, running)
    return running


def general_local(inputs, dt_raw, dt_bias, a_log, b_in, c_in, skip_gain, grad_out, doc_lengths):
    token_count = inputs.shape[1]
    head_count = dt_bias.shape[0]
    head_width = inputs.shape[2] // head_count
    state_size = b_in.shape[2]
    span_count = token_count // SPAN
    preact = dt_raw[0] + dt_bias[None, :]
    step_size = jax.nn.softplus(preact)
    decay_rate = -jnp.exp(a_log)
    log_decay = step_size * decay_rate[None, :]
    lengths = doc_lengths[0]
    starts = jnp.cumsum(lengths) - lengths
    positions = lax.axis_index("ctx") * token_count + jnp.arange(token_count, dtype=jnp.int32)
    segment = doc_index(positions, starts)
    previous = doc_index(positions[::SPAN] - 1, starts)
    shaped = (
        inputs[0].reshape(span_count, SPAN, head_count, head_width),
        grad_out[0].reshape(span_count, SPAN, head_count, head_width),
        b_in[0].reshape(span_count, SPAN, state_size),
        c_in[0].reshape(span_count, SPAN, state_size),
        step_size.reshape(span_count, SPAN, head_count),
        log_decay.reshape(span_count, SPAN, head_count),
        segment.reshape(span_count, SPAN),
        previous,
    )
    totals, state_parts, grad_parts = jax.vmap(first_pass)(*shaped)
    start_maps = (
        jnp.ones((head_count,), jnp.float32),
        jnp.zeros((head_count, head_width, state_size), jnp.float32),
    )
    forward_map, (gain_before, local_entry) = lax.scan(
        local_link, start_maps, (totals, state_parts)
    )
    backward_map, (gain_after, local_leave) = lax.scan(
        local_link, start_maps, (totals, grad_parts), reverse=True
    )
    entry_state = doubling(forward_map, False)[1]
    leave_state = doubling(backward_map, True)[1]
    entering = gain_before[:, :, None, None] * entry_state[None] + local_entry
    leaving = gain_after[:, :, None, None] * leave_state[None] + local_leave
    mapped = jax.vmap(span_grads, in_axes=(0, 0, 0, 0, 0, 0, 0, 0, 0, 0, 0, None, None))
    grad_x, grad_dt, grad_b, grad_c, grad_alog, grad_bias, grad_skip = mapped(
        *shaped,
        preact.reshape(span_count, SPAN, head_count),
        entering,
        leaving,
        decay_rate,
        skip_gain
    )
    b_total, c_total = lax.psum(
        (grad_b.reshape(token_count, state_size), grad_c.reshape(token_count, state_size)), "head"
    )
    alog_total, bias_total, skip_total = lax.psum(
        (jnp.sum(grad_alog, axis=0), jnp.sum(grad_bias, axis=0), jnp.sum(grad_skip, axis=0)),
        ("dp", "ctx"),
    )
    return (
        grad_x.reshape(1, token_count, head_count * head_width),
        grad_dt,
        b_total[None],
        c_total[None],
        alog_total,
        bias_total,
        skip_total,
    )


def dot(left, right, dims, precision=None):
    return lax.dot_general(
        left, right, (dims, ((), ())), precision=precision, preferred_element_type=F32
    )


def nn(left, right, precision=None):
    return dot(left, right, ((1,), (0,)), precision)


def nt(left, right, precision=None):
    return dot(left, right, ((1,), (1,)), precision)


def tn(left, right, precision=None):
    return dot(left, right, ((0,), (0,)), precision)


def iota(shape, axis):
    return lax.broadcasted_iota(jnp.int32, shape, axis)


def eye(size):
    return (iota((size, size), 0) == iota((size, size), 1)).astype(F32)


def head_rows(heads, features):
    width = features // heads
    start = iota((heads, features), 0) * width
    feature = iota((heads, features), 1)
    return ((feature >= start) & (feature < start + width)).astype(BF16)


def head_columns(features, heads):
    width = features // heads
    start = iota((features, heads), 1) * width
    feature = iota((features, heads), 0)
    return ((feature >= start) & (feature < start + width)).astype(BF16)


def thirds(value):
    high = value.astype(BF16)
    rest = value - high.astype(F32)
    middle = rest.astype(BF16)
    low = (rest - middle.astype(F32)).astype(BF16)
    return jnp.concatenate([high, middle, low], axis=0)


def spread(factor, rows):
    return tn(thirds(factor), jnp.concatenate([rows] * 3, axis=0))


def spread_row(factor, features):
    heads = factor.shape[1]
    wide = jnp.broadcast_to(factor, (8, heads))
    high = wide.astype(BF16)
    rest = wide - high.astype(F32)
    middle = rest.astype(BF16)
    low = (rest - middle.astype(F32)).astype(BF16)
    rows = head_rows(heads, features)
    return (nn(high, rows) + nn(middle, rows) + nn(low, rows))[:1]


def head_sum(values, columns):
    high = values.astype(BF16)
    low = (values - high.astype(F32)).astype(BF16)
    return nn(high, columns) + nn(low, columns)


def as_column(row):
    size = row.shape[1]
    return jnp.sum(jnp.where(eye(size) > 0, row, 0.0), axis=1, keepdims=True)


def as_row(column):
    size = column.shape[0]
    return jnp.sum(jnp.where(eye(size) > 0, column, 0.0), axis=0, keepdims=True)


def doc_of(lens_ref, positions):
    count = jnp.zeros(positions.shape, jnp.int32)
    start = jnp.int32(0)
    for index in range(lens_ref.shape[1]):
        count = count + (start <= positions).astype(jnp.int32)
        start = start + lens_ref[0, index]
    return count


def doc_scalar(lens_ref, position):
    count = jnp.int32(0)
    start = jnp.int32(0)
    for index in range(lens_ref.shape[1]):
        count = count + jnp.where(start <= position, 1, 0)
        start = start + lens_ref[0, index]
    return count


def doc_start(lens_ref, position):
    found = jnp.int32(0)
    start = jnp.int32(0)
    for index in range(lens_ref.shape[1]):
        found = jnp.where(start <= position, start, found)
        start = start + lens_ref[0, index]
    return found


def leads():
    return lax.rem(lax.axis_index("ctx"), 2) == 0


AUX = (
    "dt", "gate", "cum", "dout", "alpha_s", "beta_s", "alpha_u", "beta_u", "rate", "doc", "masks",
    "short",
)
LOCAL = ("first", "x_gb", "skip")
FAR = ("z_own", "w_own", "z_far", "w_far", "carried")


def take(ref, names, name, heads):
    slot = names.index(name) * heads
    return ref[slot : slot + heads, :]


def put(ref, names, heads, values):
    for name, value in values.items():
        slot = names.index(name) * heads
        ref[slot : slot + heads, :] = value


def halves(upper, lower, rows):
    width = upper.shape[1]
    return jnp.concatenate(
        [jnp.broadcast_to(item, (rows // 2, width)) for item in (upper, lower)], axis=0
    )


def prep_kernel(
    lens_hbm, raw_hbm, bias_hbm, alog_hbm, skip_hbm, x_hbm, g_hbm, b_hbm, c_hbm,
    pay_one_ref, pay_two_ref, aux_ref, xs_ref, gs_ref, x_ref, g_ref, b_ref, c_ref, tot_ref,
    gain_ref, lens_ref, raw_ref, bias_ref, alog_ref, skip_ref, sems,
):
    moves = (
        (lens_hbm, lens_ref), (raw_hbm.at[0], raw_ref), (bias_hbm, bias_ref),
        (alog_hbm, alog_ref), (skip_hbm, skip_ref), (x_hbm.at[0], x_ref), (g_hbm.at[0], g_ref),
        (b_hbm.at[0], b_ref), (c_hbm.at[0], c_ref),
    )
    copies = [
        pltpu.make_async_copy(source, target, sems.at[index])
        for index, (source, target) in enumerate(moves)
    ]
    for copy in copies:
        copy.start()
    small, large = copies[:5], copies[5:]
    span, features = x_ref.shape
    heads = raw_ref.shape[0]
    row, column = iota((span, span), 0), iota((span, span), 1)
    upto = (row <= column).astype(F32)
    beyond = (row > column).astype(F32)
    rows = head_rows(heads, features)
    for copy in small:
        copy.wait()
    base = lax.axis_index("ctx") * span
    doc = doc_of(lens_ref, base + iota((1, span), 1))
    before = doc_scalar(lens_ref, base - 1)
    last = doc_scalar(lens_ref, base + span - 1)
    inward = (doc == before).astype(F32)
    outward = (doc == last).astype(F32)
    whole = jnp.where(last == before, 1.0, 0.0)
    short_before = jnp.where(base - doc_start(lens_ref, base - 1) <= span // 2, 1.0, 0.0)
    short_last = jnp.where(
        base + span - doc_start(lens_ref, base + span - 1) <= span // 2, 1.0, 0.0
    )
    preact = raw_ref[...] + as_column(bias_ref[...])
    dt = jnp.maximum(preact, 0.0) + jnp.log1p(jnp.exp(-jnp.abs(preact)))
    gate = 1.0 / (1.0 + jnp.exp(-preact))
    rate = -jnp.exp(as_column(alog_ref[...]))
    cum = nn(dt * rate, upto, EXACT)
    cum_last = cum[:, span - 1 : span]
    din = inward * jnp.exp(cum)
    dout = outward * jnp.exp(cum_last - cum)
    tot_ref[...] = jnp.broadcast_to(
        spread_row(as_row(whole * jnp.exp(cum_last)), features), tot_ref.shape
    )
    pair = jnp.concatenate([dt, gate], axis=0)
    seen = nn(pair * inward, upto, EXACT)
    left = nn(pair * outward, beyond, EXACT)
    alpha_s = rate * left[:heads]
    beta_s = rate * left[heads:] + gate / dt
    alpha_u = rate * seen[:heads]
    beta_u = rate * seen[heads:]
    put(aux_ref, AUX, heads, dict(
        dt=dt, gate=gate, cum=cum, dout=dout,
        alpha_s=alpha_s, beta_s=beta_s, alpha_u=alpha_u, beta_u=beta_u,
        rate=jnp.broadcast_to(rate, dt.shape), doc=jnp.broadcast_to(doc.astype(F32), dt.shape),
        masks=halves(inward, outward, heads),
        short=halves(jnp.full((1, span), short_before), jnp.full((1, span), short_last), heads),
    ))
    gain_ref[...] = jnp.broadcast_to(spread_row(skip_ref[...], features), gain_ref.shape)
    x_factor, g_factor = spread(dout * dt, rows), spread(din, rows)
    for copy in large:
        copy.wait()
    xs = (x_ref[...].astype(F32) * x_factor).astype(BF16)
    gs = (g_ref[...].astype(F32) * g_factor).astype(BF16)
    xs_ref[...] = xs
    gs_ref[...] = gs

    def fill(ref, scaled, wide, small):
        blocks = features // LANES
        for block in range(blocks):
            ref[block * span : (block + 1) * span, :] = scaled[
                :, block * LANES : (block + 1) * LANES
            ].astype(F32)
        base = blocks * span
        ref[base : base + span, :] = wide.astype(F32)
        base = base + span
        for part in small:
            ref[base : base + heads, :] = part
            base = base + heads

    first = leads()

    @pl.when(first)
    def _():
        fill(pay_one_ref, xs, b_ref[...], (alpha_s, beta_s))
        fill(pay_two_ref, gs, c_ref[...], (alpha_u, beta_u))

    @pl.when(jnp.logical_not(first))
    def _():
        fill(pay_one_ref, gs, c_ref[...], (alpha_u, beta_u))
        fill(pay_two_ref, xs, b_ref[...], (alpha_s, beta_s))


def local_kernel(
    x_ref, g_ref, aux_ref, b_ref, c_ref, gb_ref, small_ref, grads_ref, own_ref
):
    span, features = x_ref.shape
    heads = aux_ref.shape[0] // len(AUX)
    width = features // heads
    row, column = iota((span, span), 0), iota((span, span), 1)
    dt = take(aux_ref, AUX, "dt", heads)
    gate = take(aux_ref, AUX, "gate", heads)
    cum = take(aux_ref, AUX, "cum", heads)
    rate = take(aux_ref, AUX, "rate", heads)
    doc = take(aux_ref, AUX, "doc", heads)
    upright = nt(eye(span), jnp.concatenate([dt, cum, doc], axis=0), EXACT)
    doc_s = upright[:, 2 * heads : 2 * heads + 1]
    closed = jnp.where((column >= row) & (jnp.abs(doc_s - doc[:1, :]) < 0.5), 0.0, -1e30)
    scores = nt(b_ref[...], c_ref[...])
    summed = jnp.zeros((span, span), F32)
    lane = iota((span, heads), 1)
    from_s = jnp.zeros((span, heads), F32)
    to_u = []
    for pair in range(0, heads, 2):
        outs = []
        for head in (pair, pair + 1):
            part = slice(head * width, (head + 1) * width)
            g_head, x_head = g_ref[:, part], x_ref[:, part]
            cross = nt(x_head, g_head)
            cum_s = upright[:, heads + head : heads + head + 1]
            decay = jnp.exp(cum[head : head + 1, :] - cum_s + closed)
            masked = decay * scores
            weighted = decay * cross * upright[:, head : head + 1]
            summed = summed + weighted
            product = weighted * scores
            from_s = jnp.where(lane == head, jnp.sum(product, axis=1, keepdims=True), from_s)
            to_u.append(jnp.sum(product, axis=0, keepdims=True))
            outs.append(nn(masked.astype(BF16), g_head))
        gb_ref[:, pair * width : (pair + 2) * width] = jnp.concatenate(outs, axis=1)
    onward = (row >= column).astype(F32)
    turn = eye(heads)
    change = jnp.concatenate(to_u, axis=0) - nt(turn, from_s, EXACT)
    first = nn(change, onward, EXACT)
    columns = head_columns(features, heads)
    x_wide = x_ref[...].astype(F32)
    sums = jnp.concatenate(
        [head_sum(x_wide * gb_ref[...], columns),
         head_sum(x_wide * g_ref[...].astype(F32), columns)], axis=1
    )
    sums = nt(eye(2 * heads), sums, EXACT)
    x_gb, skip = sums[:heads], sums[heads:]
    put(small_ref, LOCAL, heads, dict(first=first, x_gb=x_gb, skip=skip))
    own_ref[:heads, :] = rate * dt * first
    own_ref[heads : 2 * heads, :] = gate * (x_gb + rate * first)
    own_ref[2 * heads :, :] = skip
    grads_ref[:span, :] = nn(summed.astype(BF16), c_ref[...])
    grads_ref[span:, :] = nn(jnp.transpose(summed).astype(BF16), b_ref[...])


def neighbours(one_ref, two_ref):
    first = leads()

    def behind(part):
        return jnp.where(first, two_ref[part, :], one_ref[part, :])

    def ahead(part):
        return jnp.where(first, one_ref[part, :], two_ref[part, :])

    return behind, ahead


def wide(get, span, blocks):
    return jnp.concatenate(
        [get(slice(k * span, (k + 1) * span)).astype(BF16) for k in range(blocks)], axis=1
    )


def relay_kernel(
    got_one_ref, got_two_ref, xs_ref, gs_ref, aux_ref, b_ref, c_ref, own_ref, tot_ref,
    red_ref, far_ref, push_ref, far_push_ref, xp_ref, gn_ref, bp_ref, cn_ref,
):
    span, features = xs_ref.shape
    heads = aux_ref.shape[0] // len(AUX)
    blocks = features // LANES
    behind, ahead = neighbours(got_one_ref, got_two_ref)
    base = blocks * span
    xp, bp = wide(behind, span, blocks), behind(slice(base, base + span)).astype(BF16)
    gn, cn = wide(ahead, span, blocks), ahead(slice(base, base + span)).astype(BF16)
    base = base + span
    alpha_p = behind(slice(base, base + heads))
    beta_p = behind(slice(base + heads, base + 2 * heads))
    alpha_n = ahead(slice(base, base + heads))
    beta_n = ahead(slice(base + heads, base + 2 * heads))
    xs, gs, b, c = xs_ref[...], gs_ref[...], b_ref[...], c_ref[...]
    columns = head_columns(features, heads)
    gn_tot = (gn.astype(F32) * tot_ref[:1, :]).astype(BF16)

    pull = nn(nt(c, bp).astype(BF16), xp)
    push = nn(nt(b, cn).astype(BF16), gn)
    far_pull = nn(nt(cn, bp).astype(BF16), xp)
    far_push = nn(nt(bp, cn).astype(BF16), gn_tot)
    products = [
        gs.astype(F32) * pull,
        xs.astype(F32) * push,
        gn_tot.astype(F32) * far_pull,
        xp.astype(F32) * far_push,
    ]
    sums = jnp.concatenate([nn(item.astype(BF16), columns) for item in products], axis=1)
    sums = nt(eye(4 * heads), sums, EXACT)
    z_own, w_own, z_far, w_far = (sums[k * heads : (k + 1) * heads] for k in range(4))
    carried = jnp.sum(z_far, axis=1, keepdims=True)
    rate = take(aux_ref, AUX, "rate", heads)
    alog = (
        own_ref[:heads, :]
        + z_own * take(aux_ref, AUX, "alpha_u", heads)
        + w_own * take(aux_ref, AUX, "alpha_s", heads)
        + carried * rate * take(aux_ref, AUX, "dt", heads)
        + z_far * alpha_n
        + w_far * alpha_p
    )
    bias = (
        own_ref[heads : 2 * heads, :]
        + z_own * take(aux_ref, AUX, "beta_u", heads)
        + w_own * take(aux_ref, AUX, "beta_s", heads)
        + carried * rate * take(aux_ref, AUX, "gate", heads)
        + z_far * beta_n
        + w_far * beta_p
    )
    stack = jnp.concatenate([alog, bias, own_ref[2 * heads :, :]], axis=0)
    red_ref[:, : 3 * heads] = nt(jnp.ones((8, span), F32), stack, EXACT)
    red_ref[:, 3 * heads :] = jnp.zeros((8, red_ref.shape[1] - 3 * heads), F32)
    put(far_ref, FAR, heads, dict(
        z_own=z_own, w_own=w_own, z_far=z_far, w_far=w_far,
        carried=jnp.broadcast_to(carried, z_own.shape),
    ))
    push_ref[...] = push
    far_push_ref[...] = far_push
    xp_ref[...] = xp
    gn_ref[...] = gn
    bp_ref[...] = bp
    cn_ref[...] = cn


def grads_kernel(
    xp_ref, gn_ref, bp_ref, cn_ref, xs_ref, gs_ref, aux_ref, grads_ref, far_ref, far_push_ref,
    tot_ref, hop_one_ref, hop_two_ref, sums_ref,
):
    span, features = xs_ref.shape
    blocks = features // LANES
    heads = far_ref.shape[0] // len(FAR)
    xp, gn, bp, cn = xp_ref[...], gn_ref[...], bp_ref[...], cn_ref[...]
    gn_tot = (gn.astype(F32) * tot_ref[:1, :]).astype(BF16)
    sums_ref[:span, :] = grads_ref[:span, :] + nn(nt(xs_ref[...], gn).astype(BF16), cn)
    sums_ref[span:, :] = grads_ref[span:, :] + nn(nt(gs_ref[...], xp).astype(BF16), bp)
    grad_b_far = nn(nt(xp, gn_tot).astype(BF16), cn)
    grad_c_far = nn(nt(gn_tot, xp).astype(BF16), bp)
    half = span // 2
    base = blocks * half
    short = take(aux_ref, AUX, "short", heads)[:1, :] > 0.5

    def fill(ref, grad, name, heavy):
        if heavy:
            for block in range(blocks):
                part = slice(block * LANES, (block + 1) * LANES)
                ref[block * half : (block + 1) * half, :] = jnp.where(
                    short, far_push_ref[half:, part], gn_tot[:half, part].astype(F32)
                )
            ref[base : base + half, :] = cn[:half].astype(F32)
        else:
            ref[: base + half, :] = jnp.zeros((base + half, LANES), F32)
        rest = base + half
        ref[rest : rest + span, :] = grad
        ref[rest + span : rest + span + heads, :] = take(far_ref, FAR, name, heads)

    first = leads()

    @pl.when(first)
    def _():
        fill(hop_one_ref, grad_c_far, "z_far", False)
        fill(hop_two_ref, grad_b_far, "w_far", True)

    @pl.when(jnp.logical_not(first))
    def _():
        fill(hop_one_ref, grad_b_far, "w_far", True)
        fill(hop_two_ref, grad_c_far, "z_far", False)


def final_kernel(
    far_one_ref, far_two_ref, g_ref, b_ref, aux_ref, gain_ref, gbl_ref, push_ref, small_ref, far_ref,
    sums_ref, gx_ref, gdt_ref, half_ref,
):
    span, features = g_ref.shape
    heads = aux_ref.shape[0] // len(AUX)
    blocks = features // LANES
    half = span // 2
    behind, ahead = neighbours(far_one_ref, far_two_ref)
    base = blocks * half
    short = take(aux_ref, AUX, "short", heads)[heads // 2 : heads // 2 + 1, :] > 0.5
    cn = ahead(slice(base, base + half)).astype(BF16)
    scores = nt(b_ref[...], cn).astype(BF16)
    parts = [ahead(slice(k * half, (k + 1) * half)) for k in range(blocks)]
    other = nn(scores, jnp.concatenate(parts, axis=1).astype(BF16))
    blank = jnp.zeros((half, LANES), F32)
    push = push_ref[...] + jnp.concatenate(
        [
            jnp.where(
                short,
                jnp.concatenate([blank, part], axis=0),
                other[:, k * LANES : (k + 1) * LANES],
            )
            for k, part in enumerate(parts)
        ],
        axis=1,
    )
    rows = head_rows(heads, features)
    dt = take(aux_ref, AUX, "dt", heads)
    gate = take(aux_ref, AUX, "gate", heads)
    dout = take(aux_ref, AUX, "dout", heads)
    rate = take(aux_ref, AUX, "rate", heads)
    gx_ref[0] = (
        spread(dt, rows) * gbl_ref[...]
        + spread(dt * dout, rows) * push
        + gain_ref[:1, :] * g_ref[...].astype(F32)
    ).astype(BF16)
    inout = take(aux_ref, AUX, "masks", heads)
    inward, outward = inout[:1, :], inout[heads // 2 : heads // 2 + 1, :]
    rest = base + half
    z = take(far_ref, FAR, "z_own", heads) + behind(slice(rest + span, rest + span + heads))
    w = take(far_ref, FAR, "w_own", heads) + ahead(slice(rest + span, rest + span + heads))
    row, column = iota((span, span), 0), iota((span, span), 1)
    decay_grad = (
        take(small_ref, LOCAL, "first", heads)
        + inward * nn(z, (row >= column).astype(F32), EXACT)
        + outward * nn(w, (row < column).astype(F32), EXACT)
        + take(far_ref, FAR, "carried", heads)
    )
    x_gb = take(small_ref, LOCAL, "x_gb", heads) + w / dt
    gdt_ref[0] = (x_gb + rate * decay_grad) * gate
    half_ref[:span, :] = sums_ref[:span, :] + ahead(slice(rest, rest + span))
    half_ref[span:, :] = sums_ref[span:, :] + behind(slice(rest, rest + span))


def close_kernel(*refs):
    count = len(refs) - 5
    b_ref, c_ref, alog_ref, bias_ref, skip_ref = refs[count:]
    span = b_ref.shape[1]
    heads = alog_ref.shape[1]
    red = refs[0][:1, :] + refs[1][:1, :]
    alog_ref[...] = red[:, :heads]
    bias_ref[...] = red[:, heads : 2 * heads]
    skip_ref[...] = red[:, 2 * heads : 3 * heads]
    total = refs[2][...]
    for other in refs[3:count]:
        total = total + other[...]
    b_ref[0] = total[:span]
    c_ref[0] = total[span:]


def call(kernel, shapes, operands, raw=0, flops=0, scratch=()):
    def space(index):
        return pltpu.HBM if index < raw else pltpu.VMEM

    moved = sum(item.size * item.dtype.itemsize for item in operands) + sum(
        item.size * jnp.dtype(item.dtype).itemsize for item in shapes
    )
    return pl.pallas_call(
        kernel,
        out_shape=shapes,
        in_specs=[pl.BlockSpec(memory_space=space(index)) for index in range(len(operands))],
        out_specs=[pl.BlockSpec(memory_space=pltpu.VMEM)] * len(shapes),
        scratch_shapes=list(scratch),
        cost_estimate=pl.CostEstimate(flops=flops, bytes_accessed=moved, transcendentals=0),
        compiler_params=pltpu.CompilerParams(vmem_limit_bytes=VMEM_GRANT),
    )(
        *(
            pltpu.with_memory_space_constraint(item, pltpu.HBM) if index < raw else item
            for index, item in enumerate(operands)
        )
    )


def exchange(array, turn, senders):
    count = lax.axis_size("ctx")
    pairs = [(i, i + 1 if (i + turn) % 2 == 0 else i - 1) for i in range(count)]
    return lax.ppermute(
        array, "ctx", [(i, j) for i, j in pairs if 0 <= j < count and i in senders]
    )


def flip(array, axis, bit):
    return lax.ppermute(array, axis, [(i, i ^ bit) for i in range(lax.axis_size(axis))])


def near_local(inputs, dt_raw, dt_bias, a_log, b_in, c_in, skip_gain, grad_out, doc_lengths):
    _, span, features = inputs.shape
    heads = dt_bias.shape[0]
    state = b_in.shape[2]
    count = lax.axis_size("ctx")
    struct = jax.ShapeDtypeStruct
    bias, alog, skip = (item.reshape(1, heads) for item in (dt_bias, a_log, skip_gain))
    raw = jnp.swapaxes(dt_raw, 1, 2)
    base = features // LANES * span + span
    pay = struct((base + 2 * heads, LANES), F32)
    full, low = struct((span, features), F32), struct((span, features), BF16)
    line = struct((8, features), F32)
    square = struct((span, state), BF16)
    pair = struct((2 * span, state), F32)
    one_row = pltpu.VMEM((1, heads), F32)
    pay_one, pay_two, aux, xs, gs, x, g, b, c, tot, gain = call(
        prep_kernel,
        (pay, pay, struct((len(AUX) * heads, span), F32), low, low, low, low, square, square, line,
         line),
        (doc_lengths, raw, bias, alog, skip, inputs, grad_out, b_in, c_in),
        raw=9, flops=10**8,
        scratch=[pltpu.SMEM(doc_lengths.shape, jnp.int32), pltpu.VMEM((heads, span), F32),
                 one_row, one_row, one_row, pltpu.SemaphoreType.DMA((9,))],
    )
    got_one = exchange(pay_one, 0, range(count))
    got_two = exchange(pay_two, 1, range(count))
    gb_local, small, grads, own = call(
        local_kernel,
        (full, struct((len(LOCAL) * heads, span), F32), pair, struct((3 * heads, span), F32)),
        (x, g, aux, b, c),
        flops=10**8,
    )
    red, far, push, far_push, xp, gn, bp, cn = call(
        relay_kernel,
        (struct((8, LANES), F32), struct((len(FAR) * heads, span), F32), full, full, low, low,
         square, square),
        (got_one, got_two, xs, gs, aux, b, c, own, tot),
        flops=10**8,
    )
    steps = []
    for axis in ("dp", "ctx"):
        bit = 1
        while bit < lax.axis_size(axis):
            steps.append((axis, bit))
            bit *= 2
    hop = struct((base // 2 + span + heads, LANES), F32)
    hop_one, hop_two, sums = call(
        grads_kernel,
        (hop, hop, pair),
        (xp, gn, bp, cn, xs, gs, aux, grads, far, far_push, tot),
        flops=10**8,
    )
    hop_one, hop_two, red = lax.optimization_barrier((hop_one, hop_two, red))
    relays = range(1, count - 1)
    far_two = exchange(hop_two, 1, relays)
    far_one = exchange(hop_one, 0, relays)
    for axis, bit in steps[:-2]:
        red = red + flip(red, axis, bit)
    far_one, far_two, red = lax.optimization_barrier((far_one, far_two, red))
    red = red + flip(red, *steps[-2])
    last_red = flip(red, *steps[-1])
    grad_x, grad_dt, half = call(
        final_kernel,
        (struct((1, span, features), BF16), struct((1, heads, span), F32), pair),
        (far_one, far_two, g, b, aux, gain, gb_local, push, small, far, sums),
        flops=10**8,
    )
    sides = lax.axis_size("head")
    others = [
        lax.ppermute(half, "head", [(i, (i + step) % sides) for i in range(sides)])
        for step in range(1, sides)
    ]
    flat = struct((1, heads), F32)
    cube = struct((1, span, state), F32)
    b_total, c_total, alog_total, bias_total, skip_total = call(
        close_kernel, (cube, cube, flat, flat, flat), (red, last_red, half, *others)
    )
    return (
        grad_x, jnp.swapaxes(grad_dt, 1, 2), b_total, c_total,
        alog_total.reshape(heads), bias_total.reshape(heads), skip_total.reshape(heads),
    )


def local(inputs, dt_raw, dt_bias, a_log, b_in, c_in, skip_gain, grad_out, doc_lengths):
    args = (inputs, dt_raw, dt_bias, a_log, b_in, c_in, skip_gain, grad_out, doc_lengths)
    shards = [lax.axis_size(axis) for axis in ("dp", "ctx")]
    near = (
        inputs.shape[1] == SPAN
        and shards[1] in (2, 4)
        and shards[0] & (shards[0] - 1) == 0
        and b_in.shape[2] == LANES
        and inputs.shape[2] % LANES == 0
        and dt_bias.shape[0] * 8 == LANES
    )
    if not near:
        return general_local(*args)
    return near_local(*args)


def solution(mesh):
    placed = (
        P("dp", "ctx", "head"),
        P("dp", "ctx", "head"),
        P("head"),
        P("head"),
        P("dp", "ctx", None),
        P("dp", "ctx", None),
        P("head"),
        P("dp", "ctx", "head"),
        P("dp", None),
    )
    return jax.shard_map(
        local,
        mesh=mesh,
        in_specs=placed,
        out_specs=(
            P("dp", "ctx", "head"),
            P("dp", "ctx", "head"),
            P("dp", "ctx", None),
            P("dp", "ctx", None),
            P("head"),
            P("head"),
            P("head"),
        ),
        check_vma=False,
    )
```

```python
import jax
import jax.numpy as jnp
from jax import lax
from jax.experimental import pallas as pl
from jax.experimental.pallas import tpu as pltpu
from jax.sharding import PartitionSpec as P


SPAN = 128
LANES = 128
VMEM_GRANT = 16 << 20
F32 = jnp.float32
BF16 = jnp.bfloat16
EXACT = lax.Precision.HIGHEST


def from_behind(array, axis, by):
    count = lax.axis_size(axis)
    pairs = [(i, i + by) for i in range(count) if 0 <= i + by < count]
    return lax.ppermute(array, axis, pairs)


def reverse_cumsum(values, along_axis):
    return jnp.flip(jnp.cumsum(jnp.flip(values, along_axis), axis=along_axis), along_axis)


def doc_index(positions, starts):
    return jnp.sum((starts[None, :] <= positions[:, None]).astype(jnp.int32), axis=1)


def vector_factors(decay_block, segment_block, previous_block):
    cumulative = jnp.cumsum(decay_block, axis=0)
    last_segment = segment_block[-1]
    mask_in = (segment_block == previous_block).astype(jnp.float32)
    mask_out = (segment_block == last_segment).astype(jnp.float32)
    factor_in = mask_in[:, None] * jnp.exp(cumulative)
    factor_out = mask_out[:, None] * jnp.exp(cumulative[-1][None, :] - cumulative)
    span_total = (last_segment == previous_block).astype(jnp.float32) * jnp.exp(cumulative[-1])
    return (cumulative, mask_in, mask_out, factor_in, factor_out, span_total)


def pair_factor(cumulative, segment_block):
    local_pos = jnp.arange(segment_block.shape[0], dtype=jnp.int32)
    allowed = (local_pos[:, None] >= local_pos[None, :]) & (
        segment_block[:, None] == segment_block[None, :]
    )
    spread = cumulative.T[:, :, None] - cumulative.T[:, None, :]
    return jnp.where(allowed[None], jnp.exp(jnp.where(allowed[None], spread, 0.0)), 0.0)


def first_pass(
    inputs_block,
    grads_block,
    b_block,
    c_block,
    step_block,
    decay_block,
    segment_block,
    previous_block,
):
    _, _, _, factor_in, factor_out, span_total = vector_factors(
        decay_block, segment_block, previous_block
    )
    scaled_in = (inputs_block * (factor_out * step_block)[:, :, None]).astype(jnp.bfloat16)
    scaled_grad = (grads_block * factor_in[:, :, None]).astype(jnp.bfloat16)
    state_part = jnp.einsum("shp,sn->hpn", scaled_in, b_block, preferred_element_type=jnp.float32)
    grad_part = jnp.einsum("uhp,un->hpn", scaled_grad, c_block, preferred_element_type=jnp.float32)
    return (span_total, state_part, grad_part)


def span_grads(
    inputs_block,
    grads_block,
    b_block,
    c_block,
    step_block,
    decay_block,
    segment_block,
    previous_block,
    preact_block,
    state_in,
    state_grad,
    decay_rate,
    skip_gain,
):
    cumulative, mask_in, mask_out, factor_in, factor_out, _ = vector_factors(
        decay_block, segment_block, previous_block
    )
    pair_decay = pair_factor(cumulative, segment_block)
    scores = jnp.einsum("un,sn->us", c_block, b_block, preferred_element_type=jnp.float32)
    cross_term = jnp.einsum(
        "uhp,shp->hus", grads_block, inputs_block, preferred_element_type=jnp.float32
    )
    masked = (pair_decay * scores[None]).astype(jnp.bfloat16)
    weighted = pair_decay * cross_term * step_block.T[:, None, :]
    summed = jnp.sum(weighted, axis=0).astype(jnp.bfloat16)
    products = weighted * scores[None]
    change = jnp.sum(products, axis=2) - jnp.sum(products, axis=1)
    first_term = reverse_cumsum(change, 1).T
    h_low = state_in.astype(jnp.bfloat16)
    e_low = state_grad.astype(jnp.bfloat16)
    along_b = jnp.einsum("tn,hpn->thp", b_block, e_low, preferred_element_type=jnp.float32)
    grad_b_prod = (
        jnp.einsum("hut,uhp->thp", masked, grads_block, preferred_element_type=jnp.float32)
        + factor_out[:, :, None] * along_b
    )
    grad_x = (step_block[:, :, None] * grad_b_prod + skip_gain[None, :, None] * grads_block).astype(
        jnp.bfloat16
    )
    x_state = jnp.einsum("thp,hpn->thn", inputs_block, e_low, preferred_element_type=jnp.float32)
    y_state = jnp.einsum("uhp,hpn->uhn", grads_block, h_low, preferred_element_type=jnp.float32)
    grad_b = jnp.einsum("us,un->sn", summed, c_block, preferred_element_type=jnp.float32) + jnp.sum(
        (step_block * factor_out)[:, :, None] * x_state, axis=1
    )
    grad_c = jnp.einsum("us,sn->un", summed, b_block, preferred_element_type=jnp.float32) + jnp.sum(
        factor_in[:, :, None] * y_state, axis=1
    )
    z_term = jnp.sum(y_state * c_block[:, None, :], axis=2)
    w_term = step_block * jnp.sum(x_state * b_block[:, None, :], axis=2)
    second_term = mask_in[:, None] * reverse_cumsum(factor_in * z_term, 0)
    carried = factor_out * w_term
    third_term = mask_out[:, None] * (jnp.cumsum(carried, axis=0) - carried)
    fourth_term = factor_out * factor_in * jnp.sum(state_grad * state_in, axis=(1, 2))[None, :]
    decay_grad = first_term + second_term + third_term + fourth_term
    x_dot_g = jnp.sum(inputs_block * grad_b_prod, axis=2)
    grad_dt = (x_dot_g + decay_rate[None, :] * decay_grad) * jax.nn.sigmoid(preact_block)
    grad_alog = jnp.sum(decay_grad * step_block, axis=0) * decay_rate
    grad_bias = jnp.sum(grad_dt, axis=0)
    grad_skip = jnp.einsum(
        "thp,thp->h", grads_block, inputs_block, preferred_element_type=jnp.float32
    )
    return (grad_x, grad_dt, grad_b, grad_c, grad_alog, grad_bias, grad_skip)


def local_link(running, pieces):
    decay_gain, held_state = running
    span_total, span_part = pieces
    return ((decay_gain * span_total, span_total[:, None, None] * held_state + span_part), running)


def link_maps(earlier, later):
    return (earlier[0] * later[0], later[0][:, None, None] * earlier[1] + later[1])


def doubling(element, reverse):
    axis_count = lax.axis_size("ctx")
    own_index = lax.axis_index("ctx")
    distances = [1] + [2**power for power in range((axis_count - 1).bit_length())]
    running = element
    for section_num, distance in enumerate(distances):
        shift_by = -distance if reverse else distance
        received = from_behind((running[0], running[1]), "ctx", shift_by)
        source = own_index - shift_by
        present = (source >= 0) & (source < axis_count)
        fixed = (jnp.where(present, received[0], 1.0), received[1])
        if section_num == 0:
            running = fixed
        else:
            running = link_maps(fixed, running)
    return running


def general_local(inputs, dt_raw, dt_bias, a_log, b_in, c_in, skip_gain, grad_out, doc_lengths):
    token_count = inputs.shape[1]
    head_count = dt_bias.shape[0]
    head_width = inputs.shape[2] // head_count
    state_size = b_in.shape[2]
    span_count = token_count // SPAN
    preact = dt_raw[0] + dt_bias[None, :]
    step_size = jax.nn.softplus(preact)
    decay_rate = -jnp.exp(a_log)
    log_decay = step_size * decay_rate[None, :]
    lengths = doc_lengths[0]
    starts = jnp.cumsum(lengths) - lengths
    positions = lax.axis_index("ctx") * token_count + jnp.arange(token_count, dtype=jnp.int32)
    segment = doc_index(positions, starts)
    previous = doc_index(positions[::SPAN] - 1, starts)
    shaped = (
        inputs[0].reshape(span_count, SPAN, head_count, head_width),
        grad_out[0].reshape(span_count, SPAN, head_count, head_width),
        b_in[0].reshape(span_count, SPAN, state_size),
        c_in[0].reshape(span_count, SPAN, state_size),
        step_size.reshape(span_count, SPAN, head_count),
        log_decay.reshape(span_count, SPAN, head_count),
        segment.reshape(span_count, SPAN),
        previous,
    )
    totals, state_parts, grad_parts = jax.vmap(first_pass)(*shaped)
    start_maps = (
        jnp.ones((head_count,), jnp.float32),
        jnp.zeros((head_count, head_width, state_size), jnp.float32),
    )
    forward_map, (gain_before, local_entry) = lax.scan(
        local_link, start_maps, (totals, state_parts)
    )
    backward_map, (gain_after, local_leave) = lax.scan(
        local_link, start_maps, (totals, grad_parts), reverse=True
    )
    entry_state = doubling(forward_map, False)[1]
    leave_state = doubling(backward_map, True)[1]
    entering = gain_before[:, :, None, None] * entry_state[None] + local_entry
    leaving = gain_after[:, :, None, None] * leave_state[None] + local_leave
    mapped = jax.vmap(span_grads, in_axes=(0, 0, 0, 0, 0, 0, 0, 0, 0, 0, 0, None, None))
    grad_x, grad_dt, grad_b, grad_c, grad_alog, grad_bias, grad_skip = mapped(
        *shaped,
        preact.reshape(span_count, SPAN, head_count),
        entering,
        leaving,
        decay_rate,
        skip_gain
    )
    b_total, c_total = lax.psum(
        (grad_b.reshape(token_count, state_size), grad_c.reshape(token_count, state_size)), "head"
    )
    alog_total, bias_total, skip_total = lax.psum(
        (jnp.sum(grad_alog, axis=0), jnp.sum(grad_bias, axis=0), jnp.sum(grad_skip, axis=0)),
        ("dp", "ctx"),
    )
    return (
        grad_x.reshape(1, token_count, head_count * head_width),
        grad_dt,
        b_total[None],
        c_total[None],
        alog_total,
        bias_total,
        skip_total,
    )


def dot(left, right, dims, precision=None):
    return lax.dot_general(
        left, right, (dims, ((), ())), precision=precision, preferred_element_type=F32
    )


def nn(left, right, precision=None):
    return dot(left, right, ((1,), (0,)), precision)


def nt(left, right, precision=None):
    return dot(left, right, ((1,), (1,)), precision)


def tn(left, right, precision=None):
    return dot(left, right, ((0,), (0,)), precision)


def iota(shape, axis):
    return lax.broadcasted_iota(jnp.int32, shape, axis)


def eye(size):
    return (iota((size, size), 0) == iota((size, size), 1)).astype(F32)


def head_rows(heads, features):
    width = features // heads
    start = iota((heads, features), 0) * width
    feature = iota((heads, features), 1)
    return ((feature >= start) & (feature < start + width)).astype(BF16)


def head_columns(features, heads):
    width = features // heads
    start = iota((features, heads), 1) * width
    feature = iota((features, heads), 0)
    return ((feature >= start) & (feature < start + width)).astype(BF16)


def thirds(value):
    high = value.astype(BF16)
    rest = value - high.astype(F32)
    middle = rest.astype(BF16)
    low = (rest - middle.astype(F32)).astype(BF16)
    return jnp.concatenate([high, middle, low], axis=0)


def spread(factor, rows):
    return tn(thirds(factor), jnp.concatenate([rows] * 3, axis=0))


def spread_row(factor, features):
    heads = factor.shape[1]
    wide = jnp.broadcast_to(factor, (8, heads))
    high = wide.astype(BF16)
    rest = wide - high.astype(F32)
    middle = rest.astype(BF16)
    low = (rest - middle.astype(F32)).astype(BF16)
    rows = head_rows(heads, features)
    return (nn(high, rows) + nn(middle, rows) + nn(low, rows))[:1]


def head_sum(values, columns):
    high = values.astype(BF16)
    low = (values - high.astype(F32)).astype(BF16)
    return nn(high, columns) + nn(low, columns)


def as_column(row):
    size = row.shape[1]
    return jnp.sum(jnp.where(eye(size) > 0, row, 0.0), axis=1, keepdims=True)


def as_row(column):
    size = column.shape[0]
    return jnp.sum(jnp.where(eye(size) > 0, column, 0.0), axis=0, keepdims=True)


def doc_of(lens_ref, positions):
    count = jnp.zeros(positions.shape, jnp.int32)
    start = jnp.int32(0)
    for index in range(lens_ref.shape[1]):
        count = count + (start <= positions).astype(jnp.int32)
        start = start + lens_ref[0, index]
    return count


def doc_scalar(lens_ref, position):
    count = jnp.int32(0)
    start = jnp.int32(0)
    for index in range(lens_ref.shape[1]):
        count = count + jnp.where(start <= position, 1, 0)
        start = start + lens_ref[0, index]
    return count


def doc_start(lens_ref, position):
    found = jnp.int32(0)
    start = jnp.int32(0)
    for index in range(lens_ref.shape[1]):
        found = jnp.where(start <= position, start, found)
        start = start + lens_ref[0, index]
    return found


def leads():
    return lax.rem(lax.axis_index("ctx"), 2) == 0


AUX = (
    "dt", "gate", "cum", "dout", "alpha_s", "beta_s", "alpha_u", "beta_u", "rate", "doc", "masks",
    "short",
)
LOCAL = ("first", "x_gb", "skip")
FAR = ("z_own", "w_own", "z_far", "w_far", "carried")


def take(ref, names, name, heads):
    slot = names.index(name) * heads
    return ref[slot : slot + heads, :]


def put(ref, names, heads, values):
    for name, value in values.items():
        slot = names.index(name) * heads
        ref[slot : slot + heads, :] = value


def halves(upper, lower, rows):
    width = upper.shape[1]
    return jnp.concatenate(
        [jnp.broadcast_to(item, (rows // 2, width)) for item in (upper, lower)], axis=0
    )


def prep_kernel(
    lens_hbm, raw_hbm, bias_hbm, alog_hbm, skip_hbm, x_hbm, g_hbm, b_hbm, c_hbm,
    pay_one_ref, pay_two_ref, aux_ref, xs_ref, gs_ref, x_ref, g_ref, b_ref, c_ref, tot_ref,
    gain_ref, lens_ref, raw_ref, bias_ref, alog_ref, skip_ref, sems,
):
    moves = (
        (lens_hbm, lens_ref), (raw_hbm.at[0], raw_ref), (bias_hbm, bias_ref),
        (alog_hbm, alog_ref), (skip_hbm, skip_ref), (x_hbm.at[0], x_ref), (g_hbm.at[0], g_ref),
        (b_hbm.at[0], b_ref), (c_hbm.at[0], c_ref),
    )
    copies = [
        pltpu.make_async_copy(source, target, sems.at[index])
        for index, (source, target) in enumerate(moves)
    ]
    for copy in copies:
        copy.start()
    small, large = copies[:5], copies[5:]
    span, features = x_ref.shape
    heads = raw_ref.shape[0]
    row, column = iota((span, span), 0), iota((span, span), 1)
    upto = (row <= column).astype(F32)
    beyond = (row > column).astype(F32)
    rows = head_rows(heads, features)
    for copy in small:
        copy.wait()
    base = lax.axis_index("ctx") * span
    doc = doc_of(lens_ref, base + iota((1, span), 1))
    before = doc_scalar(lens_ref, base - 1)
    last = doc_scalar(lens_ref, base + span - 1)
    inward = (doc == before).astype(F32)
    outward = (doc == last).astype(F32)
    whole = jnp.where(last == before, 1.0, 0.0)
    short_before = jnp.where(base - doc_start(lens_ref, base - 1) <= span // 2, 1.0, 0.0)
    short_last = jnp.where(
        base + span - doc_start(lens_ref, base + span - 1) <= span // 2, 1.0, 0.0
    )
    preact = raw_ref[...] + as_column(bias_ref[...])
    dt = jnp.maximum(preact, 0.0) + jnp.log1p(jnp.exp(-jnp.abs(preact)))
    gate = 1.0 / (1.0 + jnp.exp(-preact))
    rate = -jnp.exp(as_column(alog_ref[...]))
    cum = nn(dt * rate, upto, EXACT)
    cum_last = cum[:, span - 1 : span]
    din = inward * jnp.exp(cum)
    dout = outward * jnp.exp(cum_last - cum)
    tot_ref[...] = jnp.broadcast_to(
        spread_row(as_row(whole * jnp.exp(cum_last)), features), tot_ref.shape
    )
    pair = jnp.concatenate([dt, gate], axis=0)
    seen = nn(pair * inward, upto, EXACT)
    left = nn(pair * outward, beyond, EXACT)
    alpha_s = rate * left[:heads]
    beta_s = rate * left[heads:] + gate / dt
    alpha_u = rate * seen[:heads]
    beta_u = rate * seen[heads:]
    put(aux_ref, AUX, heads, dict(
        dt=dt, gate=gate, cum=cum, dout=dout,
        alpha_s=alpha_s, beta_s=beta_s, alpha_u=alpha_u, beta_u=beta_u,
        rate=jnp.broadcast_to(rate, dt.shape), doc=jnp.broadcast_to(doc.astype(F32), dt.shape),
        masks=halves(inward, outward, heads),
        short=halves(jnp.full((1, span), short_before), jnp.full((1, span), short_last), heads),
    ))
    gain_ref[...] = jnp.broadcast_to(spread_row(skip_ref[...], features), gain_ref.shape)
    x_factor, g_factor = spread(dout * dt, rows), spread(din, rows)
    for copy in large:
        copy.wait()
    xs = (x_ref[...].astype(F32) * x_factor).astype(BF16)
    gs = (g_ref[...].astype(F32) * g_factor).astype(BF16)
    xs_ref[...] = xs
    gs_ref[...] = gs

    def fill(ref, scaled, wide, small):
        blocks = features // LANES
        for block in range(blocks):
            ref[block * span : (block + 1) * span, :] = scaled[
                :, block * LANES : (block + 1) * LANES
            ].astype(F32)
        base = blocks * span
        ref[base : base + span, :] = wide.astype(F32)
        base = base + span
        for part in small:
            ref[base : base + heads, :] = part
            base = base + heads

    first = leads()

    @pl.when(first)
    def _():
        fill(pay_one_ref, xs, b_ref[...], (alpha_s, beta_s))
        fill(pay_two_ref, gs, c_ref[...], (alpha_u, beta_u))

    @pl.when(jnp.logical_not(first))
    def _():
        fill(pay_one_ref, gs, c_ref[...], (alpha_u, beta_u))
        fill(pay_two_ref, xs, b_ref[...], (alpha_s, beta_s))


def local_kernel(
    x_ref, g_ref, aux_ref, b_ref, c_ref, gb_ref, small_ref, grads_ref, own_ref
):
    span, features = x_ref.shape
    heads = aux_ref.shape[0] // len(AUX)
    width = features // heads
    row, column = iota((span, span), 0), iota((span, span), 1)
    dt = take(aux_ref, AUX, "dt", heads)
    gate = take(aux_ref, AUX, "gate", heads)
    cum = take(aux_ref, AUX, "cum", heads)
    rate = take(aux_ref, AUX, "rate", heads)
    doc = take(aux_ref, AUX, "doc", heads)
    upright = nt(eye(span), jnp.concatenate([dt, cum, doc], axis=0), EXACT)
    doc_s = upright[:, 2 * heads : 2 * heads + 1]
    closed = jnp.where((column >= row) & (jnp.abs(doc_s - doc[:1, :]) < 0.5), 0.0, -1e30)
    scores = nt(b_ref[...], c_ref[...])
    summed = jnp.zeros((span, span), F32)
    lane = iota((span, heads), 1)
    from_s = jnp.zeros((span, heads), F32)
    to_u = []
    for pair in range(0, heads, 2):
        outs = []
        for head in (pair, pair + 1):
            part = slice(head * width, (head + 1) * width)
            g_head, x_head = g_ref[:, part], x_ref[:, part]
            cross = nt(x_head, g_head)
            cum_s = upright[:, heads + head : heads + head + 1]
            decay = jnp.exp(cum[head : head + 1, :] - cum_s + closed)
            masked = decay * scores
            weighted = decay * cross * upright[:, head : head + 1]
            summed = summed + weighted
            product = weighted * scores
            from_s = jnp.where(lane == head, jnp.sum(product, axis=1, keepdims=True), from_s)
            to_u.append(jnp.sum(product, axis=0, keepdims=True))
            outs.append(nn(masked.astype(BF16), g_head))
        gb_ref[:, pair * width : (pair + 2) * width] = jnp.concatenate(outs, axis=1)
    onward = (row >= column).astype(F32)
    turn = eye(heads)
    change = jnp.concatenate(to_u, axis=0) - nt(turn, from_s, EXACT)
    first = nn(change, onward, EXACT)
    columns = head_columns(features, heads)
    x_wide = x_ref[...].astype(F32)
    sums = jnp.concatenate(
        [head_sum(x_wide * gb_ref[...], columns),
         head_sum(x_wide * g_ref[...].astype(F32), columns)], axis=1
    )
    sums = nt(eye(2 * heads), sums, EXACT)
    x_gb, skip = sums[:heads], sums[heads:]
    put(small_ref, LOCAL, heads, dict(first=first, x_gb=x_gb, skip=skip))
    own_ref[:heads, :] = rate * dt * first
    own_ref[heads : 2 * heads, :] = gate * (x_gb + rate * first)
    own_ref[2 * heads :, :] = skip
    grads_ref[:span, :] = nn(summed.astype(BF16), c_ref[...])
    grads_ref[span:, :] = nn(jnp.transpose(summed).astype(BF16), b_ref[...])


def neighbours(one_ref, two_ref):
    first = leads()

    def behind(part):
        return jnp.where(first, two_ref[part, :], one_ref[part, :])

    def ahead(part):
        return jnp.where(first, one_ref[part, :], two_ref[part, :])

    return behind, ahead


def wide(get, span, blocks):
    return jnp.concatenate(
        [get(slice(k * span, (k + 1) * span)).astype(BF16) for k in range(blocks)], axis=1
    )


def relay_kernel(
    got_one_ref, got_two_ref, xs_ref, gs_ref, aux_ref, b_ref, c_ref, own_ref, tot_ref,
    red_ref, far_ref, push_ref, far_push_ref, xp_ref, gn_ref, bp_ref, cn_ref,
):
    span, features = xs_ref.shape
    heads = aux_ref.shape[0] // len(AUX)
    blocks = features // LANES
    behind, ahead = neighbours(got_one_ref, got_two_ref)
    base = blocks * span
    xp, bp = wide(behind, span, blocks), behind(slice(base, base + span)).astype(BF16)
    gn, cn = wide(ahead, span, blocks), ahead(slice(base, base + span)).astype(BF16)
    base = base + span
    alpha_p = behind(slice(base, base + heads))
    beta_p = behind(slice(base + heads, base + 2 * heads))
    alpha_n = ahead(slice(base, base + heads))
    beta_n = ahead(slice(base + heads, base + 2 * heads))
    xs, gs, b, c = xs_ref[...], gs_ref[...], b_ref[...], c_ref[...]
    columns = head_columns(features, heads)
    gn_tot = (gn.astype(F32) * tot_ref[:1, :]).astype(BF16)

    pull = nn(nt(c, bp).astype(BF16), xp)
    push = nn(nt(b, cn).astype(BF16), gn)
    far_pull = nn(nt(cn, bp).astype(BF16), xp)
    far_push = nn(nt(bp, cn).astype(BF16), gn_tot)
    products = [
        gs.astype(F32) * pull,
        xs.astype(F32) * push,
        gn_tot.astype(F32) * far_pull,
        xp.astype(F32) * far_push,
    ]
    sums = jnp.concatenate([nn(item.astype(BF16), columns) for item in products], axis=1)
    sums = nt(eye(4 * heads), sums, EXACT)
    z_own, w_own, z_far, w_far = (sums[k * heads : (k + 1) * heads] for k in range(4))
    carried = jnp.sum(z_far, axis=1, keepdims=True)
    rate = take(aux_ref, AUX, "rate", heads)
    alog = (
        own_ref[:heads, :]
        + z_own * take(aux_ref, AUX, "alpha_u", heads)
        + w_own * take(aux_ref, AUX, "alpha_s", heads)
        + carried * rate * take(aux_ref, AUX, "dt", heads)
        + z_far * alpha_n
        + w_far * alpha_p
    )
    bias = (
        own_ref[heads : 2 * heads, :]
        + z_own * take(aux_ref, AUX, "beta_u", heads)
        + w_own * take(aux_ref, AUX, "beta_s", heads)
        + carried * rate * take(aux_ref, AUX, "gate", heads)
        + z_far * beta_n
        + w_far * beta_p
    )
    stack = jnp.concatenate([alog, bias, own_ref[2 * heads :, :]], axis=0)
    red_ref[:, : 3 * heads] = nt(jnp.ones((8, span), F32), stack, EXACT)
    red_ref[:, 3 * heads :] = jnp.zeros((8, red_ref.shape[1] - 3 * heads), F32)
    put(far_ref, FAR, heads, dict(
        z_own=z_own, w_own=w_own, z_far=z_far, w_far=w_far,
        carried=jnp.broadcast_to(carried, z_own.shape),
    ))
    push_ref[...] = push
    far_push_ref[...] = far_push
    xp_ref[...] = xp
    gn_ref[...] = gn
    bp_ref[...] = bp
    cn_ref[...] = cn


def grads_kernel(
    xp_ref, gn_ref, bp_ref, cn_ref, xs_ref, gs_ref, aux_ref, grads_ref, far_ref, far_push_ref,
    tot_ref, hop_one_ref, hop_two_ref, sums_ref,
):
    span, features = xs_ref.shape
    blocks = features // LANES
    heads = far_ref.shape[0] // len(FAR)
    xp, gn, bp, cn = xp_ref[...], gn_ref[...], bp_ref[...], cn_ref[...]
    gn_tot = (gn.astype(F32) * tot_ref[:1, :]).astype(BF16)
    sums_ref[:span, :] = grads_ref[:span, :] + nn(nt(xs_ref[...], gn).astype(BF16), cn)
    sums_ref[span:, :] = grads_ref[span:, :] + nn(nt(gs_ref[...], xp).astype(BF16), bp)
    grad_b_far = nn(nt(xp, gn_tot).astype(BF16), cn)
    grad_c_far = nn(nt(gn_tot, xp).astype(BF16), bp)
    half = span // 2
    base = blocks * half
    short = take(aux_ref, AUX, "short", heads)[:1, :] > 0.5

    def fill(ref, grad, name, heavy):
        if heavy:
            for block in range(blocks):
                part = slice(block * LANES, (block + 1) * LANES)
                ref[block * half : (block + 1) * half, :] = jnp.where(
                    short, far_push_ref[half:, part], gn_tot[:half, part].astype(F32)
                )
            ref[base : base + half, :] = cn[:half].astype(F32)
        else:
            ref[: base + half, :] = jnp.zeros((base + half, LANES), F32)
        rest = base + half
        ref[rest : rest + span, :] = grad
        ref[rest + span : rest + span + heads, :] = take(far_ref, FAR, name, heads)

    first = leads()

    @pl.when(first)
    def _():
        fill(hop_one_ref, grad_c_far, "z_far", False)
        fill(hop_two_ref, grad_b_far, "w_far", True)

    @pl.when(jnp.logical_not(first))
    def _():
        fill(hop_one_ref, grad_b_far, "w_far", True)
        fill(hop_two_ref, grad_c_far, "z_far", False)


def final_kernel(
    far_one_ref, far_two_ref, g_ref, b_ref, aux_ref, gain_ref, gbl_ref, push_ref, small_ref, far_ref,
    sums_ref, gx_ref, gdt_ref, half_ref,
):
    span, features = g_ref.shape
    heads = aux_ref.shape[0] // len(AUX)
    blocks = features // LANES
    half = span // 2
    behind, ahead = neighbours(far_one_ref, far_two_ref)
    base = blocks * half
    short = take(aux_ref, AUX, "short", heads)[heads // 2 : heads // 2 + 1, :] > 0.5
    cn = ahead(slice(base, base + half)).astype(BF16)
    scores = nt(b_ref[...], cn).astype(BF16)
    parts = [ahead(slice(k * half, (k + 1) * half)) for k in range(blocks)]
    other = nn(scores, jnp.concatenate(parts, axis=1).astype(BF16))
    blank = jnp.zeros((half, LANES), F32)
    push = push_ref[...] + jnp.concatenate(
        [
            jnp.where(
                short,
                jnp.concatenate([blank, part], axis=0),
                other[:, k * LANES : (k + 1) * LANES],
            )
            for k, part in enumerate(parts)
        ],
        axis=1,
    )
    rows = head_rows(heads, features)
    dt = take(aux_ref, AUX, "dt", heads)
    gate = take(aux_ref, AUX, "gate", heads)
    dout = take(aux_ref, AUX, "dout", heads)
    rate = take(aux_ref, AUX, "rate", heads)
    gx_ref[0] = (
        spread(dt, rows) * gbl_ref[...]
        + spread(dt * dout, rows) * push
        + gain_ref[:1, :] * g_ref[...].astype(F32)
    ).astype(BF16)
    inout = take(aux_ref, AUX, "masks", heads)
    inward, outward = inout[:1, :], inout[heads // 2 : heads // 2 + 1, :]
    rest = base + half
    z = take(far_ref, FAR, "z_own", heads) + behind(slice(rest + span, rest + span + heads))
    w = take(far_ref, FAR, "w_own", heads) + ahead(slice(rest + span, rest + span + heads))
    row, column = iota((span, span), 0), iota((span, span), 1)
    decay_grad = (
        take(small_ref, LOCAL, "first", heads)
        + inward * nn(z, (row >= column).astype(F32), EXACT)
        + outward * nn(w, (row < column).astype(F32), EXACT)
        + take(far_ref, FAR, "carried", heads)
    )
    x_gb = take(small_ref, LOCAL, "x_gb", heads) + w / dt
    gdt_ref[0] = (x_gb + rate * decay_grad) * gate
    half_ref[:span, :] = sums_ref[:span, :] + ahead(slice(rest, rest + span))
    half_ref[span:, :] = sums_ref[span:, :] + behind(slice(rest, rest + span))


def close_kernel(*refs):
    count = len(refs) - 5
    b_ref, c_ref, alog_ref, bias_ref, skip_ref = refs[count:]
    span = b_ref.shape[1]
    heads = alog_ref.shape[1]
    red = refs[0][:1, :] + refs[1][:1, :]
    alog_ref[...] = red[:, :heads]
    bias_ref[...] = red[:, heads : 2 * heads]
    skip_ref[...] = red[:, 2 * heads : 3 * heads]
    total = refs[2][...]
    for other in refs[3:count]:
        total = total + other[...]
    b_ref[0] = total[:span]
    c_ref[0] = total[span:]


def call(kernel, shapes, operands, raw=0, flops=0, scratch=()):
    def space(index):
        return pltpu.HBM if index < raw else pltpu.VMEM

    moved = sum(item.size * item.dtype.itemsize for item in operands) + sum(
        item.size * jnp.dtype(item.dtype).itemsize for item in shapes
    )
    return pl.pallas_call(
        kernel,
        out_shape=shapes,
        in_specs=[pl.BlockSpec(memory_space=space(index)) for index in range(len(operands))],
        out_specs=[pl.BlockSpec(memory_space=pltpu.VMEM)] * len(shapes),
        scratch_shapes=list(scratch),
        cost_estimate=pl.CostEstimate(flops=flops, bytes_accessed=moved, transcendentals=0),
        compiler_params=pltpu.CompilerParams(vmem_limit_bytes=VMEM_GRANT),
    )(
        *(
            pltpu.with_memory_space_constraint(item, pltpu.HBM) if index < raw else item
            for index, item in enumerate(operands)
        )
    )


def exchange(array, turn, senders):
    count = lax.axis_size("ctx")
    pairs = [(i, i + 1 if (i + turn) % 2 == 0 else i - 1) for i in range(count)]
    return lax.ppermute(
        array, "ctx", [(i, j) for i, j in pairs if 0 <= j < count and i in senders]
    )


def flip(array, axis, bit):
    return lax.ppermute(array, axis, [(i, i ^ bit) for i in range(lax.axis_size(axis))])


def near_local(inputs, dt_raw, dt_bias, a_log, b_in, c_in, skip_gain, grad_out, doc_lengths):
    _, span, features = inputs.shape
    heads = dt_bias.shape[0]
    state = b_in.shape[2]
    count = lax.axis_size("ctx")
    struct = jax.ShapeDtypeStruct
    bias, alog, skip = (item.reshape(1, heads) for item in (dt_bias, a_log, skip_gain))
    raw = jnp.swapaxes(dt_raw, 1, 2)
    base = features // LANES * span + span
    pay = struct((base + 2 * heads, LANES), F32)
    full, low = struct((span, features), F32), struct((span, features), BF16)
    line = struct((8, features), F32)
    square = struct((span, state), BF16)
    pair = struct((2 * span, state), F32)
    one_row = pltpu.VMEM((1, heads), F32)
    pay_one, pay_two, aux, xs, gs, x, g, b, c, tot, gain = call(
        prep_kernel,
        (pay, pay, struct((len(AUX) * heads, span), F32), low, low, low, low, square, square, line,
         line),
        (doc_lengths, raw, bias, alog, skip, inputs, grad_out, b_in, c_in),
        raw=9, flops=10**8,
        scratch=[pltpu.SMEM(doc_lengths.shape, jnp.int32), pltpu.VMEM((heads, span), F32),
                 one_row, one_row, one_row, pltpu.SemaphoreType.DMA((9,))],
    )
    got_two = exchange(pay_two, 1, range(count))
    got_one = exchange(pay_one, 0, range(count))
    gb_local, small, grads, own = call(
        local_kernel,
        (full, struct((len(LOCAL) * heads, span), F32), pair, struct((3 * heads, span), F32)),
        (x, g, aux, b, c),
        flops=10**8,
    )
    red, far, push, far_push, xp, gn, bp, cn = call(
        relay_kernel,
        (struct((8, LANES), F32), struct((len(FAR) * heads, span), F32), full, full, low, low,
         square, square),
        (got_one, got_two, xs, gs, aux, b, c, own, tot),
        flops=10**8,
    )
    steps = []
    for axis in ("ctx", "dp"):
        bit = 1
        while bit < lax.axis_size(axis):
            steps.append((axis, bit))
            bit *= 2
    hop = struct((base // 2 + span + heads, LANES), F32)
    hop_one, hop_two, sums = call(
        grads_kernel,
        (hop, hop, pair),
        (xp, gn, bp, cn, xs, gs, aux, grads, far, far_push, tot),
        flops=10**8,
    )
    relays = range(1, count - 1)
    far_two = exchange(hop_two, 1, relays)
    far_one = exchange(hop_one, 0, relays)
    for axis, bit in steps[:-1]:
        red = red + flip(red, axis, bit)
    last_red = flip(red, *steps[-1])
    grad_x, grad_dt, half = call(
        final_kernel,
        (struct((1, span, features), BF16), struct((1, heads, span), F32), pair),
        (far_one, far_two, g, b, aux, gain, gb_local, push, small, far, sums),
        flops=10**8,
    )
    sides = lax.axis_size("head")
    others = [
        lax.ppermute(half, "head", [(i, (i + step) % sides) for i in range(sides)])
        for step in range(1, sides)
    ]
    flat = struct((1, heads), F32)
    cube = struct((1, span, state), F32)
    b_total, c_total, alog_total, bias_total, skip_total = call(
        close_kernel, (cube, cube, flat, flat, flat), (red, last_red, half, *others)
    )
    return (
        grad_x, jnp.swapaxes(grad_dt, 1, 2), b_total, c_total,
        alog_total.reshape(heads), bias_total.reshape(heads), skip_total.reshape(heads),
    )


def local(inputs, dt_raw, dt_bias, a_log, b_in, c_in, skip_gain, grad_out, doc_lengths):
    args = (inputs, dt_raw, dt_bias, a_log, b_in, c_in, skip_gain, grad_out, doc_lengths)
    shards = [lax.axis_size(axis) for axis in ("dp", "ctx")]
    near = (
        inputs.shape[1] == SPAN
        and shards[1] in (2, 4)
        and shards[0] & (shards[0] - 1) == 0
        and b_in.shape[2] == LANES
        and inputs.shape[2] % LANES == 0
        and dt_bias.shape[0] * 8 == LANES
    )
    if not near:
        return general_local(*args)
    return near_local(*args)


def solution(mesh):
    placed = (
        P("dp", "ctx", "head"),
        P("dp", "ctx", "head"),
        P("head"),
        P("head"),
        P("dp", "ctx", None),
        P("dp", "ctx", None),
        P("head"),
        P("dp", "ctx", "head"),
        P("dp", None),
    )
    return jax.shard_map(
        local,
        mesh=mesh,
        in_specs=placed,
        out_specs=(
            P("dp", "ctx", "head"),
            P("dp", "ctx", "head"),
            P("dp", "ctx", None),
            P("dp", "ctx", None),
            P("head"),
            P("head"),
            P("head"),
        ),
        check_vma=False,
    )
```

```python
import functools

import jax
import jax.numpy as jnp
from jax import lax
from jax.experimental import pallas as pl
from jax.experimental.pallas import tpu as pltpu
from jax.sharding import PartitionSpec as P


SPAN = 128
LANES = 128
VMEM_GRANT = 16 << 20
F32 = jnp.float32
BF16 = jnp.bfloat16
EXACT = lax.Precision.HIGHEST


def from_behind(array, axis, by):
    count = lax.axis_size(axis)
    pairs = [(i, i + by) for i in range(count) if 0 <= i + by < count]
    return lax.ppermute(array, axis, pairs)


def reverse_cumsum(values, along_axis):
    return jnp.flip(jnp.cumsum(jnp.flip(values, along_axis), axis=along_axis), along_axis)


def doc_index(positions, starts):
    return jnp.sum((starts[None, :] <= positions[:, None]).astype(jnp.int32), axis=1)


def vector_factors(decay_block, segment_block, previous_block):
    cumulative = jnp.cumsum(decay_block, axis=0)
    last_segment = segment_block[-1]
    mask_in = (segment_block == previous_block).astype(jnp.float32)
    mask_out = (segment_block == last_segment).astype(jnp.float32)
    factor_in = mask_in[:, None] * jnp.exp(cumulative)
    factor_out = mask_out[:, None] * jnp.exp(cumulative[-1][None, :] - cumulative)
    span_total = (last_segment == previous_block).astype(jnp.float32) * jnp.exp(cumulative[-1])
    return (cumulative, mask_in, mask_out, factor_in, factor_out, span_total)


def pair_factor(cumulative, segment_block):
    local_pos = jnp.arange(segment_block.shape[0], dtype=jnp.int32)
    allowed = (local_pos[:, None] >= local_pos[None, :]) & (
        segment_block[:, None] == segment_block[None, :]
    )
    spread = cumulative.T[:, :, None] - cumulative.T[:, None, :]
    return jnp.where(allowed[None], jnp.exp(jnp.where(allowed[None], spread, 0.0)), 0.0)


def first_pass(
    inputs_block,
    grads_block,
    b_block,
    c_block,
    step_block,
    decay_block,
    segment_block,
    previous_block,
):
    _, _, _, factor_in, factor_out, span_total = vector_factors(
        decay_block, segment_block, previous_block
    )
    scaled_in = (inputs_block * (factor_out * step_block)[:, :, None]).astype(jnp.bfloat16)
    scaled_grad = (grads_block * factor_in[:, :, None]).astype(jnp.bfloat16)
    state_part = jnp.einsum("shp,sn->hpn", scaled_in, b_block, preferred_element_type=jnp.float32)
    grad_part = jnp.einsum("uhp,un->hpn", scaled_grad, c_block, preferred_element_type=jnp.float32)
    return (span_total, state_part, grad_part)


def span_grads(
    inputs_block,
    grads_block,
    b_block,
    c_block,
    step_block,
    decay_block,
    segment_block,
    previous_block,
    preact_block,
    state_in,
    state_grad,
    decay_rate,
    skip_gain,
):
    cumulative, mask_in, mask_out, factor_in, factor_out, _ = vector_factors(
        decay_block, segment_block, previous_block
    )
    pair_decay = pair_factor(cumulative, segment_block)
    scores = jnp.einsum("un,sn->us", c_block, b_block, preferred_element_type=jnp.float32)
    cross_term = jnp.einsum(
        "uhp,shp->hus", grads_block, inputs_block, preferred_element_type=jnp.float32
    )
    masked = (pair_decay * scores[None]).astype(jnp.bfloat16)
    weighted = pair_decay * cross_term * step_block.T[:, None, :]
    summed = jnp.sum(weighted, axis=0).astype(jnp.bfloat16)
    products = weighted * scores[None]
    change = jnp.sum(products, axis=2) - jnp.sum(products, axis=1)
    first_term = reverse_cumsum(change, 1).T
    h_low = state_in.astype(jnp.bfloat16)
    e_low = state_grad.astype(jnp.bfloat16)
    along_b = jnp.einsum("tn,hpn->thp", b_block, e_low, preferred_element_type=jnp.float32)
    grad_b_prod = (
        jnp.einsum("hut,uhp->thp", masked, grads_block, preferred_element_type=jnp.float32)
        + factor_out[:, :, None] * along_b
    )
    grad_x = (step_block[:, :, None] * grad_b_prod + skip_gain[None, :, None] * grads_block).astype(
        jnp.bfloat16
    )
    x_state = jnp.einsum("thp,hpn->thn", inputs_block, e_low, preferred_element_type=jnp.float32)
    y_state = jnp.einsum("uhp,hpn->uhn", grads_block, h_low, preferred_element_type=jnp.float32)
    grad_b = jnp.einsum("us,un->sn", summed, c_block, preferred_element_type=jnp.float32) + jnp.sum(
        (step_block * factor_out)[:, :, None] * x_state, axis=1
    )
    grad_c = jnp.einsum("us,sn->un", summed, b_block, preferred_element_type=jnp.float32) + jnp.sum(
        factor_in[:, :, None] * y_state, axis=1
    )
    z_term = jnp.sum(y_state * c_block[:, None, :], axis=2)
    w_term = step_block * jnp.sum(x_state * b_block[:, None, :], axis=2)
    second_term = mask_in[:, None] * reverse_cumsum(factor_in * z_term, 0)
    carried = factor_out * w_term
    third_term = mask_out[:, None] * (jnp.cumsum(carried, axis=0) - carried)
    fourth_term = factor_out * factor_in * jnp.sum(state_grad * state_in, axis=(1, 2))[None, :]
    decay_grad = first_term + second_term + third_term + fourth_term
    x_dot_g = jnp.sum(inputs_block * grad_b_prod, axis=2)
    grad_dt = (x_dot_g + decay_rate[None, :] * decay_grad) * jax.nn.sigmoid(preact_block)
    grad_alog = jnp.sum(decay_grad * step_block, axis=0) * decay_rate
    grad_bias = jnp.sum(grad_dt, axis=0)
    grad_skip = jnp.einsum(
        "thp,thp->h", grads_block, inputs_block, preferred_element_type=jnp.float32
    )
    return (grad_x, grad_dt, grad_b, grad_c, grad_alog, grad_bias, grad_skip)


def local_link(running, pieces):
    decay_gain, held_state = running
    span_total, span_part = pieces
    return ((decay_gain * span_total, span_total[:, None, None] * held_state + span_part), running)


def link_maps(earlier, later):
    return (earlier[0] * later[0], later[0][:, None, None] * earlier[1] + later[1])


def doubling(element, reverse):
    axis_count = lax.axis_size("ctx")
    own_index = lax.axis_index("ctx")
    distances = [1] + [2**power for power in range((axis_count - 1).bit_length())]
    running = element
    for section_num, distance in enumerate(distances):
        shift_by = -distance if reverse else distance
        received = from_behind((running[0], running[1]), "ctx", shift_by)
        source = own_index - shift_by
        present = (source >= 0) & (source < axis_count)
        fixed = (jnp.where(present, received[0], 1.0), received[1])
        if section_num == 0:
            running = fixed
        else:
            running = link_maps(fixed, running)
    return running


def general_local(inputs, dt_raw, dt_bias, a_log, b_in, c_in, skip_gain, grad_out, doc_lengths):
    token_count = inputs.shape[1]
    head_count = dt_bias.shape[0]
    head_width = inputs.shape[2] // head_count
    state_size = b_in.shape[2]
    span_count = token_count // SPAN
    preact = dt_raw[0] + dt_bias[None, :]
    step_size = jax.nn.softplus(preact)
    decay_rate = -jnp.exp(a_log)
    log_decay = step_size * decay_rate[None, :]
    lengths = doc_lengths[0]
    starts = jnp.cumsum(lengths) - lengths
    positions = lax.axis_index("ctx") * token_count + jnp.arange(token_count, dtype=jnp.int32)
    segment = doc_index(positions, starts)
    previous = doc_index(positions[::SPAN] - 1, starts)
    shaped = (
        inputs[0].reshape(span_count, SPAN, head_count, head_width),
        grad_out[0].reshape(span_count, SPAN, head_count, head_width),
        b_in[0].reshape(span_count, SPAN, state_size),
        c_in[0].reshape(span_count, SPAN, state_size),
        step_size.reshape(span_count, SPAN, head_count),
        log_decay.reshape(span_count, SPAN, head_count),
        segment.reshape(span_count, SPAN),
        previous,
    )
    totals, state_parts, grad_parts = jax.vmap(first_pass)(*shaped)
    start_maps = (
        jnp.ones((head_count,), jnp.float32),
        jnp.zeros((head_count, head_width, state_size), jnp.float32),
    )
    forward_map, (gain_before, local_entry) = lax.scan(
        local_link, start_maps, (totals, state_parts)
    )
    backward_map, (gain_after, local_leave) = lax.scan(
        local_link, start_maps, (totals, grad_parts), reverse=True
    )
    entry_state = doubling(forward_map, False)[1]
    leave_state = doubling(backward_map, True)[1]
    entering = gain_before[:, :, None, None] * entry_state[None] + local_entry
    leaving = gain_after[:, :, None, None] * leave_state[None] + local_leave
    mapped = jax.vmap(span_grads, in_axes=(0, 0, 0, 0, 0, 0, 0, 0, 0, 0, 0, None, None))
    grad_x, grad_dt, grad_b, grad_c, grad_alog, grad_bias, grad_skip = mapped(
        *shaped,
        preact.reshape(span_count, SPAN, head_count),
        entering,
        leaving,
        decay_rate,
        skip_gain
    )
    b_total, c_total = lax.psum(
        (grad_b.reshape(token_count, state_size), grad_c.reshape(token_count, state_size)), "head"
    )
    alog_total, bias_total, skip_total = lax.psum(
        (jnp.sum(grad_alog, axis=0), jnp.sum(grad_bias, axis=0), jnp.sum(grad_skip, axis=0)),
        ("dp", "ctx"),
    )
    return (
        grad_x.reshape(1, token_count, head_count * head_width),
        grad_dt,
        b_total[None],
        c_total[None],
        alog_total,
        bias_total,
        skip_total,
    )


def dot(left, right, dims, precision=None):
    return lax.dot_general(
        left, right, (dims, ((), ())), precision=precision, preferred_element_type=F32
    )


def nn(left, right, precision=None):
    return dot(left, right, ((1,), (0,)), precision)


def nt(left, right, precision=None):
    return dot(left, right, ((1,), (1,)), precision)


def tn(left, right, precision=None):
    return dot(left, right, ((0,), (0,)), precision)


def iota(shape, axis):
    return lax.broadcasted_iota(jnp.int32, shape, axis)


def eye(size):
    return (iota((size, size), 0) == iota((size, size), 1)).astype(F32)


def head_rows(heads, features):
    width = features // heads
    start = iota((heads, features), 0) * width
    feature = iota((heads, features), 1)
    return ((feature >= start) & (feature < start + width)).astype(BF16)


def head_columns(features, heads):
    width = features // heads
    start = iota((features, heads), 1) * width
    feature = iota((features, heads), 0)
    return ((feature >= start) & (feature < start + width)).astype(BF16)


def thirds(value):
    high = value.astype(BF16)
    rest = value - high.astype(F32)
    middle = rest.astype(BF16)
    low = (rest - middle.astype(F32)).astype(BF16)
    return jnp.concatenate([high, middle, low], axis=0)


def spread(factor, rows):
    return tn(thirds(factor), jnp.concatenate([rows] * 3, axis=0))


def spread_row(factor, features):
    heads = factor.shape[1]
    wide = jnp.broadcast_to(factor, (8, heads))
    high = wide.astype(BF16)
    rest = wide - high.astype(F32)
    middle = rest.astype(BF16)
    low = (rest - middle.astype(F32)).astype(BF16)
    rows = head_rows(heads, features)
    return (nn(high, rows) + nn(middle, rows) + nn(low, rows))[:1]


def head_sum(values, columns):
    high = values.astype(BF16)
    low = (values - high.astype(F32)).astype(BF16)
    return nn(high, columns) + nn(low, columns)


def as_column(row):
    size = row.shape[1]
    return jnp.sum(jnp.where(eye(size) > 0, row, 0.0), axis=1, keepdims=True)


def as_row(column):
    size = column.shape[0]
    return jnp.sum(jnp.where(eye(size) > 0, column, 0.0), axis=0, keepdims=True)


def doc_of(lens_ref, positions):
    count = jnp.zeros(positions.shape, jnp.int32)
    start = jnp.int32(0)
    for index in range(lens_ref.shape[1]):
        count = count + (start <= positions).astype(jnp.int32)
        start = start + lens_ref[0, index]
    return count


def doc_scalar(lens_ref, position):
    count = jnp.int32(0)
    start = jnp.int32(0)
    for index in range(lens_ref.shape[1]):
        count = count + jnp.where(start <= position, 1, 0)
        start = start + lens_ref[0, index]
    return count


def doc_start(lens_ref, position):
    found = jnp.int32(0)
    start = jnp.int32(0)
    for index in range(lens_ref.shape[1]):
        found = jnp.where(start <= position, start, found)
        start = start + lens_ref[0, index]
    return found


def leads():
    return lax.rem(lax.axis_index("ctx"), 2) == 0


AUX = (
    "dt", "gate", "cum", "dout", "alpha_s", "beta_s", "alpha_u", "beta_u", "rate", "doc", "masks",
    "short",
)
LOCAL = ("first", "x_gb", "skip")
FAR = ("z_own", "w_own", "z_far", "w_far", "carried")


def take(ref, names, name, heads):
    slot = names.index(name) * heads
    return ref[slot : slot + heads, :]


def put(ref, names, heads, values):
    for name, value in values.items():
        slot = names.index(name) * heads
        ref[slot : slot + heads, :] = value


def halves(upper, lower, rows):
    width = upper.shape[1]
    return jnp.concatenate(
        [jnp.broadcast_to(item, (rows // 2, width)) for item in (upper, lower)], axis=0
    )


def prep_kernel(
    lens_hbm, raw_hbm, bias_hbm, alog_hbm, skip_hbm, x_hbm, g_hbm, b_hbm, c_hbm,
    pay_one_ref, pay_two_ref, aux_ref, xs_ref, gs_ref, x_ref, g_ref, b_ref, c_ref, tot_ref,
    gain_ref, lens_ref, raw_ref, bias_ref, alog_ref, skip_ref, sems,
):
    moves = (
        (lens_hbm, lens_ref), (raw_hbm.at[0], raw_ref), (bias_hbm, bias_ref),
        (alog_hbm, alog_ref), (skip_hbm, skip_ref), (x_hbm.at[0], x_ref), (g_hbm.at[0], g_ref),
        (b_hbm.at[0], b_ref), (c_hbm.at[0], c_ref),
    )
    copies = [
        pltpu.make_async_copy(source, target, sems.at[index])
        for index, (source, target) in enumerate(moves)
    ]
    for copy in copies:
        copy.start()
    small, large = copies[:5], copies[5:]
    span, features = x_ref.shape
    heads = raw_ref.shape[0]
    row, column = iota((span, span), 0), iota((span, span), 1)
    upto = (row <= column).astype(F32)
    beyond = (row > column).astype(F32)
    rows = head_rows(heads, features)
    for copy in small:
        copy.wait()
    base = lax.axis_index("ctx") * span
    doc = doc_of(lens_ref, base + iota((1, span), 1))
    before = doc_scalar(lens_ref, base - 1)
    last = doc_scalar(lens_ref, base + span - 1)
    inward = (doc == before).astype(F32)
    outward = (doc == last).astype(F32)
    whole = jnp.where(last == before, 1.0, 0.0)
    short_before = jnp.where(base - doc_start(lens_ref, base - 1) <= span // 2, 1.0, 0.0)
    short_last = jnp.where(
        base + span - doc_start(lens_ref, base + span - 1) <= span // 2, 1.0, 0.0
    )
    preact = raw_ref[...] + as_column(bias_ref[...])
    dt = jnp.maximum(preact, 0.0) + jnp.log1p(jnp.exp(-jnp.abs(preact)))
    gate = 1.0 / (1.0 + jnp.exp(-preact))
    rate = -jnp.exp(as_column(alog_ref[...]))
    cum = nn(dt * rate, upto, EXACT)
    cum_last = cum[:, span - 1 : span]
    din = inward * jnp.exp(cum)
    dout = outward * jnp.exp(cum_last - cum)
    tot_ref[...] = jnp.broadcast_to(
        spread_row(as_row(whole * jnp.exp(cum_last)), features), tot_ref.shape
    )
    pair = jnp.concatenate([dt, gate], axis=0)
    seen = nn(pair * inward, upto, EXACT)
    left = nn(pair * outward, beyond, EXACT)
    alpha_s = rate * left[:heads]
    beta_s = rate * left[heads:] + gate / dt
    alpha_u = rate * seen[:heads]
    beta_u = rate * seen[heads:]
    put(aux_ref, AUX, heads, dict(
        dt=dt, gate=gate, cum=cum, dout=dout,
        alpha_s=alpha_s, beta_s=beta_s, alpha_u=alpha_u, beta_u=beta_u,
        rate=jnp.broadcast_to(rate, dt.shape), doc=jnp.broadcast_to(doc.astype(F32), dt.shape),
        masks=halves(inward, outward, heads),
        short=halves(jnp.full((1, span), short_before), jnp.full((1, span), short_last), heads),
    ))
    gain_ref[...] = jnp.broadcast_to(spread_row(skip_ref[...], features), gain_ref.shape)
    x_factor, g_factor = spread(dout * dt, rows), spread(din, rows)
    for copy in large:
        copy.wait()
    xs = (x_ref[...].astype(F32) * x_factor).astype(BF16)
    gs = (g_ref[...].astype(F32) * g_factor).astype(BF16)
    xs_ref[...] = xs
    gs_ref[...] = gs

    def fill(ref, scaled, wide, small):
        blocks = features // LANES
        for block in range(blocks):
            ref[block * span : (block + 1) * span, :] = scaled[
                :, block * LANES : (block + 1) * LANES
            ].astype(F32)
        base = blocks * span
        ref[base : base + span, :] = wide.astype(F32)
        base = base + span
        for part in small:
            ref[base : base + heads, :] = part
            base = base + heads

    first = leads()

    @pl.when(first)
    def _():
        fill(pay_one_ref, xs, b_ref[...], (alpha_s, beta_s))
        fill(pay_two_ref, gs, c_ref[...], (alpha_u, beta_u))

    @pl.when(jnp.logical_not(first))
    def _():
        fill(pay_one_ref, gs, c_ref[...], (alpha_u, beta_u))
        fill(pay_two_ref, xs, b_ref[...], (alpha_s, beta_s))


def local_kernel(
    x_ref, g_ref, aux_ref, b_ref, c_ref, gb_ref, small_ref, grads_ref, own_ref
):
    span, features = x_ref.shape
    heads = aux_ref.shape[0] // len(AUX)
    width = features // heads
    row, column = iota((span, span), 0), iota((span, span), 1)
    dt = take(aux_ref, AUX, "dt", heads)
    gate = take(aux_ref, AUX, "gate", heads)
    cum = take(aux_ref, AUX, "cum", heads)
    rate = take(aux_ref, AUX, "rate", heads)
    doc = take(aux_ref, AUX, "doc", heads)
    upright = nt(eye(span), jnp.concatenate([dt, cum, doc], axis=0), EXACT)
    doc_s = upright[:, 2 * heads : 2 * heads + 1]
    closed = jnp.where((column >= row) & (jnp.abs(doc_s - doc[:1, :]) < 0.5), 0.0, -1e30)
    scores = nt(b_ref[...], c_ref[...])
    summed = jnp.zeros((span, span), F32)
    lane = iota((span, heads), 1)
    from_s = jnp.zeros((span, heads), F32)
    to_u = []
    for pair in range(0, heads, 2):
        outs = []
        for head in (pair, pair + 1):
            part = slice(head * width, (head + 1) * width)
            g_head, x_head = g_ref[:, part], x_ref[:, part]
            cross = nt(x_head, g_head)
            cum_s = upright[:, heads + head : heads + head + 1]
            decay = jnp.exp(cum[head : head + 1, :] - cum_s + closed)
            masked = decay * scores
            weighted = decay * cross * upright[:, head : head + 1]
            summed = summed + weighted
            product = weighted * scores
            from_s = jnp.where(lane == head, jnp.sum(product, axis=1, keepdims=True), from_s)
            to_u.append(jnp.sum(product, axis=0, keepdims=True))
            outs.append(nn(masked.astype(BF16), g_head))
        gb_ref[:, pair * width : (pair + 2) * width] = jnp.concatenate(outs, axis=1)
    onward = (row >= column).astype(F32)
    turn = eye(heads)
    change = jnp.concatenate(to_u, axis=0) - nt(turn, from_s, EXACT)
    first = nn(change, onward, EXACT)
    columns = head_columns(features, heads)
    x_wide = x_ref[...].astype(F32)
    sums = jnp.concatenate(
        [head_sum(x_wide * gb_ref[...], columns),
         head_sum(x_wide * g_ref[...].astype(F32), columns)], axis=1
    )
    sums = nt(eye(2 * heads), sums, EXACT)
    x_gb, skip = sums[:heads], sums[heads:]
    put(small_ref, LOCAL, heads, dict(first=first, x_gb=x_gb, skip=skip))
    own_ref[:heads, :] = rate * dt * first
    own_ref[heads : 2 * heads, :] = gate * (x_gb + rate * first)
    own_ref[2 * heads :, :] = skip
    grads_ref[:span, :] = nn(summed.astype(BF16), c_ref[...])
    grads_ref[span:, :] = nn(jnp.transpose(summed).astype(BF16), b_ref[...])


def neighbours(one_ref, two_ref):
    first = leads()

    def behind(part):
        return jnp.where(first, two_ref[part, :], one_ref[part, :])

    def ahead(part):
        return jnp.where(first, one_ref[part, :], two_ref[part, :])

    return behind, ahead


def wide(get, span, blocks):
    return jnp.concatenate(
        [get(slice(k * span, (k + 1) * span)).astype(BF16) for k in range(blocks)], axis=1
    )


def relay_kernel(
    got_one_ref, got_two_ref, xs_ref, gs_ref, aux_ref, b_ref, c_ref, own_ref, tot_ref,
    red_ref, far_ref, push_ref, far_push_ref, xp_ref, gn_ref, bp_ref, cn_ref,
):
    span, features = xs_ref.shape
    heads = aux_ref.shape[0] // len(AUX)
    blocks = features // LANES
    behind, ahead = neighbours(got_one_ref, got_two_ref)
    base = blocks * span
    xp, bp = wide(behind, span, blocks), behind(slice(base, base + span)).astype(BF16)
    gn, cn = wide(ahead, span, blocks), ahead(slice(base, base + span)).astype(BF16)
    base = base + span
    alpha_p = behind(slice(base, base + heads))
    beta_p = behind(slice(base + heads, base + 2 * heads))
    alpha_n = ahead(slice(base, base + heads))
    beta_n = ahead(slice(base + heads, base + 2 * heads))
    xs, gs, b, c = xs_ref[...], gs_ref[...], b_ref[...], c_ref[...]
    columns = head_columns(features, heads)
    gn_tot = (gn.astype(F32) * tot_ref[:1, :]).astype(BF16)

    pull = nn(nt(c, bp).astype(BF16), xp)
    push = nn(nt(b, cn).astype(BF16), gn)
    far_pull = nn(nt(cn, bp).astype(BF16), xp)
    far_push = nn(nt(bp, cn).astype(BF16), gn_tot)
    products = [
        gs.astype(F32) * pull,
        xs.astype(F32) * push,
        gn_tot.astype(F32) * far_pull,
        xp.astype(F32) * far_push,
    ]
    sums = jnp.concatenate([nn(item.astype(BF16), columns) for item in products], axis=1)
    sums = nt(eye(4 * heads), sums, EXACT)
    z_own, w_own, z_far, w_far = (sums[k * heads : (k + 1) * heads] for k in range(4))
    carried = jnp.sum(z_far, axis=1, keepdims=True)
    rate = take(aux_ref, AUX, "rate", heads)
    alog = (
        own_ref[:heads, :]
        + z_own * take(aux_ref, AUX, "alpha_u", heads)
        + w_own * take(aux_ref, AUX, "alpha_s", heads)
        + carried * rate * take(aux_ref, AUX, "dt", heads)
        + z_far * alpha_n
        + w_far * alpha_p
    )
    bias = (
        own_ref[heads : 2 * heads, :]
        + z_own * take(aux_ref, AUX, "beta_u", heads)
        + w_own * take(aux_ref, AUX, "beta_s", heads)
        + carried * rate * take(aux_ref, AUX, "gate", heads)
        + z_far * beta_n
        + w_far * beta_p
    )
    stack = jnp.concatenate([alog, bias, own_ref[2 * heads :, :]], axis=0)
    red_ref[:, : 3 * heads] = nt(jnp.ones((8, span), F32), stack, EXACT)
    red_ref[:, 3 * heads :] = jnp.zeros((8, red_ref.shape[1] - 3 * heads), F32)
    put(far_ref, FAR, heads, dict(
        z_own=z_own, w_own=w_own, z_far=z_far, w_far=w_far,
        carried=jnp.broadcast_to(carried, z_own.shape),
    ))
    push_ref[...] = push
    far_push_ref[...] = far_push
    xp_ref[...] = xp
    gn_ref[...] = gn
    bp_ref[...] = bp
    cn_ref[...] = cn


def grads_kernel(
    xp_ref, gn_ref, bp_ref, cn_ref, xs_ref, gs_ref, aux_ref, grads_ref, far_ref, far_push_ref,
    tot_ref, hop_one_ref, hop_two_ref, sums_ref,
):
    span, features = xs_ref.shape
    blocks = features // LANES
    heads = far_ref.shape[0] // len(FAR)
    xp, gn, bp, cn = xp_ref[...], gn_ref[...], bp_ref[...], cn_ref[...]
    gn_tot = (gn.astype(F32) * tot_ref[:1, :]).astype(BF16)
    sums_ref[:span, :] = grads_ref[:span, :] + nn(nt(xs_ref[...], gn).astype(BF16), cn)
    sums_ref[span:, :] = grads_ref[span:, :] + nn(nt(gs_ref[...], xp).astype(BF16), bp)
    grad_b_far = nn(nt(xp, gn_tot).astype(BF16), cn)
    grad_c_far = nn(nt(gn_tot, xp).astype(BF16), bp)
    half = span // 2
    base = blocks * half
    short = take(aux_ref, AUX, "short", heads)[:1, :] > 0.5

    def fill(ref, grad, name, heavy):
        if heavy:
            for block in range(blocks):
                part = slice(block * LANES, (block + 1) * LANES)
                ref[block * half : (block + 1) * half, :] = jnp.where(
                    short, far_push_ref[half:, part], gn_tot[:half, part].astype(F32)
                )
            ref[base : base + half, :] = cn[:half].astype(F32)
        else:
            ref[: base + half, :] = jnp.zeros((base + half, LANES), F32)
        rest = base + half
        ref[rest : rest + span, :] = grad
        ref[rest + span : rest + span + heads, :] = take(far_ref, FAR, name, heads)

    first = leads()

    @pl.when(first)
    def _():
        fill(hop_one_ref, grad_c_far, "z_far", False)
        fill(hop_two_ref, grad_b_far, "w_far", True)

    @pl.when(jnp.logical_not(first))
    def _():
        fill(hop_one_ref, grad_b_far, "w_far", True)
        fill(hop_two_ref, grad_c_far, "z_far", False)


def ready_kernel(g_ref, aux_ref, gain_ref, gbl_ref, push_ref, near_ref, weight_ref):
    features = g_ref.shape[1]
    heads = aux_ref.shape[0] // len(AUX)
    rows = head_rows(heads, features)
    dt = take(aux_ref, AUX, "dt", heads)
    weight = spread(dt * take(aux_ref, AUX, "dout", heads), rows)
    weight_ref[...] = weight
    near_ref[...] = (
        spread(dt, rows) * gbl_ref[...]
        + weight * push_ref[...]
        + gain_ref[:1, :] * g_ref[...].astype(F32)
    )


def final_kernel(
    far_one_ref, far_two_ref, b_ref, aux_ref, near_ref, weight_ref, small_ref, far_ref,
    gx_ref, gdt_ref,
):
    span, features = near_ref.shape
    heads = aux_ref.shape[0] // len(AUX)
    blocks = features // LANES
    half = span // 2
    behind, ahead = neighbours(far_one_ref, far_two_ref)
    base = blocks * half
    short = take(aux_ref, AUX, "short", heads)[heads // 2 : heads // 2 + 1, :] > 0.5
    cn = ahead(slice(base, base + half)).astype(BF16)
    scores = nt(b_ref[...], cn).astype(BF16)
    parts = [ahead(slice(k * half, (k + 1) * half)) for k in range(blocks)]
    other = nn(scores, jnp.concatenate(parts, axis=1).astype(BF16))
    blank = jnp.zeros((half, LANES), F32)
    push = jnp.concatenate(
        [
            jnp.where(
                short,
                jnp.concatenate([blank, part], axis=0),
                other[:, k * LANES : (k + 1) * LANES],
            )
            for k, part in enumerate(parts)
        ],
        axis=1,
    )
    gx_ref[0] = (near_ref[...] + weight_ref[...] * push).astype(BF16)
    dt = take(aux_ref, AUX, "dt", heads)
    gate = take(aux_ref, AUX, "gate", heads)
    rate = take(aux_ref, AUX, "rate", heads)
    inout = take(aux_ref, AUX, "masks", heads)
    inward, outward = inout[:1, :], inout[heads // 2 : heads // 2 + 1, :]
    rest = base + half
    z = take(far_ref, FAR, "z_own", heads) + behind(slice(rest + span, rest + span + heads))
    w = take(far_ref, FAR, "w_own", heads) + ahead(slice(rest + span, rest + span + heads))
    row, column = iota((span, span), 0), iota((span, span), 1)
    decay_grad = (
        take(small_ref, LOCAL, "first", heads)
        + inward * nn(z, (row >= column).astype(F32), EXACT)
        + outward * nn(w, (row < column).astype(F32), EXACT)
        + take(far_ref, FAR, "carried", heads)
    )
    x_gb = take(small_ref, LOCAL, "x_gb", heads) + w / dt
    gdt_ref[0] = (x_gb + rate * decay_grad) * gate


def half_kernel(rest, far_one_ref, far_two_ref, sums_ref, half_ref):
    span = sums_ref.shape[0] // 2
    behind, ahead = neighbours(far_one_ref, far_two_ref)
    half_ref[:span, :] = sums_ref[:span, :] + ahead(slice(rest, rest + span))
    half_ref[span:, :] = sums_ref[span:, :] + behind(slice(rest, rest + span))


def close_kernel(*refs):
    count = len(refs) - 5
    b_ref, c_ref, alog_ref, bias_ref, skip_ref = refs[count:]
    span = b_ref.shape[1]
    heads = alog_ref.shape[1]
    red = refs[0][:1, :] + refs[1][:1, :]
    alog_ref[...] = red[:, :heads]
    bias_ref[...] = red[:, heads : 2 * heads]
    skip_ref[...] = red[:, 2 * heads : 3 * heads]
    total = refs[2][...]
    for other in refs[3:count]:
        total = total + other[...]
    b_ref[0] = total[:span]
    c_ref[0] = total[span:]


def call(kernel, shapes, operands, raw=0, flops=0, scratch=()):
    def space(index):
        return pltpu.HBM if index < raw else pltpu.VMEM

    moved = sum(item.size * item.dtype.itemsize for item in operands) + sum(
        item.size * jnp.dtype(item.dtype).itemsize for item in shapes
    )
    return pl.pallas_call(
        kernel,
        out_shape=shapes,
        in_specs=[pl.BlockSpec(memory_space=space(index)) for index in range(len(operands))],
        out_specs=[pl.BlockSpec(memory_space=pltpu.VMEM)] * len(shapes),
        scratch_shapes=list(scratch),
        cost_estimate=pl.CostEstimate(flops=flops, bytes_accessed=moved, transcendentals=0),
        compiler_params=pltpu.CompilerParams(vmem_limit_bytes=VMEM_GRANT),
    )(
        *(
            pltpu.with_memory_space_constraint(item, pltpu.HBM) if index < raw else item
            for index, item in enumerate(operands)
        )
    )


def exchange(array, turn, senders):
    count = lax.axis_size("ctx")
    pairs = [(i, i + 1 if (i + turn) % 2 == 0 else i - 1) for i in range(count)]
    return lax.ppermute(
        array, "ctx", [(i, j) for i, j in pairs if 0 <= j < count and i in senders]
    )


def flip(array, axis, bit):
    return lax.ppermute(array, axis, [(i, i ^ bit) for i in range(lax.axis_size(axis))])


def near_local(inputs, dt_raw, dt_bias, a_log, b_in, c_in, skip_gain, grad_out, doc_lengths):
    _, span, features = inputs.shape
    heads = dt_bias.shape[0]
    state = b_in.shape[2]
    count = lax.axis_size("ctx")
    struct = jax.ShapeDtypeStruct
    bias, alog, skip = (item.reshape(1, heads) for item in (dt_bias, a_log, skip_gain))
    raw = jnp.swapaxes(dt_raw, 1, 2)
    base = features // LANES * span + span
    pay = struct((base + 2 * heads, LANES), F32)
    full, low = struct((span, features), F32), struct((span, features), BF16)
    line = struct((8, features), F32)
    square = struct((span, state), BF16)
    pair = struct((2 * span, state), F32)
    one_row = pltpu.VMEM((1, heads), F32)
    pay_one, pay_two, aux, xs, gs, x, g, b, c, tot, gain = call(
        prep_kernel,
        (pay, pay, struct((len(AUX) * heads, span), F32), low, low, low, low, square, square, line,
         line),
        (doc_lengths, raw, bias, alog, skip, inputs, grad_out, b_in, c_in),
        raw=9, flops=10**8,
        scratch=[pltpu.SMEM(doc_lengths.shape, jnp.int32), pltpu.VMEM((heads, span), F32),
                 one_row, one_row, one_row, pltpu.SemaphoreType.DMA((9,))],
    )
    got_two = exchange(pay_two, 1, range(count))
    got_one = exchange(pay_one, 0, range(count))
    gb_local, small, grads, own = call(
        local_kernel,
        (full, struct((len(LOCAL) * heads, span), F32), pair, struct((3 * heads, span), F32)),
        (x, g, aux, b, c),
        flops=10**8,
    )
    red, far, push, far_push, xp, gn, bp, cn = call(
        relay_kernel,
        (struct((8, LANES), F32), struct((len(FAR) * heads, span), F32), full, full, low, low,
         square, square),
        (got_one, got_two, xs, gs, aux, b, c, own, tot),
        flops=10**8,
    )
    steps = []
    for axis in ("ctx", "dp"):
        bit = 1
        while bit < lax.axis_size(axis):
            steps.append((axis, bit))
            bit *= 2
    hop = struct((base // 2 + span + heads, LANES), F32)
    hop_one, hop_two, sums = call(
        grads_kernel,
        (hop, hop, pair),
        (xp, gn, bp, cn, xs, gs, aux, grads, far, far_push, tot),
        flops=10**8,
    )
    relays = range(1, count - 1)
    far_two = exchange(hop_two, 1, relays)
    far_one = exchange(hop_one, 0, relays)
    for axis, bit in steps[:-1]:
        red = red + flip(red, axis, bit)
    last_red = flip(red, *steps[-1])
    near, weight = call(ready_kernel, (full, full), (g, aux, gain, gb_local, push), flops=10**8)
    half = call(
        functools.partial(half_kernel, base // 2), (pair,), (far_one, far_two, sums),
        flops=10**5,
    )[0]
    grad_x, grad_dt = call(
        final_kernel,
        (struct((1, span, features), BF16), struct((1, heads, span), F32)),
        (far_one, far_two, b, aux, near, weight, small, far),
        flops=10**8,
    )
    sides = lax.axis_size("head")
    others = [
        lax.ppermute(half, "head", [(i, (i + step) % sides) for i in range(sides)])
        for step in range(1, sides)
    ]
    flat = struct((1, heads), F32)
    cube = struct((1, span, state), F32)
    b_total, c_total, alog_total, bias_total, skip_total = call(
        close_kernel, (cube, cube, flat, flat, flat), (red, last_red, half, *others)
    )
    return (
        grad_x, jnp.swapaxes(grad_dt, 1, 2), b_total, c_total,
        alog_total.reshape(heads), bias_total.reshape(heads), skip_total.reshape(heads),
    )


def local(inputs, dt_raw, dt_bias, a_log, b_in, c_in, skip_gain, grad_out, doc_lengths):
    args = (inputs, dt_raw, dt_bias, a_log, b_in, c_in, skip_gain, grad_out, doc_lengths)
    shards = [lax.axis_size(axis) for axis in ("dp", "ctx")]
    near = (
        inputs.shape[1] == SPAN
        and shards[1] in (2, 4)
        and shards[0] & (shards[0] - 1) == 0
        and b_in.shape[2] == LANES
        and inputs.shape[2] % LANES == 0
        and dt_bias.shape[0] * 8 == LANES
    )
    if not near:
        return general_local(*args)
    return near_local(*args)


def solution(mesh):
    placed = (
        P("dp", "ctx", "head"),
        P("dp", "ctx", "head"),
        P("head"),
        P("head"),
        P("dp", "ctx", None),
        P("dp", "ctx", None),
        P("head"),
        P("dp", "ctx", "head"),
        P("dp", None),
    )
    return jax.shard_map(
        local,
        mesh=mesh,
        in_specs=placed,
        out_specs=(
            P("dp", "ctx", "head"),
            P("dp", "ctx", "head"),
            P("dp", "ctx", None),
            P("dp", "ctx", None),
            P("head"),
            P("head"),
            P("head"),
        ),
        check_vma=False,
    )
```

```python
import functools

import jax
import jax.numpy as jnp
from jax import lax
from jax.experimental import pallas as pl
from jax.experimental.pallas import tpu as pltpu
from jax.sharding import PartitionSpec as P


SPAN = 128
LANES = 128
VMEM_GRANT = 16 << 20
F32 = jnp.float32
BF16 = jnp.bfloat16
EXACT = lax.Precision.HIGHEST


def from_behind(array, axis, by):
    count = lax.axis_size(axis)
    pairs = [(i, i + by) for i in range(count) if 0 <= i + by < count]
    return lax.ppermute(array, axis, pairs)


def reverse_cumsum(values, along_axis):
    return jnp.flip(jnp.cumsum(jnp.flip(values, along_axis), axis=along_axis), along_axis)


def doc_index(positions, starts):
    return jnp.sum((starts[None, :] <= positions[:, None]).astype(jnp.int32), axis=1)


def vector_factors(decay_block, segment_block, previous_block):
    cumulative = jnp.cumsum(decay_block, axis=0)
    last_segment = segment_block[-1]
    mask_in = (segment_block == previous_block).astype(jnp.float32)
    mask_out = (segment_block == last_segment).astype(jnp.float32)
    factor_in = mask_in[:, None] * jnp.exp(cumulative)
    factor_out = mask_out[:, None] * jnp.exp(cumulative[-1][None, :] - cumulative)
    span_total = (last_segment == previous_block).astype(jnp.float32) * jnp.exp(cumulative[-1])
    return (cumulative, mask_in, mask_out, factor_in, factor_out, span_total)


def pair_factor(cumulative, segment_block):
    local_pos = jnp.arange(segment_block.shape[0], dtype=jnp.int32)
    allowed = (local_pos[:, None] >= local_pos[None, :]) & (
        segment_block[:, None] == segment_block[None, :]
    )
    spread = cumulative.T[:, :, None] - cumulative.T[:, None, :]
    return jnp.where(allowed[None], jnp.exp(jnp.where(allowed[None], spread, 0.0)), 0.0)


def first_pass(
    inputs_block,
    grads_block,
    b_block,
    c_block,
    step_block,
    decay_block,
    segment_block,
    previous_block,
):
    _, _, _, factor_in, factor_out, span_total = vector_factors(
        decay_block, segment_block, previous_block
    )
    scaled_in = (inputs_block * (factor_out * step_block)[:, :, None]).astype(jnp.bfloat16)
    scaled_grad = (grads_block * factor_in[:, :, None]).astype(jnp.bfloat16)
    state_part = jnp.einsum("shp,sn->hpn", scaled_in, b_block, preferred_element_type=jnp.float32)
    grad_part = jnp.einsum("uhp,un->hpn", scaled_grad, c_block, preferred_element_type=jnp.float32)
    return (span_total, state_part, grad_part)


def span_grads(
    inputs_block,
    grads_block,
    b_block,
    c_block,
    step_block,
    decay_block,
    segment_block,
    previous_block,
    preact_block,
    state_in,
    state_grad,
    decay_rate,
    skip_gain,
):
    cumulative, mask_in, mask_out, factor_in, factor_out, _ = vector_factors(
        decay_block, segment_block, previous_block
    )
    pair_decay = pair_factor(cumulative, segment_block)
    scores = jnp.einsum("un,sn->us", c_block, b_block, preferred_element_type=jnp.float32)
    cross_term = jnp.einsum(
        "uhp,shp->hus", grads_block, inputs_block, preferred_element_type=jnp.float32
    )
    masked = (pair_decay * scores[None]).astype(jnp.bfloat16)
    weighted = pair_decay * cross_term * step_block.T[:, None, :]
    summed = jnp.sum(weighted, axis=0).astype(jnp.bfloat16)
    products = weighted * scores[None]
    change = jnp.sum(products, axis=2) - jnp.sum(products, axis=1)
    first_term = reverse_cumsum(change, 1).T
    h_low = state_in.astype(jnp.bfloat16)
    e_low = state_grad.astype(jnp.bfloat16)
    along_b = jnp.einsum("tn,hpn->thp", b_block, e_low, preferred_element_type=jnp.float32)
    grad_b_prod = (
        jnp.einsum("hut,uhp->thp", masked, grads_block, preferred_element_type=jnp.float32)
        + factor_out[:, :, None] * along_b
    )
    grad_x = (step_block[:, :, None] * grad_b_prod + skip_gain[None, :, None] * grads_block).astype(
        jnp.bfloat16
    )
    x_state = jnp.einsum("thp,hpn->thn", inputs_block, e_low, preferred_element_type=jnp.float32)
    y_state = jnp.einsum("uhp,hpn->uhn", grads_block, h_low, preferred_element_type=jnp.float32)
    grad_b = jnp.einsum("us,un->sn", summed, c_block, preferred_element_type=jnp.float32) + jnp.sum(
        (step_block * factor_out)[:, :, None] * x_state, axis=1
    )
    grad_c = jnp.einsum("us,sn->un", summed, b_block, preferred_element_type=jnp.float32) + jnp.sum(
        factor_in[:, :, None] * y_state, axis=1
    )
    z_term = jnp.sum(y_state * c_block[:, None, :], axis=2)
    w_term = step_block * jnp.sum(x_state * b_block[:, None, :], axis=2)
    second_term = mask_in[:, None] * reverse_cumsum(factor_in * z_term, 0)
    carried = factor_out * w_term
    third_term = mask_out[:, None] * (jnp.cumsum(carried, axis=0) - carried)
    fourth_term = factor_out * factor_in * jnp.sum(state_grad * state_in, axis=(1, 2))[None, :]
    decay_grad = first_term + second_term + third_term + fourth_term
    x_dot_g = jnp.sum(inputs_block * grad_b_prod, axis=2)
    grad_dt = (x_dot_g + decay_rate[None, :] * decay_grad) * jax.nn.sigmoid(preact_block)
    grad_alog = jnp.sum(decay_grad * step_block, axis=0) * decay_rate
    grad_bias = jnp.sum(grad_dt, axis=0)
    grad_skip = jnp.einsum(
        "thp,thp->h", grads_block, inputs_block, preferred_element_type=jnp.float32
    )
    return (grad_x, grad_dt, grad_b, grad_c, grad_alog, grad_bias, grad_skip)


def local_link(running, pieces):
    decay_gain, held_state = running
    span_total, span_part = pieces
    return ((decay_gain * span_total, span_total[:, None, None] * held_state + span_part), running)


def link_maps(earlier, later):
    return (earlier[0] * later[0], later[0][:, None, None] * earlier[1] + later[1])


def doubling(element, reverse):
    axis_count = lax.axis_size("ctx")
    own_index = lax.axis_index("ctx")
    distances = [1] + [2**power for power in range((axis_count - 1).bit_length())]
    running = element
    for section_num, distance in enumerate(distances):
        shift_by = -distance if reverse else distance
        received = from_behind((running[0], running[1]), "ctx", shift_by)
        source = own_index - shift_by
        present = (source >= 0) & (source < axis_count)
        fixed = (jnp.where(present, received[0], 1.0), received[1])
        if section_num == 0:
            running = fixed
        else:
            running = link_maps(fixed, running)
    return running


def general_local(inputs, dt_raw, dt_bias, a_log, b_in, c_in, skip_gain, grad_out, doc_lengths):
    token_count = inputs.shape[1]
    head_count = dt_bias.shape[0]
    head_width = inputs.shape[2] // head_count
    state_size = b_in.shape[2]
    span_count = token_count // SPAN
    preact = dt_raw[0] + dt_bias[None, :]
    step_size = jax.nn.softplus(preact)
    decay_rate = -jnp.exp(a_log)
    log_decay = step_size * decay_rate[None, :]
    lengths = doc_lengths[0]
    starts = jnp.cumsum(lengths) - lengths
    positions = lax.axis_index("ctx") * token_count + jnp.arange(token_count, dtype=jnp.int32)
    segment = doc_index(positions, starts)
    previous = doc_index(positions[::SPAN] - 1, starts)
    shaped = (
        inputs[0].reshape(span_count, SPAN, head_count, head_width),
        grad_out[0].reshape(span_count, SPAN, head_count, head_width),
        b_in[0].reshape(span_count, SPAN, state_size),
        c_in[0].reshape(span_count, SPAN, state_size),
        step_size.reshape(span_count, SPAN, head_count),
        log_decay.reshape(span_count, SPAN, head_count),
        segment.reshape(span_count, SPAN),
        previous,
    )
    totals, state_parts, grad_parts = jax.vmap(first_pass)(*shaped)
    start_maps = (
        jnp.ones((head_count,), jnp.float32),
        jnp.zeros((head_count, head_width, state_size), jnp.float32),
    )
    forward_map, (gain_before, local_entry) = lax.scan(
        local_link, start_maps, (totals, state_parts)
    )
    backward_map, (gain_after, local_leave) = lax.scan(
        local_link, start_maps, (totals, grad_parts), reverse=True
    )
    entry_state = doubling(forward_map, False)[1]
    leave_state = doubling(backward_map, True)[1]
    entering = gain_before[:, :, None, None] * entry_state[None] + local_entry
    leaving = gain_after[:, :, None, None] * leave_state[None] + local_leave
    mapped = jax.vmap(span_grads, in_axes=(0, 0, 0, 0, 0, 0, 0, 0, 0, 0, 0, None, None))
    grad_x, grad_dt, grad_b, grad_c, grad_alog, grad_bias, grad_skip = mapped(
        *shaped,
        preact.reshape(span_count, SPAN, head_count),
        entering,
        leaving,
        decay_rate,
        skip_gain
    )
    b_total, c_total = lax.psum(
        (grad_b.reshape(token_count, state_size), grad_c.reshape(token_count, state_size)), "head"
    )
    alog_total, bias_total, skip_total = lax.psum(
        (jnp.sum(grad_alog, axis=0), jnp.sum(grad_bias, axis=0), jnp.sum(grad_skip, axis=0)),
        ("dp", "ctx"),
    )
    return (
        grad_x.reshape(1, token_count, head_count * head_width),
        grad_dt,
        b_total[None],
        c_total[None],
        alog_total,
        bias_total,
        skip_total,
    )


def dot(left, right, dims, precision=None):
    return lax.dot_general(
        left, right, (dims, ((), ())), precision=precision, preferred_element_type=F32
    )


def nn(left, right, precision=None):
    return dot(left, right, ((1,), (0,)), precision)


def nt(left, right, precision=None):
    return dot(left, right, ((1,), (1,)), precision)


def tn(left, right, precision=None):
    return dot(left, right, ((0,), (0,)), precision)


def iota(shape, axis):
    return lax.broadcasted_iota(jnp.int32, shape, axis)


def eye(size):
    return (iota((size, size), 0) == iota((size, size), 1)).astype(F32)


def head_rows(heads, width, chunk=slice(None)):
    begin, end, _ = chunk.indices(heads * width)
    shape = (heads, end - begin)
    start = iota(shape, 0) * width
    feature = iota(shape, 1) + begin
    return ((feature >= start) & (feature < start + width)).astype(BF16)


def head_columns(features, heads):
    width = features // heads
    start = iota((features, heads), 1) * width
    feature = iota((features, heads), 0)
    return ((feature >= start) & (feature < start + width)).astype(BF16)


def thirds(value):
    high = value.astype(BF16)
    rest = value - high.astype(F32)
    middle = rest.astype(BF16)
    low = (rest - middle.astype(F32)).astype(BF16)
    return jnp.concatenate([high, middle, low], axis=0)


def spread(factor, rows):
    return tn(thirds(factor), jnp.concatenate([rows] * 3, axis=0))


def spread_row(factor, features):
    heads = factor.shape[1]
    wide = jnp.broadcast_to(factor, (8, heads))
    high = wide.astype(BF16)
    rest = wide - high.astype(F32)
    middle = rest.astype(BF16)
    low = (rest - middle.astype(F32)).astype(BF16)
    rows = head_rows(heads, features // heads)
    return (nn(high, rows) + nn(middle, rows) + nn(low, rows))[:1]


def head_sum(values, columns):
    high = values.astype(BF16)
    low = (values - high.astype(F32)).astype(BF16)
    return nn(high, columns) + nn(low, columns)


def as_column(row):
    size = row.shape[1]
    return jnp.sum(jnp.where(eye(size) > 0, row, 0.0), axis=1, keepdims=True)


def as_row(column):
    size = column.shape[0]
    return jnp.sum(jnp.where(eye(size) > 0, column, 0.0), axis=0, keepdims=True)


def doc_of(lens_ref, positions):
    count = jnp.zeros(positions.shape, jnp.int32)
    start = jnp.int32(0)
    for index in range(lens_ref.shape[1]):
        count = count + (start <= positions).astype(jnp.int32)
        start = start + lens_ref[0, index]
    return count


def doc_scalar(lens_ref, position):
    count = jnp.int32(0)
    start = jnp.int32(0)
    for index in range(lens_ref.shape[1]):
        count = count + jnp.where(start <= position, 1, 0)
        start = start + lens_ref[0, index]
    return count


def doc_start(lens_ref, position):
    found = jnp.int32(0)
    start = jnp.int32(0)
    for index in range(lens_ref.shape[1]):
        found = jnp.where(start <= position, start, found)
        start = start + lens_ref[0, index]
    return found


def leads():
    return lax.rem(lax.axis_index("ctx"), 2) == 0


AUX = (
    "dt", "gate", "cum", "din", "dout", "tot", "alpha_s", "beta_s", "alpha_u", "beta_u", "rate", "doc", "masks",
    "short", "gain",
)
LOCAL = ("first", "x_gb", "skip")
FAR = ("z_own", "w_own", "z_far", "w_far", "carried")


def take(ref, names, name, heads):
    slot = names.index(name) * heads
    return ref[slot : slot + heads, :]


def put(ref, names, heads, values):
    for name, value in values.items():
        slot = names.index(name) * heads
        ref[slot : slot + heads, :] = value


def halves(upper, lower, rows):
    width = upper.shape[1]
    return jnp.concatenate(
        [jnp.broadcast_to(item, (rows // 2, width)) for item in (upper, lower)], axis=0
    )


def fill(ref, scaled, *others):
    span = scaled.shape[0]
    base = 0
    for block in range(scaled.shape[1] // LANES):
        ref[base : base + span, :] = scaled[:, block * LANES : (block + 1) * LANES].astype(F32)
        base = base + span
    for part in others:
        ref[base : base + part.shape[0], :] = part
        base = base + part.shape[0]


def prep_kernel(
    lens_hbm, raw_hbm, bias_hbm, alog_hbm, skip_hbm, x_hbm, g_hbm, b_hbm, c_hbm,
    pay_one_ref, pay_two_ref, aux_ref, xs_ref, gs_ref, x_ref, g_ref, b_ref, c_ref, lens_ref, raw_ref, bias_ref, alog_ref, skip_ref, sems,
):
    moves = (
        (lens_hbm, lens_ref), (raw_hbm.at[0], raw_ref), (bias_hbm, bias_ref),
        (alog_hbm, alog_ref), (skip_hbm, skip_ref), (x_hbm.at[0], x_ref), (g_hbm.at[0], g_ref),
        (b_hbm.at[0], b_ref), (c_hbm.at[0], c_ref),
    )
    copies = [
        pltpu.make_async_copy(source, target, sems.at[index])
        for index, (source, target) in enumerate(moves)
    ]
    for copy in copies:
        copy.start()
    small, large = copies[:5], copies[5:]
    span, features = x_ref.shape
    heads = raw_ref.shape[0]
    row, column = iota((span, span), 0), iota((span, span), 1)
    upto = (row <= column).astype(F32)
    beyond = (row > column).astype(F32)
    part = slice(0, features // 2)
    rows = head_rows(heads, features // heads, part)
    for copy in small:
        copy.wait()
    base = lax.axis_index("ctx") * span
    doc = doc_of(lens_ref, base + iota((1, span), 1))
    before = doc_scalar(lens_ref, base - 1)
    last = doc_scalar(lens_ref, base + span - 1)
    inward = (doc == before).astype(F32)
    outward = (doc == last).astype(F32)
    whole = jnp.where(last == before, 1.0, 0.0)
    short_before = jnp.where(base - doc_start(lens_ref, base - 1) <= span // 2, 1.0, 0.0)
    short_last = jnp.where(
        base + span - doc_start(lens_ref, base + span - 1) <= span // 2, 1.0, 0.0
    )
    preact = raw_ref[...] + as_column(bias_ref[...])
    dt = jnp.maximum(preact, 0.0) + jnp.log1p(jnp.exp(-jnp.abs(preact)))
    gate = 1.0 / (1.0 + jnp.exp(-preact))
    rate = -jnp.exp(as_column(alog_ref[...]))
    cum = nn(dt * rate, upto, EXACT)
    cum_last = cum[:, span - 1 : span]
    din = inward * jnp.exp(cum)
    dout = outward * jnp.exp(cum_last - cum)
    pair = jnp.concatenate([dt, gate], axis=0)
    seen = nn(pair * inward, upto, EXACT)
    left = nn(pair * outward, beyond, EXACT)
    alpha_s = rate * left[:heads]
    beta_s = rate * left[heads:] + gate / dt
    alpha_u = rate * seen[:heads]
    beta_u = rate * seen[heads:]
    put(aux_ref, AUX, heads, dict(
        dt=dt, gate=gate, cum=cum, din=din, dout=dout,
        tot=jnp.broadcast_to(whole * jnp.exp(cum_last), dt.shape),
        gain=jnp.broadcast_to(as_column(skip_ref[...]), dt.shape),
        alpha_s=alpha_s, beta_s=beta_s, alpha_u=alpha_u, beta_u=beta_u,
        rate=jnp.broadcast_to(rate, dt.shape), doc=jnp.broadcast_to(doc.astype(F32), dt.shape),
        masks=halves(inward, outward, heads),
        short=halves(jnp.full((1, span), short_before), jnp.full((1, span), short_last), heads),
    ))
    x_factor, g_factor = spread(dout * dt, rows), spread(din, rows)
    for copy in large:
        copy.wait()
    xs = (x_ref[:, part].astype(F32) * x_factor).astype(BF16)
    gs = (g_ref[:, part].astype(F32) * g_factor).astype(BF16)
    xs_ref[...] = xs
    gs_ref[...] = gs
    first = leads()

    def mine(ref):
        rows = span // lax.axis_size("head")
        start = pl.multiple_of(lax.axis_index("head") * rows, rows)
        return ref[pl.ds(start, rows), :].astype(F32)

    @pl.when(first)
    def _():
        fill(pay_one_ref, xs, mine(b_ref), alpha_s, beta_s)
        fill(pay_two_ref, gs, mine(c_ref), alpha_u, beta_u)

    @pl.when(jnp.logical_not(first))
    def _():
        fill(pay_one_ref, gs, mine(c_ref), alpha_u, beta_u)
        fill(pay_two_ref, xs, mine(b_ref), alpha_s, beta_s)


def rest_kernel(x_ref, g_ref, aux_ref, pay_one_ref, pay_two_ref, xs_ref, gs_ref, tot_ref, gain_ref):
    features = x_ref.shape[1]
    heads = aux_ref.shape[0] // len(AUX)
    part = slice(features // 2, features)
    rows = head_rows(heads, features // heads, part)
    dout, dt = take(aux_ref, AUX, "dout", heads), take(aux_ref, AUX, "dt", heads)
    xs = (x_ref[:, part].astype(F32) * spread(dout * dt, rows)).astype(BF16)
    gs = (g_ref[:, part].astype(F32) * spread(take(aux_ref, AUX, "din", heads), rows)).astype(BF16)
    xs_ref[...] = xs
    gs_ref[...] = gs
    for name, ref in (("tot", tot_ref), ("gain", gain_ref)):
        row = as_row(take(aux_ref, AUX, name, heads)[:, :1])
        ref[...] = jnp.broadcast_to(spread_row(row, features), ref.shape)
    first = leads()

    @pl.when(first)
    def _():
        fill(pay_one_ref, xs)
        fill(pay_two_ref, gs)

    @pl.when(jnp.logical_not(first))
    def _():
        fill(pay_one_ref, gs)
        fill(pay_two_ref, xs)


def local_kernel(
    x_ref, g_ref, aux_ref, b_ref, c_ref, gb_ref, small_ref, grads_ref, own_ref
):
    span, features = x_ref.shape
    heads = aux_ref.shape[0] // len(AUX)
    width = features // heads
    row, column = iota((span, span), 0), iota((span, span), 1)
    dt = take(aux_ref, AUX, "dt", heads)
    gate = take(aux_ref, AUX, "gate", heads)
    cum = take(aux_ref, AUX, "cum", heads)
    rate = take(aux_ref, AUX, "rate", heads)
    doc = take(aux_ref, AUX, "doc", heads)
    upright = nt(eye(span), jnp.concatenate([dt, cum, doc], axis=0), EXACT)
    doc_s = upright[:, 2 * heads : 2 * heads + 1]
    closed = jnp.where((column >= row) & (jnp.abs(doc_s - doc[:1, :]) < 0.5), 0.0, -1e30)
    scores = nt(b_ref[...], c_ref[...])
    summed = jnp.zeros((span, span), F32)
    lane = iota((span, heads), 1)
    from_s = jnp.zeros((span, heads), F32)
    to_u = []
    for pair in range(0, heads, 2):
        outs = []
        for head in (pair, pair + 1):
            part = slice(head * width, (head + 1) * width)
            g_head, x_head = g_ref[:, part], x_ref[:, part]
            cross = nt(x_head, g_head)
            cum_s = upright[:, heads + head : heads + head + 1]
            decay = jnp.exp(cum[head : head + 1, :] - cum_s + closed)
            masked = decay * scores
            weighted = decay * cross * upright[:, head : head + 1]
            summed = summed + weighted
            product = weighted * scores
            from_s = jnp.where(lane == head, jnp.sum(product, axis=1, keepdims=True), from_s)
            to_u.append(jnp.sum(product, axis=0, keepdims=True))
            outs.append(nn(masked.astype(BF16), g_head))
        gb_ref[:, pair * width : (pair + 2) * width] = jnp.concatenate(outs, axis=1)
    onward = (row >= column).astype(F32)
    turn = eye(heads)
    change = jnp.concatenate(to_u, axis=0) - nt(turn, from_s, EXACT)
    first = nn(change, onward, EXACT)
    columns = head_columns(features, heads)
    x_wide = x_ref[...].astype(F32)
    sums = jnp.concatenate(
        [head_sum(x_wide * gb_ref[...], columns),
         head_sum(x_wide * g_ref[...].astype(F32), columns)], axis=1
    )
    sums = nt(eye(2 * heads), sums, EXACT)
    x_gb, skip = sums[:heads], sums[heads:]
    put(small_ref, LOCAL, heads, dict(first=first, x_gb=x_gb, skip=skip))
    own_ref[:heads, :] = rate * dt * first
    own_ref[heads : 2 * heads, :] = gate * (x_gb + rate * first)
    own_ref[2 * heads :, :] = skip
    grads_ref[:span, :] = nn(summed.astype(BF16), c_ref[...])
    grads_ref[span:, :] = nn(jnp.transpose(summed).astype(BF16), b_ref[...])


def neighbours(one_ref, two_ref):
    first = leads()

    def behind(part):
        return jnp.where(first, two_ref[part, :], one_ref[part, :])

    def ahead(part):
        return jnp.where(first, one_ref[part, :], two_ref[part, :])

    return behind, ahead


def wide(get, span, blocks):
    return jnp.concatenate(
        [get(slice(k * span, (k + 1) * span)).astype(BF16) for k in range(blocks)], axis=1
    )


def relay_terms(xp, gn, xs, gs, tot, scores, rows, push_ref, far_push_ref):
    gn_tot = (gn.astype(F32) * tot).astype(BF16)
    pull, push = nn(scores[0], xp), nn(scores[1], gn)
    far_pull, far_push = nn(scores[2], xp), nn(scores[3], gn_tot)
    push_ref[...] = push
    far_push_ref[...] = far_push
    products = (
        gs.astype(F32) * pull,
        xs.astype(F32) * push,
        gn_tot.astype(F32) * far_pull,
        xp.astype(F32) * far_push,
    )
    return [nt(rows, item.astype(BF16)) for item in products]


def maps_kernel(base, got_one_ref, got_two_ref, maps_ref):
    behind, ahead = neighbours(got_one_ref, got_two_ref)
    rows = maps_ref.shape[0] // 2
    maps_ref[:rows, :] = behind(slice(base, base + rows))
    maps_ref[rows:, :] = ahead(slice(base, base + rows))


def relay_first_kernel(
    got_one_ref, got_two_ref, maps_ref, other_ref, xs_ref, gs_ref, b_ref, c_ref, tot_ref, aux_ref,
    push_ref, far_push_ref, xp_ref, gn_ref, bp_ref, cn_ref, scores_ref, part_ref, weights_ref,
):
    span, features = xs_ref.shape
    heads = aux_ref.shape[0] // len(AUX)
    width = tot_ref.shape[1] // heads
    blocks = features // LANES
    behind, ahead = neighbours(got_one_ref, got_two_ref)
    rows = span // 2
    lower = lax.axis_index("head") == 0

    def whole(part):
        one, two = maps_ref[part, :], other_ref[part, :]
        return jnp.concatenate(
            [jnp.where(lower, one, two), jnp.where(lower, two, one)], axis=0
        ).astype(BF16)

    xp, bp = wide(behind, span, blocks), whole(slice(0, rows))
    gn, cn = wide(ahead, span, blocks), whole(slice(rows, 2 * rows))
    base = blocks * span + rows
    weights_ref[: 2 * heads, :] = behind(slice(base, base + 2 * heads))
    weights_ref[2 * heads :, :] = ahead(slice(base, base + 2 * heads))
    b, c = b_ref[...], c_ref[...]
    scores = [item.astype(BF16) for item in (nt(c, bp), nt(b, cn), nt(cn, bp), nt(bp, cn))]
    part = slice(0, features)
    sums = relay_terms(
        xp, gn, xs_ref[...], gs_ref[...], tot_ref[:1, part], scores,
        head_rows(heads, width, part), push_ref, far_push_ref,
    )
    for index in range(4):
        scores_ref[index * span : (index + 1) * span, :] = scores[index]
        part_ref[index * heads : (index + 1) * heads, :] = sums[index]
    xp_ref[...] = xp
    gn_ref[...] = gn
    bp_ref[...] = bp
    cn_ref[...] = cn


def relay_kernel(
    got_one_ref, got_two_ref, xs_ref, gs_ref, tot_ref, aux_ref, scores_ref, part_ref, weights_ref,
    own_ref, red_ref, far_ref, push_ref, far_push_ref, xp_ref, gn_ref,
):
    span, features = xs_ref.shape
    heads = aux_ref.shape[0] // len(AUX)
    total = tot_ref.shape[1]
    blocks = features // LANES
    behind, ahead = neighbours(got_one_ref, got_two_ref)
    xp, gn = wide(behind, span, blocks), wide(ahead, span, blocks)
    part = slice(total - features, total)
    sums = relay_terms(
        xp, gn, xs_ref[...], gs_ref[...], tot_ref[:1, part],
        [scores_ref[index * span : (index + 1) * span, :] for index in range(4)],
        head_rows(heads, total // heads, part), push_ref, far_push_ref,
    )
    z_own, w_own, z_far, w_far = (
        sums[index] + part_ref[index * heads : (index + 1) * heads, :] for index in range(4)
    )
    alpha_p, beta_p, alpha_n, beta_n = (
        weights_ref[index * heads : (index + 1) * heads, :] for index in range(4)
    )
    carried = jnp.sum(z_far, axis=1, keepdims=True)
    rate = take(aux_ref, AUX, "rate", heads)
    alog = (
        own_ref[:heads, :]
        + z_own * take(aux_ref, AUX, "alpha_u", heads)
        + w_own * take(aux_ref, AUX, "alpha_s", heads)
        + carried * rate * take(aux_ref, AUX, "dt", heads)
        + z_far * alpha_n
        + w_far * alpha_p
    )
    bias = (
        own_ref[heads : 2 * heads, :]
        + z_own * take(aux_ref, AUX, "beta_u", heads)
        + w_own * take(aux_ref, AUX, "beta_s", heads)
        + carried * rate * take(aux_ref, AUX, "gate", heads)
        + z_far * beta_n
        + w_far * beta_p
    )
    stack = jnp.concatenate([alog, bias, own_ref[2 * heads :, :]], axis=0)
    red_ref[:, : 3 * heads] = nt(jnp.ones((8, span), F32), stack, EXACT)
    red_ref[:, 3 * heads :] = jnp.zeros((8, red_ref.shape[1] - 3 * heads), F32)
    put(far_ref, FAR, heads, dict(
        z_own=z_own, w_own=w_own, z_far=z_far, w_far=w_far,
        carried=jnp.broadcast_to(carried, z_own.shape),
    ))
    xp_ref[...] = xp
    gn_ref[...] = gn


def both(one_ref, two_ref):
    return jnp.concatenate([one_ref[...], two_ref[...]], axis=1)


def hops_kernel(
    xp0_ref, xp1_ref, gn0_ref, gn1_ref, bp_ref, cn_ref, aux_ref, far_ref, push0_ref, push1_ref,
    tot_ref, hop_one_ref, hop_two_ref,
):
    xp, gn, bp, cn = both(xp0_ref, xp1_ref), both(gn0_ref, gn1_ref), bp_ref[...], cn_ref[...]
    span, features = xp.shape
    blocks = features // LANES
    heads = far_ref.shape[0] // len(FAR)
    gn_tot = (gn.astype(F32) * tot_ref[:1, :]).astype(BF16)
    grad_b_far = nn(nt(xp, gn_tot).astype(BF16), cn)
    grad_c_far = nn(nt(gn_tot, xp).astype(BF16), bp)
    half = span // 2
    base = blocks * half
    short = take(aux_ref, AUX, "short", heads)[:1, :] > 0.5

    def load(ref, grad, name, heavy):
        if heavy:
            for block in range(blocks):
                push_ref = (push0_ref, push1_ref)[block * 2 // blocks]
                inner = (block % (blocks // 2)) * LANES
                ref[block * half : (block + 1) * half, :] = jnp.where(
                    short,
                    push_ref[half:, inner : inner + LANES],
                    gn_tot[:half, block * LANES : (block + 1) * LANES].astype(F32),
                )
            ref[base : base + half, :] = jnp.where(short, grad[half:], cn[:half].astype(F32))
        else:
            ref[:span, :] = grad
            ref[span : base + half, :] = jnp.zeros((base + half - span, LANES), F32)
        rest = base + half
        ref[rest : rest + heads, :] = take(far_ref, FAR, name, heads)

    first = leads()

    @pl.when(first)
    def _():
        load(hop_one_ref, grad_c_far, "z_far", False)
        load(hop_two_ref, grad_b_far, "w_far", True)

    @pl.when(jnp.logical_not(first))
    def _():
        load(hop_one_ref, grad_b_far, "w_far", True)
        load(hop_two_ref, grad_c_far, "z_far", False)


def grads_kernel(
    xp0_ref, xp1_ref, gn0_ref, gn1_ref, bp_ref, cn_ref, xs0_ref, xs1_ref, gs0_ref, gs1_ref,
    grads_ref, sums_ref,
):
    xp, gn = both(xp0_ref, xp1_ref), both(gn0_ref, gn1_ref)
    xs, gs = both(xs0_ref, xs1_ref), both(gs0_ref, gs1_ref)
    span = xp.shape[0]
    sums_ref[:span, :] = grads_ref[:span, :] + nn(nt(xs, gn).astype(BF16), cn_ref[...])
    sums_ref[span:, :] = grads_ref[span:, :] + nn(nt(gs, xp).astype(BF16), bp_ref[...])


def ready_kernel(
    g_ref, aux_ref, gain_ref, gbl_ref, push0_ref, push1_ref, near_ref, weight_ref
):
    features = g_ref.shape[1]
    heads = aux_ref.shape[0] // len(AUX)
    rows = head_rows(heads, features // heads)
    dt = take(aux_ref, AUX, "dt", heads)
    weight = spread(dt * take(aux_ref, AUX, "dout", heads), rows)
    weight_ref[...] = weight
    near_ref[...] = (
        spread(dt, rows) * gbl_ref[...]
        + weight * both(push0_ref, push1_ref)
        + gain_ref[:1, :] * g_ref[...].astype(F32)
    )


def final_kernel(
    far_one_ref, far_two_ref, b_ref, aux_ref, near_ref, weight_ref, small_ref, far_ref,
    gx_ref, gdt_ref,
):
    span, features = near_ref.shape
    heads = aux_ref.shape[0] // len(AUX)
    blocks = features // LANES
    half = span // 2
    behind, ahead = neighbours(far_one_ref, far_two_ref)
    base = blocks * half
    short = take(aux_ref, AUX, "short", heads)[heads // 2 : heads // 2 + 1, :] > 0.5
    cn = ahead(slice(base, base + half)).astype(BF16)
    scores = nt(b_ref[...], cn).astype(BF16)
    parts = [ahead(slice(k * half, (k + 1) * half)) for k in range(blocks)]
    other = nn(scores, jnp.concatenate(parts, axis=1).astype(BF16))
    blank = jnp.zeros((half, LANES), F32)
    push = jnp.concatenate(
        [
            jnp.where(
                short,
                jnp.concatenate([blank, part], axis=0),
                other[:, k * LANES : (k + 1) * LANES],
            )
            for k, part in enumerate(parts)
        ],
        axis=1,
    )
    gx_ref[0] = (near_ref[...] + weight_ref[...] * push).astype(BF16)
    dt = take(aux_ref, AUX, "dt", heads)
    gate = take(aux_ref, AUX, "gate", heads)
    rate = take(aux_ref, AUX, "rate", heads)
    inout = take(aux_ref, AUX, "masks", heads)
    inward, outward = inout[:1, :], inout[heads // 2 : heads // 2 + 1, :]
    rest = base + half
    z = take(far_ref, FAR, "z_own", heads) + behind(slice(rest, rest + heads))
    w = take(far_ref, FAR, "w_own", heads) + ahead(slice(rest, rest + heads))
    row, column = iota((span, span), 0), iota((span, span), 1)
    decay_grad = (
        take(small_ref, LOCAL, "first", heads)
        + inward * nn(z, (row >= column).astype(F32), EXACT)
        + outward * nn(w, (row < column).astype(F32), EXACT)
        + take(far_ref, FAR, "carried", heads)
    )
    x_gb = take(small_ref, LOCAL, "x_gb", heads) + w / dt
    gdt_ref[0] = (x_gb + rate * decay_grad) * gate


def half_kernel(far_one_ref, far_two_ref, xs0_ref, xs1_ref, aux_ref, sums_ref, half_ref):
    xs = both(xs0_ref, xs1_ref)
    span, features = xs.shape
    heads = aux_ref.shape[0] // len(AUX)
    half = span // 2
    blocks = features // LANES
    base = blocks * half
    behind, ahead = neighbours(far_one_ref, far_two_ref)
    short = take(aux_ref, AUX, "short", heads)[heads // 2 : heads // 2 + 1, :] > 0.5
    last = ahead(slice(base, base + half))
    gn = wide(ahead, half, blocks)
    grad = nn(nt(xs, gn).astype(BF16), last.astype(BF16))
    share = jnp.concatenate([jnp.zeros_like(last), last], axis=0)
    half_ref[:span, :] = sums_ref[:span, :] + jnp.where(short, share, grad)
    half_ref[span:, :] = sums_ref[span:, :] + behind(slice(0, span))


def close_kernel(
    red_ref, last_ref, half_ref, other_ref, b_ref, c_ref, alog_ref, bias_ref, skip_ref
):
    span = b_ref.shape[1]
    heads = alog_ref.shape[1]
    red = red_ref[:1, :] + last_ref[:1, :]
    alog_ref[...] = red[:, :heads]
    bias_ref[...] = red[:, heads : 2 * heads]
    skip_ref[...] = red[:, 2 * heads : 3 * heads]
    b_ref[0] = half_ref[:span, :] + other_ref[:span, :]
    c_ref[0] = half_ref[span:, :] + other_ref[span:, :]


def call(kernel, shapes, operands, raw=0, flops=0, scratch=()):
    def space(index):
        return pltpu.HBM if index < raw else pltpu.VMEM

    moved = sum(item.size * item.dtype.itemsize for item in operands) + sum(
        item.size * jnp.dtype(item.dtype).itemsize for item in shapes
    )
    return pl.pallas_call(
        kernel,
        out_shape=shapes,
        in_specs=[pl.BlockSpec(memory_space=space(index)) for index in range(len(operands))],
        out_specs=[pl.BlockSpec(memory_space=pltpu.VMEM)] * len(shapes),
        scratch_shapes=list(scratch),
        cost_estimate=pl.CostEstimate(flops=flops, bytes_accessed=moved, transcendentals=0),
        compiler_params=pltpu.CompilerParams(vmem_limit_bytes=VMEM_GRANT),
    )(
        *(
            pltpu.with_memory_space_constraint(item, pltpu.HBM) if index < raw else item
            for index, item in enumerate(operands)
        )
    )


def exchange(array, turn, senders):
    count = lax.axis_size("ctx")
    pairs = [(i, i + 1 if (i + turn) % 2 == 0 else i - 1) for i in range(count)]
    return lax.ppermute(
        array, "ctx", [(i, j) for i, j in pairs if 0 <= j < count and i in senders]
    )


def flip(array, axis, bit):
    return lax.ppermute(array, axis, [(i, i ^ bit) for i in range(lax.axis_size(axis))])


def near_local(inputs, dt_raw, dt_bias, a_log, b_in, c_in, skip_gain, grad_out, doc_lengths):
    _, span, features = inputs.shape
    heads = dt_bias.shape[0]
    state = b_in.shape[2]
    count = lax.axis_size("ctx")
    struct = jax.ShapeDtypeStruct
    bias, alog, skip = (item.reshape(1, heads) for item in (dt_bias, a_log, skip_gain))
    raw = jnp.swapaxes(dt_raw, 1, 2)
    split = features // 2
    sides = lax.axis_size("head")
    blocks = split // LANES * span
    base = 2 * blocks + span
    pay = struct((blocks + span // sides + 2 * heads, LANES), F32)
    pay_rest = struct((blocks, LANES), F32)
    full, low = struct((span, features), F32), struct((span, features), BF16)
    full_part, low_part = struct((span, split), F32), struct((span, split), BF16)
    line = struct((8, features), F32)
    square = struct((span, state), BF16)
    pair = struct((2 * span, state), F32)
    quad = struct((4 * heads, span), F32)
    one_row = pltpu.VMEM((1, heads), F32)
    pay_one, pay_two, aux, xs0, gs0, x, g, b, c = call(
        prep_kernel,
        (pay, pay, struct((len(AUX) * heads, span), F32), low_part, low_part, low, low, square,
         square),
        (doc_lengths, raw, bias, alog, skip, inputs, grad_out, b_in, c_in),
        raw=9, flops=10**8,
        scratch=[pltpu.SMEM(doc_lengths.shape, jnp.int32), pltpu.VMEM((heads, span), F32),
                 one_row, one_row, one_row, pltpu.SemaphoreType.DMA((9,))],
    )
    got_two = exchange(pay_two, 1, range(count))
    got_one = exchange(pay_one, 0, range(count))
    pay_one, pay_two, xs1, gs1, tot, gain = call(
        rest_kernel, (pay_rest, pay_rest, low_part, low_part, line, line), (x, g, aux), flops=10**7
    )
    more_two = exchange(pay_two, 1, range(count))
    more_one = exchange(pay_one, 0, range(count))
    gb_local, small, grads, own = call(
        local_kernel,
        (full, struct((len(LOCAL) * heads, span), F32), pair, struct((3 * heads, span), F32)),
        (x, g, aux, b, c),
        flops=10**8,
    )
    maps = call(
        functools.partial(maps_kernel, blocks), (struct((2 * span // sides, state), F32),),
        (got_one, got_two), flops=10**5,
    )[0]
    other_maps = flip(maps, "head", 1)
    push0, far_push0, xp0, gn0, bp, cn, scores, part, weights = call(
        relay_first_kernel,
        (full_part, full_part, low_part, low_part, square, square,
         struct((4 * span, span), BF16), quad, quad),
        (got_one, got_two, maps, other_maps, xs0, gs0, b, c, tot, aux),
        flops=10**8,
    )
    red, far, push1, far_push1, xp1, gn1 = call(
        relay_kernel,
        (struct((8, LANES), F32), struct((len(FAR) * heads, span), F32), full_part, full_part,
         low_part, low_part),
        (more_one, more_two, xs1, gs1, tot, aux, scores, part, weights, own),
        flops=10**8,
    )
    steps = []
    for axis in ("ctx", "dp"):
        bit = 1
        while bit < lax.axis_size(axis):
            steps.append((axis, bit))
            bit *= 2
    hop = struct((base // 2 + heads, LANES), F32)
    hop_one, hop_two = call(
        hops_kernel,
        (hop, hop),
        (xp0, xp1, gn0, gn1, bp, cn, aux, far, far_push0, far_push1, tot),
        flops=10**8,
    )
    sums = call(
        grads_kernel, (pair,), (xp0, xp1, gn0, gn1, bp, cn, xs0, xs1, gs0, gs1, grads), flops=10**8
    )[0]
    relays = range(1, count - 1)
    far_two = exchange(hop_two, 1, relays)
    far_one = exchange(hop_one, 0, relays)
    for axis, bit in steps[:-1]:
        red = red + flip(red, axis, bit)
    last_red = flip(red, *steps[-1])
    near, weight = call(
        ready_kernel, (full, full), (g, aux, gain, gb_local, push0, push1), flops=10**8
    )
    half = call(
        half_kernel, (pair,), (far_one, far_two, xs0, xs1, aux, sums),
        flops=10**7,
    )[0]
    grad_x, grad_dt = call(
        final_kernel,
        (struct((1, span, features), BF16), struct((1, heads, span), F32)),
        (far_one, far_two, b, aux, near, weight, small, far),
        flops=10**8,
    )
    other = flip(half, "head", 1)
    flat = struct((1, heads), F32)
    cube = struct((1, span, state), F32)
    b_total, c_total, alog_total, bias_total, skip_total = call(
        close_kernel, (cube, cube, flat, flat, flat), (red, last_red, half, other)
    )
    return (
        grad_x, jnp.swapaxes(grad_dt, 1, 2), b_total, c_total,
        alog_total.reshape(heads), bias_total.reshape(heads), skip_total.reshape(heads),
    )


def local(inputs, dt_raw, dt_bias, a_log, b_in, c_in, skip_gain, grad_out, doc_lengths):
    args = (inputs, dt_raw, dt_bias, a_log, b_in, c_in, skip_gain, grad_out, doc_lengths)
    shards = [lax.axis_size(axis) for axis in ("dp", "ctx")]
    near = (
        inputs.shape[1] == SPAN
        and shards[1] in (2, 4)
        and lax.axis_size("head") == 2
        and shards[0] & (shards[0] - 1) == 0
        and b_in.shape[2] == LANES
        and inputs.shape[2] % LANES == 0
        and dt_bias.shape[0] * 8 == LANES
    )
    if not near:
        return general_local(*args)
    return near_local(*args)


def solution(mesh):
    placed = (
        P("dp", "ctx", "head"),
        P("dp", "ctx", "head"),
        P("head"),
        P("head"),
        P("dp", "ctx", None),
        P("dp", "ctx", None),
        P("head"),
        P("dp", "ctx", "head"),
        P("dp", None),
    )
    return jax.shard_map(
        local,
        mesh=mesh,
        in_specs=placed,
        out_specs=(
            P("dp", "ctx", "head"),
            P("dp", "ctx", "head"),
            P("dp", "ctx", None),
            P("dp", "ctx", None),
            P("head"),
            P("head"),
            P("head"),
        ),
        check_vma=False,
    )
```

```python
import functools

import jax
import jax.numpy as jnp
from jax import lax
from jax.experimental import pallas as pl
from jax.experimental.pallas import tpu as pltpu
from jax.sharding import PartitionSpec as P


SPAN = 128
LANES = 128
VMEM_GRANT = 16 << 20
F32 = jnp.float32
BF16 = jnp.bfloat16
EXACT = lax.Precision.HIGHEST


def from_behind(array, axis, by):
    count = lax.axis_size(axis)
    pairs = [(i, i + by) for i in range(count) if 0 <= i + by < count]
    return lax.ppermute(array, axis, pairs)


def reverse_cumsum(values, along_axis):
    return jnp.flip(jnp.cumsum(jnp.flip(values, along_axis), axis=along_axis), along_axis)


def doc_index(positions, starts):
    return jnp.sum((starts[None, :] <= positions[:, None]).astype(jnp.int32), axis=1)


def vector_factors(decay_block, segment_block, previous_block):
    cumulative = jnp.cumsum(decay_block, axis=0)
    last_segment = segment_block[-1]
    mask_in = (segment_block == previous_block).astype(jnp.float32)
    mask_out = (segment_block == last_segment).astype(jnp.float32)
    factor_in = mask_in[:, None] * jnp.exp(cumulative)
    factor_out = mask_out[:, None] * jnp.exp(cumulative[-1][None, :] - cumulative)
    span_total = (last_segment == previous_block).astype(jnp.float32) * jnp.exp(cumulative[-1])
    return (cumulative, mask_in, mask_out, factor_in, factor_out, span_total)


def pair_factor(cumulative, segment_block):
    local_pos = jnp.arange(segment_block.shape[0], dtype=jnp.int32)
    allowed = (local_pos[:, None] >= local_pos[None, :]) & (
        segment_block[:, None] == segment_block[None, :]
    )
    spread = cumulative.T[:, :, None] - cumulative.T[:, None, :]
    return jnp.where(allowed[None], jnp.exp(jnp.where(allowed[None], spread, 0.0)), 0.0)


def first_pass(
    inputs_block,
    grads_block,
    b_block,
    c_block,
    step_block,
    decay_block,
    segment_block,
    previous_block,
):
    _, _, _, factor_in, factor_out, span_total = vector_factors(
        decay_block, segment_block, previous_block
    )
    scaled_in = (inputs_block * (factor_out * step_block)[:, :, None]).astype(jnp.bfloat16)
    scaled_grad = (grads_block * factor_in[:, :, None]).astype(jnp.bfloat16)
    state_part = jnp.einsum("shp,sn->hpn", scaled_in, b_block, preferred_element_type=jnp.float32)
    grad_part = jnp.einsum("uhp,un->hpn", scaled_grad, c_block, preferred_element_type=jnp.float32)
    return (span_total, state_part, grad_part)


def span_grads(
    inputs_block,
    grads_block,
    b_block,
    c_block,
    step_block,
    decay_block,
    segment_block,
    previous_block,
    preact_block,
    state_in,
    state_grad,
    decay_rate,
    skip_gain,
):
    cumulative, mask_in, mask_out, factor_in, factor_out, _ = vector_factors(
        decay_block, segment_block, previous_block
    )
    pair_decay = pair_factor(cumulative, segment_block)
    scores = jnp.einsum("un,sn->us", c_block, b_block, preferred_element_type=jnp.float32)
    cross_term = jnp.einsum(
        "uhp,shp->hus", grads_block, inputs_block, preferred_element_type=jnp.float32
    )
    masked = (pair_decay * scores[None]).astype(jnp.bfloat16)
    weighted = pair_decay * cross_term * step_block.T[:, None, :]
    summed = jnp.sum(weighted, axis=0).astype(jnp.bfloat16)
    products = weighted * scores[None]
    change = jnp.sum(products, axis=2) - jnp.sum(products, axis=1)
    first_term = reverse_cumsum(change, 1).T
    h_low = state_in.astype(jnp.bfloat16)
    e_low = state_grad.astype(jnp.bfloat16)
    along_b = jnp.einsum("tn,hpn->thp", b_block, e_low, preferred_element_type=jnp.float32)
    grad_b_prod = (
        jnp.einsum("hut,uhp->thp", masked, grads_block, preferred_element_type=jnp.float32)
        + factor_out[:, :, None] * along_b
    )
    grad_x = (step_block[:, :, None] * grad_b_prod + skip_gain[None, :, None] * grads_block).astype(
        jnp.bfloat16
    )
    x_state = jnp.einsum("thp,hpn->thn", inputs_block, e_low, preferred_element_type=jnp.float32)
    y_state = jnp.einsum("uhp,hpn->uhn", grads_block, h_low, preferred_element_type=jnp.float32)
    grad_b = jnp.einsum("us,un->sn", summed, c_block, preferred_element_type=jnp.float32) + jnp.sum(
        (step_block * factor_out)[:, :, None] * x_state, axis=1
    )
    grad_c = jnp.einsum("us,sn->un", summed, b_block, preferred_element_type=jnp.float32) + jnp.sum(
        factor_in[:, :, None] * y_state, axis=1
    )
    z_term = jnp.sum(y_state * c_block[:, None, :], axis=2)
    w_term = step_block * jnp.sum(x_state * b_block[:, None, :], axis=2)
    second_term = mask_in[:, None] * reverse_cumsum(factor_in * z_term, 0)
    carried = factor_out * w_term
    third_term = mask_out[:, None] * (jnp.cumsum(carried, axis=0) - carried)
    fourth_term = factor_out * factor_in * jnp.sum(state_grad * state_in, axis=(1, 2))[None, :]
    decay_grad = first_term + second_term + third_term + fourth_term
    x_dot_g = jnp.sum(inputs_block * grad_b_prod, axis=2)
    grad_dt = (x_dot_g + decay_rate[None, :] * decay_grad) * jax.nn.sigmoid(preact_block)
    grad_alog = jnp.sum(decay_grad * step_block, axis=0) * decay_rate
    grad_bias = jnp.sum(grad_dt, axis=0)
    grad_skip = jnp.einsum(
        "thp,thp->h", grads_block, inputs_block, preferred_element_type=jnp.float32
    )
    return (grad_x, grad_dt, grad_b, grad_c, grad_alog, grad_bias, grad_skip)


def local_link(running, pieces):
    decay_gain, held_state = running
    span_total, span_part = pieces
    return ((decay_gain * span_total, span_total[:, None, None] * held_state + span_part), running)


def link_maps(earlier, later):
    return (earlier[0] * later[0], later[0][:, None, None] * earlier[1] + later[1])


def doubling(element, reverse):
    axis_count = lax.axis_size("ctx")
    own_index = lax.axis_index("ctx")
    distances = [1] + [2**power for power in range((axis_count - 1).bit_length())]
    running = element
    for section_num, distance in enumerate(distances):
        shift_by = -distance if reverse else distance
        received = from_behind((running[0], running[1]), "ctx", shift_by)
        source = own_index - shift_by
        present = (source >= 0) & (source < axis_count)
        fixed = (jnp.where(present, received[0], 1.0), received[1])
        if section_num == 0:
            running = fixed
        else:
            running = link_maps(fixed, running)
    return running


def general_local(inputs, dt_raw, dt_bias, a_log, b_in, c_in, skip_gain, grad_out, doc_lengths):
    token_count = inputs.shape[1]
    head_count = dt_bias.shape[0]
    head_width = inputs.shape[2] // head_count
    state_size = b_in.shape[2]
    span_count = token_count // SPAN
    preact = dt_raw[0] + dt_bias[None, :]
    step_size = jax.nn.softplus(preact)
    decay_rate = -jnp.exp(a_log)
    log_decay = step_size * decay_rate[None, :]
    lengths = doc_lengths[0]
    starts = jnp.cumsum(lengths) - lengths
    positions = lax.axis_index("ctx") * token_count + jnp.arange(token_count, dtype=jnp.int32)
    segment = doc_index(positions, starts)
    previous = doc_index(positions[::SPAN] - 1, starts)
    shaped = (
        inputs[0].reshape(span_count, SPAN, head_count, head_width),
        grad_out[0].reshape(span_count, SPAN, head_count, head_width),
        b_in[0].reshape(span_count, SPAN, state_size),
        c_in[0].reshape(span_count, SPAN, state_size),
        step_size.reshape(span_count, SPAN, head_count),
        log_decay.reshape(span_count, SPAN, head_count),
        segment.reshape(span_count, SPAN),
        previous,
    )
    totals, state_parts, grad_parts = jax.vmap(first_pass)(*shaped)
    start_maps = (
        jnp.ones((head_count,), jnp.float32),
        jnp.zeros((head_count, head_width, state_size), jnp.float32),
    )
    forward_map, (gain_before, local_entry) = lax.scan(
        local_link, start_maps, (totals, state_parts)
    )
    backward_map, (gain_after, local_leave) = lax.scan(
        local_link, start_maps, (totals, grad_parts), reverse=True
    )
    entry_state = doubling(forward_map, False)[1]
    leave_state = doubling(backward_map, True)[1]
    entering = gain_before[:, :, None, None] * entry_state[None] + local_entry
    leaving = gain_after[:, :, None, None] * leave_state[None] + local_leave
    mapped = jax.vmap(span_grads, in_axes=(0, 0, 0, 0, 0, 0, 0, 0, 0, 0, 0, None, None))
    grad_x, grad_dt, grad_b, grad_c, grad_alog, grad_bias, grad_skip = mapped(
        *shaped,
        preact.reshape(span_count, SPAN, head_count),
        entering,
        leaving,
        decay_rate,
        skip_gain
    )
    b_total, c_total = lax.psum(
        (grad_b.reshape(token_count, state_size), grad_c.reshape(token_count, state_size)), "head"
    )
    alog_total, bias_total, skip_total = lax.psum(
        (jnp.sum(grad_alog, axis=0), jnp.sum(grad_bias, axis=0), jnp.sum(grad_skip, axis=0)),
        ("dp", "ctx"),
    )
    return (
        grad_x.reshape(1, token_count, head_count * head_width),
        grad_dt,
        b_total[None],
        c_total[None],
        alog_total,
        bias_total,
        skip_total,
    )


def dot(left, right, dims, precision=None):
    return lax.dot_general(
        left, right, (dims, ((), ())), precision=precision, preferred_element_type=F32
    )


def nn(left, right, precision=None):
    return dot(left, right, ((1,), (0,)), precision)


def nt(left, right, precision=None):
    return dot(left, right, ((1,), (1,)), precision)


def tn(left, right, precision=None):
    return dot(left, right, ((0,), (0,)), precision)


def iota(shape, axis):
    return lax.broadcasted_iota(jnp.int32, shape, axis)


def eye(size):
    return (iota((size, size), 0) == iota((size, size), 1)).astype(F32)


def head_rows(heads, width, chunk=slice(None)):
    begin, end, _ = chunk.indices(heads * width)
    shape = (heads, end - begin)
    start = iota(shape, 0) * width
    feature = iota(shape, 1) + begin
    return ((feature >= start) & (feature < start + width)).astype(BF16)


def head_columns(features, heads):
    width = features // heads
    start = iota((features, heads), 1) * width
    feature = iota((features, heads), 0)
    return ((feature >= start) & (feature < start + width)).astype(BF16)


def thirds(value):
    high = value.astype(BF16)
    rest = value - high.astype(F32)
    middle = rest.astype(BF16)
    low = (rest - middle.astype(F32)).astype(BF16)
    return jnp.concatenate([high, middle, low], axis=0)


def spread(factor, rows):
    return tn(thirds(factor), jnp.concatenate([rows] * 3, axis=0))


def spread_row(factor, features):
    heads = factor.shape[1]
    wide = jnp.broadcast_to(factor, (8, heads))
    high = wide.astype(BF16)
    rest = wide - high.astype(F32)
    middle = rest.astype(BF16)
    low = (rest - middle.astype(F32)).astype(BF16)
    rows = head_rows(heads, features // heads)
    return (nn(high, rows) + nn(middle, rows) + nn(low, rows))[:1]


def head_sum(values, columns):
    high = values.astype(BF16)
    low = (values - high.astype(F32)).astype(BF16)
    return nn(high, columns) + nn(low, columns)


def as_column(row):
    size = row.shape[1]
    return jnp.sum(jnp.where(eye(size) > 0, row, 0.0), axis=1, keepdims=True)


def as_row(column):
    size = column.shape[0]
    return jnp.sum(jnp.where(eye(size) > 0, column, 0.0), axis=0, keepdims=True)


def doc_of(lens_ref, positions):
    count = jnp.zeros(positions.shape, jnp.int32)
    start = jnp.int32(0)
    for index in range(lens_ref.shape[1]):
        count = count + (start <= positions).astype(jnp.int32)
        start = start + lens_ref[0, index]
    return count


def doc_scalar(lens_ref, position):
    count = jnp.int32(0)
    start = jnp.int32(0)
    for index in range(lens_ref.shape[1]):
        count = count + jnp.where(start <= position, 1, 0)
        start = start + lens_ref[0, index]
    return count


def doc_start(lens_ref, position):
    found = jnp.int32(0)
    start = jnp.int32(0)
    for index in range(lens_ref.shape[1]):
        found = jnp.where(start <= position, start, found)
        start = start + lens_ref[0, index]
    return found


def leads():
    return lax.rem(lax.axis_index("ctx"), 2) == 0


(
    DT, GATE, CUM, DIN, DOUT, TOT, ALPHA_S, BETA_S, ALPHA_U, BETA_U, RATE, DOC, MASKS, SHORT, GAIN
) = range(15)
AUX = 15
FIRST, X_GB = range(2)
Z_OWN, W_OWN, Z_FAR, W_FAR, CARRIED = range(5)
FAR = 5


def take(ref, slot, heads):
    return ref[slot * heads : (slot + 1) * heads, :]


def put(ref, heads, values):
    for slot, value in values.items():
        ref[slot * heads : (slot + 1) * heads, :] = value


def halves(upper, lower, rows):
    width = upper.shape[1]
    return jnp.concatenate(
        [jnp.broadcast_to(item, (rows // 2, width)) for item in (upper, lower)], axis=0
    )


def fill(ref, scaled, *others):
    span = scaled.shape[0]
    base = 0
    for block in range(scaled.shape[1] // LANES):
        ref[base : base + span, :] = scaled[:, block * LANES : (block + 1) * LANES].astype(F32)
        base = base + span
    for part in others:
        ref[base : base + part.shape[0], :] = part
        base = base + part.shape[0]


def prep_kernel(
    lens_hbm, raw_hbm, bias_hbm, alog_hbm, skip_hbm, x_hbm, g_hbm, b_hbm, c_hbm,
    pay_one_ref, pay_two_ref, aux_ref, xs_ref, gs_ref, x_ref, g_ref, b_ref, c_ref, lens_ref, raw_ref, bias_ref, alog_ref, skip_ref, sems,
):
    moves = (
        (lens_hbm, lens_ref), (raw_hbm.at[0], raw_ref), (bias_hbm, bias_ref),
        (alog_hbm, alog_ref), (skip_hbm, skip_ref), (x_hbm.at[0], x_ref), (g_hbm.at[0], g_ref),
        (b_hbm.at[0], b_ref), (c_hbm.at[0], c_ref),
    )
    copies = [
        pltpu.make_async_copy(source, target, sems.at[index])
        for index, (source, target) in enumerate(moves)
    ]
    for copy in copies:
        copy.start()
    small, large = copies[:5], copies[5:]
    span, features = x_ref.shape
    heads = raw_ref.shape[0]
    row, column = iota((span, span), 0), iota((span, span), 1)
    upto = (row <= column).astype(F32)
    beyond = (row > column).astype(F32)
    part = slice(0, features // 2)
    rows = head_rows(heads, features // heads, part)
    for copy in small:
        copy.wait()
    base = lax.axis_index("ctx") * span
    doc = doc_of(lens_ref, base + iota((1, span), 1))
    before = doc_scalar(lens_ref, base - 1)
    last = doc_scalar(lens_ref, base + span - 1)
    inward = (doc == before).astype(F32)
    outward = (doc == last).astype(F32)
    whole = jnp.where(last == before, 1.0, 0.0)
    short_before = jnp.where(base - doc_start(lens_ref, base - 1) <= span // 2, 1.0, 0.0)
    short_last = jnp.where(
        base + span - doc_start(lens_ref, base + span - 1) <= span // 2, 1.0, 0.0
    )
    preact = raw_ref[...] + as_column(bias_ref[...])
    dt = jnp.maximum(preact, 0.0) + jnp.log1p(jnp.exp(-jnp.abs(preact)))
    gate = 1.0 / (1.0 + jnp.exp(-preact))
    rate = -jnp.exp(as_column(alog_ref[...]))
    cum = nn(dt * rate, upto, EXACT)
    cum_last = cum[:, span - 1 : span]
    din = inward * jnp.exp(cum)
    dout = outward * jnp.exp(cum_last - cum)
    pair = jnp.concatenate([dt, gate], axis=0)
    seen = nn(pair * inward, upto, EXACT)
    left = nn(pair * outward, beyond, EXACT)
    alpha_s = rate * left[:heads]
    beta_s = rate * left[heads:] + gate / dt
    alpha_u = rate * seen[:heads]
    beta_u = rate * seen[heads:]
    put(aux_ref, heads, {
        DT: dt, GATE: gate, CUM: cum, DIN: din, DOUT: dout,
        TOT: jnp.broadcast_to(whole * jnp.exp(cum_last), dt.shape),
        GAIN: jnp.broadcast_to(as_column(skip_ref[...]), dt.shape),
        ALPHA_S: alpha_s, BETA_S: beta_s, ALPHA_U: alpha_u, BETA_U: beta_u,
        RATE: jnp.broadcast_to(rate, dt.shape), DOC: jnp.broadcast_to(doc.astype(F32), dt.shape),
        MASKS: halves(inward, outward, heads),
        SHORT: halves(jnp.full((1, span), short_before), jnp.full((1, span), short_last), heads),
    })
    x_factor, g_factor = spread(dout * dt, rows), spread(din, rows)
    for copy in large:
        copy.wait()
    xs = (x_ref[:, part].astype(F32) * x_factor).astype(BF16)
    gs = (g_ref[:, part].astype(F32) * g_factor).astype(BF16)
    xs_ref[...] = xs
    gs_ref[...] = gs
    first = leads()

    def mine(ref):
        rows = span // lax.axis_size("head")
        start = pl.multiple_of(lax.axis_index("head") * rows, rows)
        return ref[pl.ds(start, rows), :].astype(F32)

    @pl.when(first)
    def _():
        fill(pay_one_ref, xs, mine(b_ref), alpha_s, beta_s)
        fill(pay_two_ref, gs, mine(c_ref), alpha_u, beta_u)

    @pl.when(jnp.logical_not(first))
    def _():
        fill(pay_one_ref, gs, mine(c_ref), alpha_u, beta_u)
        fill(pay_two_ref, xs, mine(b_ref), alpha_s, beta_s)


def rest_kernel(x_ref, g_ref, aux_ref, pay_one_ref, pay_two_ref, xs_ref, gs_ref, tot_ref, gain_ref):
    features = x_ref.shape[1]
    heads = aux_ref.shape[0] // AUX
    part = slice(features // 2, features)
    rows = head_rows(heads, features // heads, part)
    dout, dt = take(aux_ref, DOUT, heads), take(aux_ref, DT, heads)
    xs = (x_ref[:, part].astype(F32) * spread(dout * dt, rows)).astype(BF16)
    gs = (g_ref[:, part].astype(F32) * spread(take(aux_ref, DIN, heads), rows)).astype(BF16)
    xs_ref[...] = xs
    gs_ref[...] = gs
    for slot, ref in ((TOT, tot_ref), (GAIN, gain_ref)):
        row = as_row(take(aux_ref, slot, heads)[:, :1])
        ref[...] = jnp.broadcast_to(spread_row(row, features), ref.shape)
    first = leads()

    @pl.when(first)
    def _():
        fill(pay_one_ref, xs)
        fill(pay_two_ref, gs)

    @pl.when(jnp.logical_not(first))
    def _():
        fill(pay_one_ref, gs)
        fill(pay_two_ref, xs)


def local_kernel(
    x_ref, g_ref, aux_ref, b_ref, c_ref, gb_ref, small_ref, grads_ref, own_ref
):
    span, features = x_ref.shape
    heads = aux_ref.shape[0] // AUX
    width = features // heads
    row, column = iota((span, span), 0), iota((span, span), 1)
    dt = take(aux_ref, DT, heads)
    gate = take(aux_ref, GATE, heads)
    cum = take(aux_ref, CUM, heads)
    rate = take(aux_ref, RATE, heads)
    doc = take(aux_ref, DOC, heads)
    upright = nt(eye(span), jnp.concatenate([dt, cum, doc], axis=0), EXACT)
    doc_s = upright[:, 2 * heads : 2 * heads + 1]
    closed = jnp.where((column >= row) & (jnp.abs(doc_s - doc[:1, :]) < 0.5), 0.0, -1e30)
    scores = nt(b_ref[...], c_ref[...])
    summed = jnp.zeros((span, span), F32)
    lane = iota((span, heads), 1)
    from_s = jnp.zeros((span, heads), F32)
    to_u = []
    for pair in range(0, heads, 2):
        outs = []
        for head in (pair, pair + 1):
            part = slice(head * width, (head + 1) * width)
            g_head, x_head = g_ref[:, part], x_ref[:, part]
            cross = nt(x_head, g_head)
            cum_s = upright[:, heads + head : heads + head + 1]
            decay = jnp.exp(cum[head : head + 1, :] - cum_s + closed)
            masked = decay * scores
            weighted = decay * cross * upright[:, head : head + 1]
            summed = summed + weighted
            product = weighted * scores
            from_s = jnp.where(lane == head, jnp.sum(product, axis=1, keepdims=True), from_s)
            to_u.append(jnp.sum(product, axis=0, keepdims=True))
            outs.append(nn(masked.astype(BF16), g_head))
        gb_ref[:, pair * width : (pair + 2) * width] = jnp.concatenate(outs, axis=1)
    onward = (row >= column).astype(F32)
    turn = eye(heads)
    change = jnp.concatenate(to_u, axis=0) - nt(turn, from_s, EXACT)
    first = nn(change, onward, EXACT)
    columns = head_columns(features, heads)
    x_wide = x_ref[...].astype(F32)
    sums = jnp.concatenate(
        [head_sum(x_wide * gb_ref[...], columns),
         head_sum(x_wide * g_ref[...].astype(F32), columns)], axis=1
    )
    sums = nt(eye(2 * heads), sums, EXACT)
    x_gb, skip = sums[:heads], sums[heads:]
    put(small_ref, heads, {FIRST: first, X_GB: x_gb})
    own_ref[:heads, :] = rate * dt * first
    own_ref[heads : 2 * heads, :] = gate * (x_gb + rate * first)
    own_ref[2 * heads :, :] = skip
    grads_ref[:span, :] = nn(summed.astype(BF16), c_ref[...])
    grads_ref[span:, :] = nn(jnp.transpose(summed).astype(BF16), b_ref[...])


def neighbours(one_ref, two_ref):
    first = leads()

    def behind(part):
        return jnp.where(first, two_ref[part, :], one_ref[part, :])

    def ahead(part):
        return jnp.where(first, one_ref[part, :], two_ref[part, :])

    return behind, ahead


def wide(get, span, blocks):
    return jnp.concatenate(
        [get(slice(k * span, (k + 1) * span)).astype(BF16) for k in range(blocks)], axis=1
    )


def relay_terms(xp, gn, xs, gs, tot, scores, rows, push_ref, far_push_ref):
    gn_tot = (gn.astype(F32) * tot).astype(BF16)
    pull, push = nn(scores[0], xp), nn(scores[1], gn)
    far_pull, far_push = nn(scores[2], xp), nn(scores[3], gn_tot)
    push_ref[...] = push
    far_push_ref[...] = far_push
    products = (
        gs.astype(F32) * pull,
        xs.astype(F32) * push,
        gn_tot.astype(F32) * far_pull,
        xp.astype(F32) * far_push,
    )
    return [nt(rows, item.astype(BF16)) for item in products]


def maps_kernel(base, got_one_ref, got_two_ref, maps_ref):
    behind, ahead = neighbours(got_one_ref, got_two_ref)
    rows = maps_ref.shape[0] // 2
    maps_ref[:rows, :] = behind(slice(base, base + rows))
    maps_ref[rows:, :] = ahead(slice(base, base + rows))


def relay_first_kernel(
    got_one_ref, got_two_ref, maps_ref, other_ref, xs_ref, gs_ref, b_ref, c_ref, tot_ref, aux_ref,
    push_ref, far_push_ref, xp_ref, gn_ref, bp_ref, cn_ref, scores_ref, part_ref, weights_ref,
):
    span, features = xs_ref.shape
    heads = aux_ref.shape[0] // AUX
    width = tot_ref.shape[1] // heads
    blocks = features // LANES
    behind, ahead = neighbours(got_one_ref, got_two_ref)
    rows = span // 2
    lower = lax.axis_index("head") == 0

    def whole(part):
        one, two = maps_ref[part, :], other_ref[part, :]
        return jnp.concatenate(
            [jnp.where(lower, one, two), jnp.where(lower, two, one)], axis=0
        ).astype(BF16)

    xp, bp = wide(behind, span, blocks), whole(slice(0, rows))
    gn, cn = wide(ahead, span, blocks), whole(slice(rows, 2 * rows))
    base = blocks * span + rows
    weights_ref[: 2 * heads, :] = behind(slice(base, base + 2 * heads))
    weights_ref[2 * heads :, :] = ahead(slice(base, base + 2 * heads))
    b, c = b_ref[...], c_ref[...]
    scores = [item.astype(BF16) for item in (nt(c, bp), nt(b, cn), nt(cn, bp), nt(bp, cn))]
    part = slice(0, features)
    sums = relay_terms(
        xp, gn, xs_ref[...], gs_ref[...], tot_ref[:1, part], scores,
        head_rows(heads, width, part), push_ref, far_push_ref,
    )
    for index in range(4):
        scores_ref[index * span : (index + 1) * span, :] = scores[index]
        part_ref[index * heads : (index + 1) * heads, :] = sums[index]
    xp_ref[...] = xp
    gn_ref[...] = gn
    bp_ref[...] = bp
    cn_ref[...] = cn


def relay_kernel(
    got_one_ref, got_two_ref, xs_ref, gs_ref, tot_ref, aux_ref, scores_ref, part_ref, weights_ref,
    own_ref, red_ref, far_ref, push_ref, far_push_ref, xp_ref, gn_ref,
):
    span, features = xs_ref.shape
    heads = aux_ref.shape[0] // AUX
    total = tot_ref.shape[1]
    blocks = features // LANES
    behind, ahead = neighbours(got_one_ref, got_two_ref)
    xp, gn = wide(behind, span, blocks), wide(ahead, span, blocks)
    part = slice(total - features, total)
    sums = relay_terms(
        xp, gn, xs_ref[...], gs_ref[...], tot_ref[:1, part],
        [scores_ref[index * span : (index + 1) * span, :] for index in range(4)],
        head_rows(heads, total // heads, part), push_ref, far_push_ref,
    )
    z_own, w_own, z_far, w_far = (
        sums[index] + part_ref[index * heads : (index + 1) * heads, :] for index in range(4)
    )
    alpha_p, beta_p, alpha_n, beta_n = (
        weights_ref[index * heads : (index + 1) * heads, :] for index in range(4)
    )
    carried = jnp.sum(z_far, axis=1, keepdims=True)
    rate = take(aux_ref, RATE, heads)
    alog = (
        own_ref[:heads, :]
        + z_own * take(aux_ref, ALPHA_U, heads)
        + w_own * take(aux_ref, ALPHA_S, heads)
        + carried * rate * take(aux_ref, DT, heads)
        + z_far * alpha_n
        + w_far * alpha_p
    )
    bias = (
        own_ref[heads : 2 * heads, :]
        + z_own * take(aux_ref, BETA_U, heads)
        + w_own * take(aux_ref, BETA_S, heads)
        + carried * rate * take(aux_ref, GATE, heads)
        + z_far * beta_n
        + w_far * beta_p
    )
    stack = jnp.concatenate([alog, bias, own_ref[2 * heads :, :]], axis=0)
    red_ref[:, : 3 * heads] = nt(jnp.ones((8, span), F32), stack, EXACT)
    red_ref[:, 3 * heads :] = jnp.zeros((8, red_ref.shape[1] - 3 * heads), F32)
    put(far_ref, heads, {
        Z_OWN: z_own, W_OWN: w_own, Z_FAR: z_far, W_FAR: w_far,
        CARRIED: jnp.broadcast_to(carried, z_own.shape),
    })
    xp_ref[...] = xp
    gn_ref[...] = gn


def both(one_ref, two_ref):
    return jnp.concatenate([one_ref[...], two_ref[...]], axis=1)


def hops_kernel(
    xp0_ref, xp1_ref, gn0_ref, gn1_ref, bp_ref, cn_ref, aux_ref, far_ref, push0_ref, push1_ref,
    tot_ref, hop_one_ref, hop_two_ref,
):
    ctx = lax.axis_index("ctx")

    @pl.when((ctx > 0) & (ctx < lax.axis_size("ctx") - 1))
    def _():
        xp, gn, bp, cn = both(xp0_ref, xp1_ref), both(gn0_ref, gn1_ref), bp_ref[...], cn_ref[...]
        span, features = xp.shape
        blocks = features // LANES
        heads = far_ref.shape[0] // FAR
        gn_tot = (gn.astype(F32) * tot_ref[:1, :]).astype(BF16)
        grad_b_far = nn(nt(xp, gn_tot).astype(BF16), cn)
        grad_c_far = nn(nt(gn_tot, xp).astype(BF16), bp)
        half = span // 2
        base = blocks * half
        short = take(aux_ref, SHORT, heads)[:1, :] > 0.5

        def load(ref, grad, slot, heavy):
            if heavy:
                for block in range(blocks):
                    push_ref = (push0_ref, push1_ref)[block * 2 // blocks]
                    inner = (block % (blocks // 2)) * LANES
                    ref[block * half : (block + 1) * half, :] = jnp.where(
                        short,
                        push_ref[half:, inner : inner + LANES],
                        gn_tot[:half, block * LANES : (block + 1) * LANES].astype(F32),
                    )
                ref[base : base + half, :] = jnp.where(short, grad[half:], cn[:half].astype(F32))
            else:
                ref[:span, :] = grad
                ref[span : base + half, :] = jnp.zeros((base + half - span, LANES), F32)
            rest = base + half
            ref[rest : rest + heads, :] = take(far_ref, slot, heads)

        first = leads()

        @pl.when(first)
        def _():
            load(hop_one_ref, grad_c_far, Z_FAR, False)
            load(hop_two_ref, grad_b_far, W_FAR, True)

        @pl.when(jnp.logical_not(first))
        def _():
            load(hop_one_ref, grad_b_far, W_FAR, True)
            load(hop_two_ref, grad_c_far, Z_FAR, False)


def grads_kernel(
    xp0_ref, xp1_ref, gn0_ref, gn1_ref, bp_ref, cn_ref, xs0_ref, xs1_ref, gs0_ref, gs1_ref,
    grads_ref, sums_ref,
):
    xp, gn = both(xp0_ref, xp1_ref), both(gn0_ref, gn1_ref)
    xs, gs = both(xs0_ref, xs1_ref), both(gs0_ref, gs1_ref)
    span = xp.shape[0]
    sums_ref[:span, :] = grads_ref[:span, :] + nn(nt(xs, gn).astype(BF16), cn_ref[...])
    sums_ref[span:, :] = grads_ref[span:, :] + nn(nt(gs, xp).astype(BF16), bp_ref[...])


def ready_kernel(
    g_ref, aux_ref, gain_ref, gbl_ref, push0_ref, push1_ref, near_ref, weight_ref
):
    features = g_ref.shape[1]
    heads = aux_ref.shape[0] // AUX
    rows = head_rows(heads, features // heads)
    dt = take(aux_ref, DT, heads)
    weight = spread(dt * take(aux_ref, DOUT, heads), rows)
    weight_ref[...] = weight
    near_ref[...] = (
        spread(dt, rows) * gbl_ref[...]
        + weight * both(push0_ref, push1_ref)
        + gain_ref[:1, :] * g_ref[...].astype(F32)
    )


def final_kernel(
    far_one_ref, far_two_ref, b_ref, aux_ref, near_ref, weight_ref, small_ref, far_ref,
    gx_ref, gdt_ref,
):
    span, features = near_ref.shape
    heads = aux_ref.shape[0] // AUX
    blocks = features // LANES
    half = span // 2
    behind, ahead = neighbours(far_one_ref, far_two_ref)
    base = blocks * half
    short = take(aux_ref, SHORT, heads)[heads // 2 : heads // 2 + 1, :] > 0.5
    cn = ahead(slice(base, base + half)).astype(BF16)
    scores = nt(b_ref[...], cn).astype(BF16)
    parts = [ahead(slice(k * half, (k + 1) * half)) for k in range(blocks)]
    other = nn(scores, jnp.concatenate(parts, axis=1).astype(BF16))
    blank = jnp.zeros((half, LANES), F32)
    push = jnp.concatenate(
        [
            jnp.where(
                short,
                jnp.concatenate([blank, part], axis=0),
                other[:, k * LANES : (k + 1) * LANES],
            )
            for k, part in enumerate(parts)
        ],
        axis=1,
    )
    gx_ref[0] = (near_ref[...] + weight_ref[...] * push).astype(BF16)
    dt = take(aux_ref, DT, heads)
    gate = take(aux_ref, GATE, heads)
    rate = take(aux_ref, RATE, heads)
    inout = take(aux_ref, MASKS, heads)
    inward, outward = inout[:1, :], inout[heads // 2 : heads // 2 + 1, :]
    rest = base + half
    z = take(far_ref, Z_OWN, heads) + behind(slice(rest, rest + heads))
    w = take(far_ref, W_OWN, heads) + ahead(slice(rest, rest + heads))
    row, column = iota((span, span), 0), iota((span, span), 1)
    decay_grad = (
        take(small_ref, FIRST, heads)
        + inward * nn(z, (row >= column).astype(F32), EXACT)
        + outward * nn(w, (row < column).astype(F32), EXACT)
        + take(far_ref, CARRIED, heads)
    )
    x_gb = take(small_ref, X_GB, heads) + w / dt
    gdt_ref[0] = (x_gb + rate * decay_grad) * gate


def half_kernel(far_one_ref, far_two_ref, xs0_ref, xs1_ref, aux_ref, sums_ref, half_ref):
    xs = both(xs0_ref, xs1_ref)
    span, features = xs.shape
    heads = aux_ref.shape[0] // AUX
    half = span // 2
    blocks = features // LANES
    base = blocks * half
    behind, ahead = neighbours(far_one_ref, far_two_ref)
    short = take(aux_ref, SHORT, heads)[heads // 2 : heads // 2 + 1, :] > 0.5
    last = ahead(slice(base, base + half))
    gn = wide(ahead, half, blocks)
    grad = nn(nt(xs, gn).astype(BF16), last.astype(BF16))
    share = jnp.concatenate([jnp.zeros_like(last), last], axis=0)
    half_ref[:span, :] = sums_ref[:span, :] + jnp.where(short, share, grad)
    half_ref[span:, :] = sums_ref[span:, :] + behind(slice(0, span))


def close_kernel(
    red_ref, last_ref, half_ref, other_ref, b_ref, c_ref, alog_ref, bias_ref, skip_ref
):
    span = b_ref.shape[1]
    heads = alog_ref.shape[1]
    red = red_ref[:1, :] + last_ref[:1, :]
    alog_ref[...] = red[:, :heads]
    bias_ref[...] = red[:, heads : 2 * heads]
    skip_ref[...] = red[:, 2 * heads : 3 * heads]
    b_ref[0] = half_ref[:span, :] + other_ref[:span, :]
    c_ref[0] = half_ref[span:, :] + other_ref[span:, :]


def call(kernel, shapes, operands, raw=0, flops=0, scratch=()):
    def space(index):
        return pltpu.HBM if index < raw else pltpu.VMEM

    moved = sum(item.size * item.dtype.itemsize for item in operands) + sum(
        item.size * jnp.dtype(item.dtype).itemsize for item in shapes
    )
    return pl.pallas_call(
        kernel,
        out_shape=shapes,
        in_specs=[pl.BlockSpec(memory_space=space(index)) for index in range(len(operands))],
        out_specs=[pl.BlockSpec(memory_space=pltpu.VMEM)] * len(shapes),
        scratch_shapes=list(scratch),
        cost_estimate=pl.CostEstimate(flops=flops, bytes_accessed=moved, transcendentals=0),
        compiler_params=pltpu.CompilerParams(vmem_limit_bytes=VMEM_GRANT),
    )(
        *(
            pltpu.with_memory_space_constraint(item, pltpu.HBM) if index < raw else item
            for index, item in enumerate(operands)
        )
    )


def exchange(array, turn, senders):
    count = lax.axis_size("ctx")
    pairs = [(i, i + 1 if (i + turn) % 2 == 0 else i - 1) for i in range(count)]
    return lax.ppermute(
        array, "ctx", [(i, j) for i, j in pairs if 0 <= j < count and i in senders]
    )


def flip(array, axis, bit):
    return lax.ppermute(array, axis, [(i, i ^ bit) for i in range(lax.axis_size(axis))])


def near_local(inputs, dt_raw, dt_bias, a_log, b_in, c_in, skip_gain, grad_out, doc_lengths):
    _, span, features = inputs.shape
    heads = dt_bias.shape[0]
    state = b_in.shape[2]
    count = lax.axis_size("ctx")
    struct = jax.ShapeDtypeStruct
    bias, alog, skip = (item.reshape(1, heads) for item in (dt_bias, a_log, skip_gain))
    raw = jnp.swapaxes(dt_raw, 1, 2)
    split = features // 2
    sides = lax.axis_size("head")
    blocks = split // LANES * span
    base = 2 * blocks + span
    pay = struct((blocks + span // sides + 2 * heads, LANES), F32)
    pay_rest = struct((blocks, LANES), F32)
    full, low = struct((span, features), F32), struct((span, features), BF16)
    full_part, low_part = struct((span, split), F32), struct((span, split), BF16)
    line = struct((8, features), F32)
    square = struct((span, state), BF16)
    pair = struct((2 * span, state), F32)
    quad = struct((4 * heads, span), F32)
    one_row = pltpu.VMEM((1, heads), F32)
    pay_one, pay_two, aux, xs0, gs0, x, g, b, c = call(
        prep_kernel,
        (pay, pay, struct((AUX * heads, span), F32), low_part, low_part, low, low, square,
         square),
        (doc_lengths, raw, bias, alog, skip, inputs, grad_out, b_in, c_in),
        raw=9, flops=10**8,
        scratch=[pltpu.SMEM(doc_lengths.shape, jnp.int32), pltpu.VMEM((heads, span), F32),
                 one_row, one_row, one_row, pltpu.SemaphoreType.DMA((9,))],
    )
    got_two = exchange(pay_two, 1, range(count))
    got_one = exchange(pay_one, 0, range(count))
    pay_one, pay_two, xs1, gs1, tot, gain = call(
        rest_kernel, (pay_rest, pay_rest, low_part, low_part, line, line), (x, g, aux), flops=10**7
    )
    more_two = exchange(pay_two, 1, range(count))
    more_one = exchange(pay_one, 0, range(count))
    gb_local, small, grads, own = call(
        local_kernel,
        (full, struct((2 * heads, span), F32), pair, struct((3 * heads, span), F32)),
        (x, g, aux, b, c),
        flops=10**8,
    )
    maps = call(
        functools.partial(maps_kernel, blocks), (struct((2 * span // sides, state), F32),),
        (got_one, got_two), flops=10**5,
    )[0]
    other_maps = flip(maps, "head", 1)
    push0, far_push0, xp0, gn0, bp, cn, scores, part, weights = call(
        relay_first_kernel,
        (full_part, full_part, low_part, low_part, square, square,
         struct((4 * span, span), BF16), quad, quad),
        (got_one, got_two, maps, other_maps, xs0, gs0, b, c, tot, aux),
        flops=10**8,
    )
    red, far, push1, far_push1, xp1, gn1 = call(
        relay_kernel,
        (struct((8, LANES), F32), struct((FAR * heads, span), F32), full_part, full_part,
         low_part, low_part),
        (more_one, more_two, xs1, gs1, tot, aux, scores, part, weights, own),
        flops=10**8,
    )
    steps = []
    for axis in ("ctx", "dp"):
        bit = 1
        while bit < lax.axis_size(axis):
            steps.append((axis, bit))
            bit *= 2
    hop = struct((base // 2 + heads, LANES), F32)
    hop_one, hop_two = call(
        hops_kernel,
        (hop, hop),
        (xp0, xp1, gn0, gn1, bp, cn, aux, far, far_push0, far_push1, tot),
        flops=10**8,
    )
    sums = call(
        grads_kernel, (pair,), (xp0, xp1, gn0, gn1, bp, cn, xs0, xs1, gs0, gs1, grads), flops=10**8
    )[0]
    relays = range(1, count - 1)
    far_two = exchange(hop_two, 1, relays)
    far_one = exchange(hop_one, 0, relays)
    for axis, bit in steps[:-1]:
        red = red + flip(red, axis, bit)
    last_red = flip(red, *steps[-1])
    near, weight = call(
        ready_kernel, (full, full), (g, aux, gain, gb_local, push0, push1), flops=10**8
    )
    half = call(
        half_kernel, (pair,), (far_one, far_two, xs0, xs1, aux, sums),
        flops=10**7,
    )[0]
    grad_x, grad_dt = call(
        final_kernel,
        (struct((1, span, features), BF16), struct((1, heads, span), F32)),
        (far_one, far_two, b, aux, near, weight, small, far),
        flops=10**8,
    )
    other = flip(half, "head", 1)
    flat = struct((1, heads), F32)
    cube = struct((1, span, state), F32)
    b_total, c_total, alog_total, bias_total, skip_total = call(
        close_kernel, (cube, cube, flat, flat, flat), (red, last_red, half, other)
    )
    return (
        grad_x, jnp.swapaxes(grad_dt, 1, 2), b_total, c_total,
        alog_total.reshape(heads), bias_total.reshape(heads), skip_total.reshape(heads),
    )


def local(inputs, dt_raw, dt_bias, a_log, b_in, c_in, skip_gain, grad_out, doc_lengths):
    args = (inputs, dt_raw, dt_bias, a_log, b_in, c_in, skip_gain, grad_out, doc_lengths)
    shards = [lax.axis_size(axis) for axis in ("dp", "ctx")]
    near = (
        inputs.shape[1] == SPAN
        and shards[1] in (2, 4)
        and lax.axis_size("head") == 2
        and shards[0] & (shards[0] - 1) == 0
        and b_in.shape[2] == LANES
        and inputs.shape[2] % LANES == 0
        and dt_bias.shape[0] * 8 == LANES
    )
    if not near:
        return general_local(*args)
    return near_local(*args)


def solution(mesh):
    placed = (
        P("dp", "ctx", "head"),
        P("dp", "ctx", "head"),
        P("head"),
        P("head"),
        P("dp", "ctx", None),
        P("dp", "ctx", None),
        P("head"),
        P("dp", "ctx", "head"),
        P("dp", None),
    )
    return jax.shard_map(
        local,
        mesh=mesh,
        in_specs=placed,
        out_specs=(
            P("dp", "ctx", "head"),
            P("dp", "ctx", "head"),
            P("dp", "ctx", None),
            P("dp", "ctx", None),
            P("head"),
            P("head"),
            P("head"),
        ),
        check_vma=False,
    )
```

```python
import functools

import jax
import jax.numpy as jnp
from jax import lax
from jax.experimental import pallas as pl
from jax.experimental.pallas import tpu as pltpu
from jax.sharding import PartitionSpec as P


SPAN = 128
LANES = 128
VMEM_GRANT = 16 << 20
F32 = jnp.float32
BF16 = jnp.bfloat16
EXACT = lax.Precision.HIGHEST


def from_behind(array, axis, by):
    count = lax.axis_size(axis)
    pairs = [(i, i + by) for i in range(count) if 0 <= i + by < count]
    return lax.ppermute(array, axis, pairs)


def reverse_cumsum(values, along_axis):
    return jnp.flip(jnp.cumsum(jnp.flip(values, along_axis), axis=along_axis), along_axis)


def doc_index(positions, starts):
    return jnp.sum((starts[None, :] <= positions[:, None]).astype(jnp.int32), axis=1)


def vector_factors(decay_block, segment_block, previous_block):
    cumulative = jnp.cumsum(decay_block, axis=0)
    last_segment = segment_block[-1]
    mask_in = (segment_block == previous_block).astype(jnp.float32)
    mask_out = (segment_block == last_segment).astype(jnp.float32)
    factor_in = mask_in[:, None] * jnp.exp(cumulative)
    factor_out = mask_out[:, None] * jnp.exp(cumulative[-1][None, :] - cumulative)
    span_total = (last_segment == previous_block).astype(jnp.float32) * jnp.exp(cumulative[-1])
    return (cumulative, mask_in, mask_out, factor_in, factor_out, span_total)


def pair_factor(cumulative, segment_block):
    local_pos = jnp.arange(segment_block.shape[0], dtype=jnp.int32)
    allowed = (local_pos[:, None] >= local_pos[None, :]) & (
        segment_block[:, None] == segment_block[None, :]
    )
    spread = cumulative.T[:, :, None] - cumulative.T[:, None, :]
    return jnp.where(allowed[None], jnp.exp(jnp.where(allowed[None], spread, 0.0)), 0.0)


def first_pass(
    inputs_block,
    grads_block,
    b_block,
    c_block,
    step_block,
    decay_block,
    segment_block,
    previous_block,
):
    _, _, _, factor_in, factor_out, span_total = vector_factors(
        decay_block, segment_block, previous_block
    )
    scaled_in = (inputs_block * (factor_out * step_block)[:, :, None]).astype(jnp.bfloat16)
    scaled_grad = (grads_block * factor_in[:, :, None]).astype(jnp.bfloat16)
    state_part = jnp.einsum("shp,sn->hpn", scaled_in, b_block, preferred_element_type=jnp.float32)
    grad_part = jnp.einsum("uhp,un->hpn", scaled_grad, c_block, preferred_element_type=jnp.float32)
    return (span_total, state_part, grad_part)


def span_grads(
    inputs_block,
    grads_block,
    b_block,
    c_block,
    step_block,
    decay_block,
    segment_block,
    previous_block,
    preact_block,
    state_in,
    state_grad,
    decay_rate,
    skip_gain,
):
    cumulative, mask_in, mask_out, factor_in, factor_out, _ = vector_factors(
        decay_block, segment_block, previous_block
    )
    pair_decay = pair_factor(cumulative, segment_block)
    scores = jnp.einsum("un,sn->us", c_block, b_block, preferred_element_type=jnp.float32)
    cross_term = jnp.einsum(
        "uhp,shp->hus", grads_block, inputs_block, preferred_element_type=jnp.float32
    )
    masked = (pair_decay * scores[None]).astype(jnp.bfloat16)
    weighted = pair_decay * cross_term * step_block.T[:, None, :]
    summed = jnp.sum(weighted, axis=0).astype(jnp.bfloat16)
    products = weighted * scores[None]
    change = jnp.sum(products, axis=2) - jnp.sum(products, axis=1)
    first_term = reverse_cumsum(change, 1).T
    h_low = state_in.astype(jnp.bfloat16)
    e_low = state_grad.astype(jnp.bfloat16)
    along_b = jnp.einsum("tn,hpn->thp", b_block, e_low, preferred_element_type=jnp.float32)
    grad_b_prod = (
        jnp.einsum("hut,uhp->thp", masked, grads_block, preferred_element_type=jnp.float32)
        + factor_out[:, :, None] * along_b
    )
    grad_x = (step_block[:, :, None] * grad_b_prod + skip_gain[None, :, None] * grads_block).astype(
        jnp.bfloat16
    )
    x_state = jnp.einsum("thp,hpn->thn", inputs_block, e_low, preferred_element_type=jnp.float32)
    y_state = jnp.einsum("uhp,hpn->uhn", grads_block, h_low, preferred_element_type=jnp.float32)
    grad_b = jnp.einsum("us,un->sn", summed, c_block, preferred_element_type=jnp.float32) + jnp.sum(
        (step_block * factor_out)[:, :, None] * x_state, axis=1
    )
    grad_c = jnp.einsum("us,sn->un", summed, b_block, preferred_element_type=jnp.float32) + jnp.sum(
        factor_in[:, :, None] * y_state, axis=1
    )
    z_term = jnp.sum(y_state * c_block[:, None, :], axis=2)
    w_term = step_block * jnp.sum(x_state * b_block[:, None, :], axis=2)
    second_term = mask_in[:, None] * reverse_cumsum(factor_in * z_term, 0)
    carried = factor_out * w_term
    third_term = mask_out[:, None] * (jnp.cumsum(carried, axis=0) - carried)
    fourth_term = factor_out * factor_in * jnp.sum(state_grad * state_in, axis=(1, 2))[None, :]
    decay_grad = first_term + second_term + third_term + fourth_term
    x_dot_g = jnp.sum(inputs_block * grad_b_prod, axis=2)
    grad_dt = (x_dot_g + decay_rate[None, :] * decay_grad) * jax.nn.sigmoid(preact_block)
    grad_alog = jnp.sum(decay_grad * step_block, axis=0) * decay_rate
    grad_bias = jnp.sum(grad_dt, axis=0)
    grad_skip = jnp.einsum(
        "thp,thp->h", grads_block, inputs_block, preferred_element_type=jnp.float32
    )
    return (grad_x, grad_dt, grad_b, grad_c, grad_alog, grad_bias, grad_skip)


def local_link(running, pieces):
    decay_gain, held_state = running
    span_total, span_part = pieces
    return ((decay_gain * span_total, span_total[:, None, None] * held_state + span_part), running)


def link_maps(earlier, later):
    return (earlier[0] * later[0], later[0][:, None, None] * earlier[1] + later[1])


def doubling(element, reverse):
    axis_count = lax.axis_size("ctx")
    own_index = lax.axis_index("ctx")
    distances = [1] + [2**power for power in range((axis_count - 1).bit_length())]
    running = element
    for section_num, distance in enumerate(distances):
        shift_by = -distance if reverse else distance
        received = from_behind((running[0], running[1]), "ctx", shift_by)
        source = own_index - shift_by
        present = (source >= 0) & (source < axis_count)
        fixed = (jnp.where(present, received[0], 1.0), received[1])
        if section_num == 0:
            running = fixed
        else:
            running = link_maps(fixed, running)
    return running


def general_local(inputs, dt_raw, dt_bias, a_log, b_in, c_in, skip_gain, grad_out, doc_lengths):
    token_count = inputs.shape[1]
    head_count = dt_bias.shape[0]
    head_width = inputs.shape[2] // head_count
    state_size = b_in.shape[2]
    span_count = token_count // SPAN
    preact = dt_raw[0] + dt_bias[None, :]
    step_size = jax.nn.softplus(preact)
    decay_rate = -jnp.exp(a_log)
    log_decay = step_size * decay_rate[None, :]
    lengths = doc_lengths[0]
    starts = jnp.cumsum(lengths) - lengths
    positions = lax.axis_index("ctx") * token_count + jnp.arange(token_count, dtype=jnp.int32)
    segment = doc_index(positions, starts)
    previous = doc_index(positions[::SPAN] - 1, starts)
    shaped = (
        inputs[0].reshape(span_count, SPAN, head_count, head_width),
        grad_out[0].reshape(span_count, SPAN, head_count, head_width),
        b_in[0].reshape(span_count, SPAN, state_size),
        c_in[0].reshape(span_count, SPAN, state_size),
        step_size.reshape(span_count, SPAN, head_count),
        log_decay.reshape(span_count, SPAN, head_count),
        segment.reshape(span_count, SPAN),
        previous,
    )
    totals, state_parts, grad_parts = jax.vmap(first_pass)(*shaped)
    start_maps = (
        jnp.ones((head_count,), jnp.float32),
        jnp.zeros((head_count, head_width, state_size), jnp.float32),
    )
    forward_map, (gain_before, local_entry) = lax.scan(
        local_link, start_maps, (totals, state_parts)
    )
    backward_map, (gain_after, local_leave) = lax.scan(
        local_link, start_maps, (totals, grad_parts), reverse=True
    )
    entry_state = doubling(forward_map, False)[1]
    leave_state = doubling(backward_map, True)[1]
    entering = gain_before[:, :, None, None] * entry_state[None] + local_entry
    leaving = gain_after[:, :, None, None] * leave_state[None] + local_leave
    mapped = jax.vmap(span_grads, in_axes=(0, 0, 0, 0, 0, 0, 0, 0, 0, 0, 0, None, None))
    grad_x, grad_dt, grad_b, grad_c, grad_alog, grad_bias, grad_skip = mapped(
        *shaped,
        preact.reshape(span_count, SPAN, head_count),
        entering,
        leaving,
        decay_rate,
        skip_gain
    )
    b_total, c_total = lax.psum(
        (grad_b.reshape(token_count, state_size), grad_c.reshape(token_count, state_size)), "head"
    )
    alog_total, bias_total, skip_total = lax.psum(
        (jnp.sum(grad_alog, axis=0), jnp.sum(grad_bias, axis=0), jnp.sum(grad_skip, axis=0)),
        ("dp", "ctx"),
    )
    return (
        grad_x.reshape(1, token_count, head_count * head_width),
        grad_dt,
        b_total[None],
        c_total[None],
        alog_total,
        bias_total,
        skip_total,
    )


def dot(left, right, dims, precision=None):
    return lax.dot_general(
        left, right, (dims, ((), ())), precision=precision, preferred_element_type=F32
    )


def nn(left, right, precision=None):
    return dot(left, right, ((1,), (0,)), precision)


def nt(left, right, precision=None):
    return dot(left, right, ((1,), (1,)), precision)


def tn(left, right, precision=None):
    return dot(left, right, ((0,), (0,)), precision)


def iota(shape, axis):
    return lax.broadcasted_iota(jnp.int32, shape, axis)


def eye(size):
    return (iota((size, size), 0) == iota((size, size), 1)).astype(F32)


def head_rows(heads, width, chunk=slice(None)):
    begin, end, _ = chunk.indices(heads * width)
    shape = (heads, end - begin)
    start = iota(shape, 0) * width
    feature = iota(shape, 1) + begin
    return ((feature >= start) & (feature < start + width)).astype(BF16)


def head_columns(features, heads):
    width = features // heads
    start = iota((features, heads), 1) * width
    feature = iota((features, heads), 0)
    return ((feature >= start) & (feature < start + width)).astype(BF16)


def thirds(value):
    high = value.astype(BF16)
    rest = value - high.astype(F32)
    middle = rest.astype(BF16)
    low = (rest - middle.astype(F32)).astype(BF16)
    return jnp.concatenate([high, middle, low], axis=0)


def spread(factor, rows):
    return tn(thirds(factor), jnp.concatenate([rows] * 3, axis=0))


def spread_row(factor, features):
    heads = factor.shape[1]
    wide = jnp.broadcast_to(factor, (8, heads))
    high = wide.astype(BF16)
    rest = wide - high.astype(F32)
    middle = rest.astype(BF16)
    low = (rest - middle.astype(F32)).astype(BF16)
    rows = head_rows(heads, features // heads)
    return (nn(high, rows) + nn(middle, rows) + nn(low, rows))[:1]


def head_sum(values, columns):
    high = values.astype(BF16)
    low = (values - high.astype(F32)).astype(BF16)
    return nn(high, columns) + nn(low, columns)


def as_column(row):
    size = row.shape[1]
    return jnp.sum(jnp.where(eye(size) > 0, row, 0.0), axis=1, keepdims=True)


def as_row(column):
    size = column.shape[0]
    return jnp.sum(jnp.where(eye(size) > 0, column, 0.0), axis=0, keepdims=True)


def doc_of(lens_ref, positions):
    count = jnp.zeros(positions.shape, jnp.int32)
    start = jnp.int32(0)
    for index in range(lens_ref.shape[1]):
        count = count + (start <= positions).astype(jnp.int32)
        start = start + lens_ref[0, index]
    return count


def doc_scalar(lens_ref, position):
    count = jnp.int32(0)
    start = jnp.int32(0)
    for index in range(lens_ref.shape[1]):
        count = count + jnp.where(start <= position, 1, 0)
        start = start + lens_ref[0, index]
    return count


def doc_start(lens_ref, position):
    found = jnp.int32(0)
    start = jnp.int32(0)
    for index in range(lens_ref.shape[1]):
        found = jnp.where(start <= position, start, found)
        start = start + lens_ref[0, index]
    return found


def leads():
    return lax.rem(lax.axis_index("ctx"), 2) == 0


(
    DT, GATE, CUM, DIN, DOUT, TOT, RATE, DOC, MASKS, SHORT, GAIN
) = range(11)
AUX = 11
ALPHA_S, BETA_S, ALPHA_U, BETA_U = range(4)
FIRST, X_GB = range(2)
Z_OWN, W_OWN, Z_FAR, W_FAR, CARRIED = range(5)
FAR = 5


def take(ref, slot, heads):
    return ref[slot * heads : (slot + 1) * heads, :]


def put(ref, heads, values):
    for slot, value in values.items():
        ref[slot * heads : (slot + 1) * heads, :] = value


def halves(upper, lower, rows):
    width = upper.shape[1]
    return jnp.concatenate(
        [jnp.broadcast_to(item, (rows // 2, width)) for item in (upper, lower)], axis=0
    )


def fill(ref, scaled, *others):
    span = scaled.shape[0]
    base = 0
    for block in range(scaled.shape[1] // LANES):
        ref[base : base + span, :] = scaled[:, block * LANES : (block + 1) * LANES].astype(F32)
        base = base + span
    for part in others:
        ref[base : base + part.shape[0], :] = part
        base = base + part.shape[0]


def prep_kernel(
    lens_hbm, raw_hbm, bias_hbm, alog_hbm, skip_hbm, x_hbm, g_hbm, b_hbm, c_hbm,
    pay_one_ref, pay_two_ref, aux_ref, xs_ref, gs_ref, x_ref, g_ref, b_ref, c_ref, lens_ref, raw_ref, bias_ref, alog_ref, skip_ref, sems,
):
    moves = (
        (lens_hbm, lens_ref), (raw_hbm.at[0], raw_ref), (bias_hbm, bias_ref),
        (alog_hbm, alog_ref), (skip_hbm, skip_ref), (x_hbm.at[0], x_ref), (g_hbm.at[0], g_ref),
        (b_hbm.at[0], b_ref), (c_hbm.at[0], c_ref),
    )
    copies = [
        pltpu.make_async_copy(source, target, sems.at[index])
        for index, (source, target) in enumerate(moves)
    ]
    for copy in copies:
        copy.start()
    small, large = copies[:5], copies[5:]
    span, features = x_ref.shape
    heads = raw_ref.shape[0]
    row, column = iota((span, span), 0), iota((span, span), 1)
    upto = (row <= column).astype(F32)
    part = slice(0, features // 2)
    rows = head_rows(heads, features // heads, part)
    for copy in small[1:4]:
        copy.wait()
    preact = raw_ref[...] + as_column(bias_ref[...])
    dt = jnp.maximum(preact, 0.0) + jnp.log1p(jnp.exp(-jnp.abs(preact)))
    gate = 1.0 / (1.0 + jnp.exp(-preact))
    rate = -jnp.exp(as_column(alog_ref[...]))
    cum = nn(dt * rate, upto, EXACT)
    cum_last = cum[:, span - 1 : span]
    small[0].wait()
    small[4].wait()
    base = lax.axis_index("ctx") * span
    doc = doc_of(lens_ref, base + iota((1, span), 1))
    before = doc_scalar(lens_ref, base - 1)
    last = doc_scalar(lens_ref, base + span - 1)
    inward = (doc == before).astype(F32)
    outward = (doc == last).astype(F32)
    whole = jnp.where(last == before, 1.0, 0.0)
    short_before = jnp.where(base - doc_start(lens_ref, base - 1) <= span // 2, 1.0, 0.0)
    short_last = jnp.where(
        base + span - doc_start(lens_ref, base + span - 1) <= span // 2, 1.0, 0.0
    )
    din = inward * jnp.exp(cum)
    dout = outward * jnp.exp(cum_last - cum)
    put(aux_ref, heads, {
        DT: dt, GATE: gate, CUM: cum, DIN: din, DOUT: dout,
        TOT: jnp.broadcast_to(whole * jnp.exp(cum_last), dt.shape),
        GAIN: jnp.broadcast_to(as_column(skip_ref[...]), dt.shape),
        RATE: jnp.broadcast_to(rate, dt.shape), DOC: jnp.broadcast_to(doc.astype(F32), dt.shape),
        MASKS: halves(inward, outward, heads),
        SHORT: halves(jnp.full((1, span), short_before), jnp.full((1, span), short_last), heads),
    })
    x_factor, g_factor = spread(dout * dt, rows), spread(din, rows)
    for copy in large:
        copy.wait()
    xs = (x_ref[:, part].astype(F32) * x_factor).astype(BF16)
    gs = (g_ref[:, part].astype(F32) * g_factor).astype(BF16)
    xs_ref[...] = xs
    gs_ref[...] = gs
    first = leads()

    def mine(ref):
        rows = span // lax.axis_size("head")
        start = pl.multiple_of(lax.axis_index("head") * rows, rows)
        return ref[pl.ds(start, rows), :].astype(F32)

    @pl.when(first)
    def _():
        fill(pay_one_ref, xs, mine(b_ref))
        fill(pay_two_ref, gs, mine(c_ref))

    @pl.when(jnp.logical_not(first))
    def _():
        fill(pay_one_ref, gs, mine(c_ref))
        fill(pay_two_ref, xs, mine(b_ref))


def rest_kernel(
    x_ref, g_ref, aux_ref,
    pay_one_ref, pay_two_ref, xs_ref, gs_ref, tot_ref, gain_ref, weights_ref,
):
    span, features = x_ref.shape
    heads = aux_ref.shape[0] // AUX
    part = slice(features // 2, features)
    rows = head_rows(heads, features // heads, part)
    dout, dt = take(aux_ref, DOUT, heads), take(aux_ref, DT, heads)
    xs = (x_ref[:, part].astype(F32) * spread(dout * dt, rows)).astype(BF16)
    gs = (g_ref[:, part].astype(F32) * spread(take(aux_ref, DIN, heads), rows)).astype(BF16)
    xs_ref[...] = xs
    gs_ref[...] = gs
    for slot, ref in ((TOT, tot_ref), (GAIN, gain_ref)):
        row = as_row(take(aux_ref, slot, heads)[:, :1])
        ref[...] = jnp.broadcast_to(spread_row(row, features), ref.shape)
    row, column = iota((span, span), 0), iota((span, span), 1)
    gate, rate = take(aux_ref, GATE, heads), take(aux_ref, RATE, heads)
    inout = take(aux_ref, MASKS, heads)
    inward, outward = inout[:1, :], inout[heads // 2 : heads // 2 + 1, :]
    pair = jnp.concatenate([dt, gate], axis=0)
    seen = nn(pair * inward, (row <= column).astype(F32), EXACT)
    left = nn(pair * outward, (row > column).astype(F32), EXACT)
    alpha_s, beta_s = rate * left[:heads], rate * left[heads:] + gate / dt
    alpha_u, beta_u = rate * seen[:heads], rate * seen[heads:]
    put(weights_ref, heads, {ALPHA_S: alpha_s, BETA_S: beta_s, ALPHA_U: alpha_u, BETA_U: beta_u})
    first = leads()

    @pl.when(first)
    def _():
        fill(pay_one_ref, xs, alpha_s, beta_s)
        fill(pay_two_ref, gs, alpha_u, beta_u)

    @pl.when(jnp.logical_not(first))
    def _():
        fill(pay_one_ref, gs, alpha_u, beta_u)
        fill(pay_two_ref, xs, alpha_s, beta_s)


def local_kernel(
    x_ref, g_ref, aux_ref, b_ref, c_ref, gb_ref, small_ref, grads_ref, own_ref
):
    span, features = x_ref.shape
    heads = aux_ref.shape[0] // AUX
    width = features // heads
    row, column = iota((span, span), 0), iota((span, span), 1)
    dt = take(aux_ref, DT, heads)
    gate = take(aux_ref, GATE, heads)
    cum = take(aux_ref, CUM, heads)
    rate = take(aux_ref, RATE, heads)
    doc = take(aux_ref, DOC, heads)
    upright = nt(eye(span), jnp.concatenate([dt, cum, doc], axis=0), EXACT)
    doc_s = upright[:, 2 * heads : 2 * heads + 1]
    closed = jnp.where((column >= row) & (jnp.abs(doc_s - doc[:1, :]) < 0.5), 0.0, -1e30)
    scores = nt(b_ref[...], c_ref[...])
    summed = jnp.zeros((span, span), F32)
    lane = iota((span, heads), 1)
    from_s = jnp.zeros((span, heads), F32)
    to_u = []
    for pair in range(0, heads, 2):
        outs = []
        for head in (pair, pair + 1):
            part = slice(head * width, (head + 1) * width)
            g_head, x_head = g_ref[:, part], x_ref[:, part]
            cross = nt(x_head, g_head)
            cum_s = upright[:, heads + head : heads + head + 1]
            decay = jnp.exp(cum[head : head + 1, :] - cum_s + closed)
            masked = decay * scores
            weighted = decay * cross * upright[:, head : head + 1]
            summed = summed + weighted
            product = weighted * scores
            from_s = jnp.where(lane == head, jnp.sum(product, axis=1, keepdims=True), from_s)
            to_u.append(jnp.sum(product, axis=0, keepdims=True))
            outs.append(nn(masked.astype(BF16), g_head))
        gb_ref[:, pair * width : (pair + 2) * width] = jnp.concatenate(outs, axis=1)
    onward = (row >= column).astype(F32)
    turn = eye(heads)
    change = jnp.concatenate(to_u, axis=0) - nt(turn, from_s, EXACT)
    first = nn(change, onward, EXACT)
    columns = head_columns(features, heads)
    x_wide = x_ref[...].astype(F32)
    sums = jnp.concatenate(
        [head_sum(x_wide * gb_ref[...], columns),
         head_sum(x_wide * g_ref[...].astype(F32), columns)], axis=1
    )
    sums = nt(eye(2 * heads), sums, EXACT)
    x_gb, skip = sums[:heads], sums[heads:]
    put(small_ref, heads, {FIRST: first, X_GB: x_gb})
    own_ref[:heads, :] = rate * dt * first
    own_ref[heads : 2 * heads, :] = gate * (x_gb + rate * first)
    own_ref[2 * heads :, :] = skip
    grads_ref[:span, :] = nn(summed.astype(BF16), c_ref[...])
    grads_ref[span:, :] = nn(jnp.transpose(summed).astype(BF16), b_ref[...])


def neighbours(one_ref, two_ref):
    first = leads()

    def behind(part):
        return jnp.where(first, two_ref[part, :], one_ref[part, :])

    def ahead(part):
        return jnp.where(first, one_ref[part, :], two_ref[part, :])

    return behind, ahead


def wide(get, span, blocks):
    return jnp.concatenate(
        [get(slice(k * span, (k + 1) * span)).astype(BF16) for k in range(blocks)], axis=1
    )


def relay_terms(xp, gn, xs, gs, tot, scores, rows, push_ref, far_push_ref):
    gn_tot = (gn.astype(F32) * tot).astype(BF16)
    pull, push = nn(scores[0], xp), nn(scores[1], gn)
    far_pull, far_push = nn(scores[2], xp), nn(scores[3], gn_tot)
    push_ref[...] = push
    far_push_ref[...] = far_push
    products = (
        gs.astype(F32) * pull,
        xs.astype(F32) * push,
        gn_tot.astype(F32) * far_pull,
        xp.astype(F32) * far_push,
    )
    return [nt(rows, item.astype(BF16)) for item in products], gn_tot


def maps_kernel(base, got_one_ref, got_two_ref, maps_ref):
    behind, ahead = neighbours(got_one_ref, got_two_ref)
    rows = maps_ref.shape[0] // 2
    maps_ref[:rows, :] = behind(slice(base, base + rows))
    maps_ref[rows:, :] = ahead(slice(base, base + rows))


def relay_first_kernel(
    got_one_ref, got_two_ref, maps_ref, other_ref, xs_ref, gs_ref, b_ref, c_ref, tot_ref, aux_ref,
    push_ref, far_push_ref, xp_ref, gn_ref, bp_ref, cn_ref, scores_ref, part_ref, cross_b_ref, cross_c_ref,
):
    span, features = xs_ref.shape
    heads = aux_ref.shape[0] // AUX
    width = tot_ref.shape[1] // heads
    blocks = features // LANES
    behind, ahead = neighbours(got_one_ref, got_two_ref)
    rows = span // 2
    lower = lax.axis_index("head") == 0

    def whole(part):
        one, two = maps_ref[part, :], other_ref[part, :]
        return jnp.concatenate(
            [jnp.where(lower, one, two), jnp.where(lower, two, one)], axis=0
        ).astype(BF16)

    xp, bp = wide(behind, span, blocks), whole(slice(0, rows))
    gn, cn = wide(ahead, span, blocks), whole(slice(rows, 2 * rows))
    b, c = b_ref[...], c_ref[...]
    scores = [item.astype(BF16) for item in (nt(c, bp), nt(b, cn), nt(cn, bp), nt(bp, cn))]
    part = slice(0, features)
    sums, gn_tot = relay_terms(
        xp, gn, xs_ref[...], gs_ref[...], tot_ref[:1, part], scores,
        head_rows(heads, width, part), push_ref, far_push_ref,
    )
    for index in range(4):
        scores_ref[index * span : (index + 1) * span, :] = scores[index]
        part_ref[index * heads : (index + 1) * heads, :] = sums[index]
    cross_b_ref[...] = nt(xp, gn_tot)
    cross_c_ref[...] = nt(gn_tot, xp)
    xp_ref[...] = xp
    gn_ref[...] = gn
    bp_ref[...] = bp
    cn_ref[...] = cn


def relay_kernel(
    got_one_ref, got_two_ref, xs_ref, gs_ref, tot_ref, aux_ref, scores_ref, part_ref, weights_ref,
    own_ref, red_ref, far_ref, push_ref, far_push_ref, xp_ref, gn_ref,
):
    span, features = xs_ref.shape
    heads = aux_ref.shape[0] // AUX
    total = tot_ref.shape[1]
    blocks = features // LANES
    behind, ahead = neighbours(got_one_ref, got_two_ref)
    xp, gn = wide(behind, span, blocks), wide(ahead, span, blocks)
    part = slice(total - features, total)
    sums, _ = relay_terms(
        xp, gn, xs_ref[...], gs_ref[...], tot_ref[:1, part],
        [scores_ref[index * span : (index + 1) * span, :] for index in range(4)],
        head_rows(heads, total // heads, part), push_ref, far_push_ref,
    )
    z_own, w_own, z_far, w_far = (
        sums[index] + part_ref[index * heads : (index + 1) * heads, :] for index in range(4)
    )
    base = blocks * span
    alpha_p, beta_p = behind(slice(base, base + heads)), behind(slice(base + heads, base + 2 * heads))
    alpha_n, beta_n = ahead(slice(base, base + heads)), ahead(slice(base + heads, base + 2 * heads))
    carried = jnp.sum(z_far, axis=1, keepdims=True)
    rate = take(aux_ref, RATE, heads)
    alog = (
        own_ref[:heads, :]
        + z_own * take(weights_ref, ALPHA_U, heads)
        + w_own * take(weights_ref, ALPHA_S, heads)
        + carried * rate * take(aux_ref, DT, heads)
        + z_far * alpha_n
        + w_far * alpha_p
    )
    bias = (
        own_ref[heads : 2 * heads, :]
        + z_own * take(weights_ref, BETA_U, heads)
        + w_own * take(weights_ref, BETA_S, heads)
        + carried * rate * take(aux_ref, GATE, heads)
        + z_far * beta_n
        + w_far * beta_p
    )
    stack = jnp.concatenate([alog, bias, own_ref[2 * heads :, :]], axis=0)
    red_ref[:, : 3 * heads] = nt(jnp.ones((8, span), F32), stack, EXACT)[:1]
    red_ref[:, 3 * heads :] = jnp.zeros((1, red_ref.shape[1] - 3 * heads), F32)
    put(far_ref, heads, {
        Z_OWN: z_own, W_OWN: w_own, Z_FAR: z_far, W_FAR: w_far,
        CARRIED: jnp.broadcast_to(carried, z_own.shape),
    })
    xp_ref[...] = xp
    gn_ref[...] = gn


def both(one_ref, two_ref):
    return jnp.concatenate([one_ref[...], two_ref[...]], axis=1)


def hops_kernel(
    xp1_ref, gn0_ref, gn1_ref, bp_ref, cn_ref, aux_ref, far_ref, push0_ref, push1_ref, tot_ref,
    cross_b_ref, cross_c_ref, hop_one_ref, hop_two_ref,
):
    ctx = lax.axis_index("ctx")

    @pl.when((ctx > 0) & (ctx < lax.axis_size("ctx") - 1))
    def _():
        bp, cn, xp = bp_ref[...], cn_ref[...], xp1_ref[...]
        span, split = xp.shape
        features = tot_ref.shape[1]
        blocks = features // LANES
        heads = far_ref.shape[0] // FAR
        scaled = (gn1_ref[...].astype(F32) * tot_ref[:1, features - split :]).astype(BF16)
        grad_b_far = nn((cross_b_ref[...] + nt(xp, scaled)).astype(BF16), cn)
        grad_c_far = nn((cross_c_ref[...] + nt(scaled, xp)).astype(BF16), bp)
        half = span // 2
        base = blocks * half
        short = take(aux_ref, SHORT, heads)[:1, :] > 0.5

        def load(ref, grad, slot, heavy):
            if heavy:
                for block in range(blocks):
                    late = block * 2 // blocks
                    push_ref, g_ref = ((push0_ref, gn0_ref), (push1_ref, gn1_ref))[late]
                    inner = (block % (blocks // 2)) * LANES
                    tot = tot_ref[:1, block * LANES : (block + 1) * LANES]
                    g_rows = g_ref[:half, inner : inner + LANES].astype(F32)
                    ref[block * half : (block + 1) * half, :] = jnp.where(
                        short,
                        push_ref[half:, inner : inner + LANES],
                        (g_rows * tot).astype(BF16).astype(F32),
                    )
                ref[base : base + half, :] = jnp.where(short, grad[half:], cn[:half].astype(F32))
            else:
                ref[:span, :] = grad
                ref[span : base + half, :] = jnp.zeros((base + half - span, LANES), F32)
            rest = base + half
            ref[rest : rest + heads, :] = take(far_ref, slot, heads)

        first = leads()

        @pl.when(first)
        def _():
            load(hop_one_ref, grad_c_far, Z_FAR, False)
            load(hop_two_ref, grad_b_far, W_FAR, True)

        @pl.when(jnp.logical_not(first))
        def _():
            load(hop_one_ref, grad_b_far, W_FAR, True)
            load(hop_two_ref, grad_c_far, Z_FAR, False)


def grads_kernel(
    xp0_ref, xp1_ref, gn0_ref, gn1_ref, bp_ref, cn_ref, xs0_ref, xs1_ref, gs0_ref, gs1_ref,
    grads_ref, sums_ref,
):
    xp, gn = both(xp0_ref, xp1_ref), both(gn0_ref, gn1_ref)
    xs, gs = both(xs0_ref, xs1_ref), both(gs0_ref, gs1_ref)
    span = xp.shape[0]
    sums_ref[:span, :] = grads_ref[:span, :] + nn(nt(xs, gn).astype(BF16), cn_ref[...])
    sums_ref[span:, :] = grads_ref[span:, :] + nn(nt(gs, xp).astype(BF16), bp_ref[...])


def ready_kernel(
    g_ref, aux_ref, gain_ref, gbl_ref, push0_ref, push1_ref, near_ref, weight_ref
):
    features = g_ref.shape[1]
    heads = aux_ref.shape[0] // AUX
    rows = head_rows(heads, features // heads)
    dt = take(aux_ref, DT, heads)
    weight = spread(dt * take(aux_ref, DOUT, heads), rows)
    weight_ref[...] = weight
    near_ref[...] = (
        spread(dt, rows) * gbl_ref[...]
        + weight * both(push0_ref, push1_ref)
        + gain_ref[:1, :] * g_ref[...].astype(F32)
    )


def final_kernel(
    far_one_ref, far_two_ref, b_ref, aux_ref, near_ref, weight_ref, small_ref, far_ref,
    gx_ref, gdt_ref,
):
    span, features = near_ref.shape
    heads = aux_ref.shape[0] // AUX
    blocks = features // LANES
    half = span // 2
    behind, ahead = neighbours(far_one_ref, far_two_ref)
    base = blocks * half
    short = take(aux_ref, SHORT, heads)[heads // 2 : heads // 2 + 1, :] > 0.5
    cn = ahead(slice(base, base + half)).astype(BF16)
    scores = nt(b_ref[...], cn).astype(BF16)
    parts = [ahead(slice(k * half, (k + 1) * half)) for k in range(blocks)]
    other = nn(scores, jnp.concatenate(parts, axis=1).astype(BF16))
    blank = jnp.zeros((half, LANES), F32)
    push = jnp.concatenate(
        [
            jnp.where(
                short,
                jnp.concatenate([blank, part], axis=0),
                other[:, k * LANES : (k + 1) * LANES],
            )
            for k, part in enumerate(parts)
        ],
        axis=1,
    )
    gx_ref[0] = (near_ref[...] + weight_ref[...] * push).astype(BF16)
    dt = take(aux_ref, DT, heads)
    gate = take(aux_ref, GATE, heads)
    rate = take(aux_ref, RATE, heads)
    inout = take(aux_ref, MASKS, heads)
    inward, outward = inout[:1, :], inout[heads // 2 : heads // 2 + 1, :]
    rest = base + half
    z = take(far_ref, Z_OWN, heads) + behind(slice(rest, rest + heads))
    w = take(far_ref, W_OWN, heads) + ahead(slice(rest, rest + heads))
    row, column = iota((span, span), 0), iota((span, span), 1)
    decay_grad = (
        take(small_ref, FIRST, heads)
        + inward * nn(z, (row >= column).astype(F32), EXACT)
        + outward * nn(w, (row < column).astype(F32), EXACT)
        + take(far_ref, CARRIED, heads)
    )
    x_gb = take(small_ref, X_GB, heads) + w / dt
    gdt_ref[0] = (x_gb + rate * decay_grad) * gate


def half_kernel(far_one_ref, far_two_ref, xs0_ref, xs1_ref, aux_ref, sums_ref, half_ref):
    xs = both(xs0_ref, xs1_ref)
    span, features = xs.shape
    heads = aux_ref.shape[0] // AUX
    half = span // 2
    blocks = features // LANES
    base = blocks * half
    behind, ahead = neighbours(far_one_ref, far_two_ref)
    short = take(aux_ref, SHORT, heads)[heads // 2 : heads // 2 + 1, :] > 0.5
    last = ahead(slice(base, base + half))
    gn = wide(ahead, half, blocks)
    grad = nn(nt(xs, gn).astype(BF16), last.astype(BF16))
    share = jnp.concatenate([jnp.zeros_like(last), last], axis=0)
    half_ref[:span, :] = sums_ref[:span, :] + jnp.where(short, share, grad)
    half_ref[span:, :] = sums_ref[span:, :] + behind(slice(0, span))


def close_kernel(
    red_ref, last_ref, half_ref, other_ref, b_ref, c_ref, alog_ref, bias_ref, skip_ref
):
    span = b_ref.shape[1]
    heads = alog_ref.shape[1]
    red = red_ref[:1, :] + last_ref[:1, :]
    alog_ref[...] = red[:, :heads]
    bias_ref[...] = red[:, heads : 2 * heads]
    skip_ref[...] = red[:, 2 * heads : 3 * heads]
    b_ref[0] = half_ref[:span, :] + other_ref[:span, :]
    c_ref[0] = half_ref[span:, :] + other_ref[span:, :]


def call(kernel, shapes, operands, raw=0, flops=0, scratch=()):
    def space(index):
        return pltpu.HBM if index < raw else pltpu.VMEM

    moved = sum(item.size * item.dtype.itemsize for item in operands) + sum(
        item.size * jnp.dtype(item.dtype).itemsize for item in shapes
    )
    return pl.pallas_call(
        kernel,
        out_shape=shapes,
        in_specs=[pl.BlockSpec(memory_space=space(index)) for index in range(len(operands))],
        out_specs=[pl.BlockSpec(memory_space=pltpu.VMEM)] * len(shapes),
        scratch_shapes=list(scratch),
        cost_estimate=pl.CostEstimate(flops=flops, bytes_accessed=moved, transcendentals=0),
        compiler_params=pltpu.CompilerParams(vmem_limit_bytes=VMEM_GRANT),
    )(
        *(
            pltpu.with_memory_space_constraint(item, pltpu.HBM) if index < raw else item
            for index, item in enumerate(operands)
        )
    )


def exchange(array, turn, senders):
    count = lax.axis_size("ctx")
    pairs = [(i, i + 1 if (i + turn) % 2 == 0 else i - 1) for i in range(count)]
    return lax.ppermute(
        array, "ctx", [(i, j) for i, j in pairs if 0 <= j < count and i in senders]
    )


def flip(array, axis, bit):
    return lax.ppermute(array, axis, [(i, i ^ bit) for i in range(lax.axis_size(axis))])


def near_local(inputs, dt_raw, dt_bias, a_log, b_in, c_in, skip_gain, grad_out, doc_lengths):
    _, span, features = inputs.shape
    heads = dt_bias.shape[0]
    state = b_in.shape[2]
    count = lax.axis_size("ctx")
    struct = jax.ShapeDtypeStruct
    bias, alog, skip = (item.reshape(1, heads) for item in (dt_bias, a_log, skip_gain))
    raw = jnp.swapaxes(dt_raw, 1, 2)
    split = features // 2
    sides = lax.axis_size("head")
    blocks = split // LANES * span
    base = 2 * blocks + span
    pay = struct((blocks + span // sides, LANES), F32)
    pay_rest = struct((blocks + 2 * heads, LANES), F32)
    full, low = struct((span, features), F32), struct((span, features), BF16)
    full_part, low_part = struct((span, split), F32), struct((span, split), BF16)
    line = struct((8, features), F32)
    square = struct((span, state), BF16)
    pair = struct((2 * span, state), F32)
    tile = struct((span, span), F32)
    quad = struct((4 * heads, span), F32)
    one_row = pltpu.VMEM((1, heads), F32)
    pay_one, pay_two, aux, xs0, gs0, x, g, b, c = call(
        prep_kernel,
        (pay, pay, struct((AUX * heads, span), F32), low_part, low_part, low, low, square,
         square),
        (doc_lengths, raw, bias, alog, skip, inputs, grad_out, b_in, c_in),
        raw=9, flops=10**8,
        scratch=[pltpu.SMEM(doc_lengths.shape, jnp.int32), pltpu.VMEM((heads, span), F32),
                 one_row, one_row, one_row, pltpu.SemaphoreType.DMA((9,))],
    )
    got_two = exchange(pay_two, 1, range(count))
    got_one = exchange(pay_one, 0, range(count))
    pay_one, pay_two, xs1, gs1, tot, gain, weights = call(
        rest_kernel,
        (pay_rest, pay_rest, low_part, low_part, line, line, quad),
        (x, g, aux),
        flops=10**7,
    )
    more_two = exchange(pay_two, 1, range(count))
    more_one = exchange(pay_one, 0, range(count))
    gb_local, small, grads, own = call(
        local_kernel,
        (full, struct((2 * heads, span), F32), pair, struct((3 * heads, span), F32)),
        (x, g, aux, b, c),
        flops=10**8,
    )
    maps = call(
        functools.partial(maps_kernel, blocks), (struct((2 * span // sides, state), F32),),
        (got_one, got_two), flops=10**5,
    )[0]
    other_maps = flip(maps, "head", 1)
    push0, far_push0, xp0, gn0, bp, cn, scores, part, cross_b, cross_c = call(
        relay_first_kernel,
        (full_part, full_part, low_part, low_part, square, square,
         struct((4 * span, span), BF16), quad, tile, tile),
        (got_one, got_two, maps, other_maps, xs0, gs0, b, c, tot, aux),
        flops=10**8,
    )
    red, far, push1, far_push1, xp1, gn1 = call(
        relay_kernel,
        (struct((1, LANES), F32), struct((FAR * heads, span), F32), full_part, full_part,
         low_part, low_part),
        (more_one, more_two, xs1, gs1, tot, aux, scores, part, weights, own),
        flops=10**8,
    )
    steps = []
    for axis in ("ctx", "dp"):
        bit = 1
        while bit < lax.axis_size(axis):
            steps.append((axis, bit))
            bit *= 2
    hop = struct((base // 2 + heads, LANES), F32)
    hop_one, hop_two = call(
        hops_kernel,
        (hop, hop),
        (xp1, gn0, gn1, bp, cn, aux, far, far_push0, far_push1, tot, cross_b, cross_c),
        flops=10**8,
    )
    sums = call(
        grads_kernel, (pair,), (xp0, xp1, gn0, gn1, bp, cn, xs0, xs1, gs0, gs1, grads), flops=10**8
    )[0]
    relays = range(1, count - 1)
    far_two = exchange(hop_two, 1, relays)
    far_one = exchange(hop_one, 0, relays)
    for axis, bit in steps[:-1]:
        red = red + flip(red, axis, bit)
    last_red = flip(red, *steps[-1])
    near, weight = call(
        ready_kernel, (full, full), (g, aux, gain, gb_local, push0, push1), flops=10**8
    )
    half = call(
        half_kernel, (pair,), (far_one, far_two, xs0, xs1, aux, sums),
        flops=10**7,
    )[0]
    grad_x, grad_dt = call(
        final_kernel,
        (struct((1, span, features), BF16), struct((1, heads, span), F32)),
        (far_one, far_two, b, aux, near, weight, small, far),
        flops=10**8,
    )
    other = flip(half, "head", 1)
    flat = struct((1, heads), F32)
    cube = struct((1, span, state), F32)
    b_total, c_total, alog_total, bias_total, skip_total = call(
        close_kernel, (cube, cube, flat, flat, flat), (red, last_red, half, other)
    )
    return (
        grad_x, jnp.swapaxes(grad_dt, 1, 2), b_total, c_total,
        alog_total.reshape(heads), bias_total.reshape(heads), skip_total.reshape(heads),
    )


def local(inputs, dt_raw, dt_bias, a_log, b_in, c_in, skip_gain, grad_out, doc_lengths):
    args = (inputs, dt_raw, dt_bias, a_log, b_in, c_in, skip_gain, grad_out, doc_lengths)
    shards = [lax.axis_size(axis) for axis in ("dp", "ctx")]
    near = (
        inputs.shape[1] == SPAN
        and shards[1] in (2, 4)
        and lax.axis_size("head") == 2
        and shards[0] & (shards[0] - 1) == 0
        and b_in.shape[2] == LANES
        and inputs.shape[2] % LANES == 0
        and dt_bias.shape[0] * 8 == LANES
    )
    if not near:
        return general_local(*args)
    return near_local(*args)


def solution(mesh):
    placed = (
        P("dp", "ctx", "head"),
        P("dp", "ctx", "head"),
        P("head"),
        P("head"),
        P("dp", "ctx", None),
        P("dp", "ctx", None),
        P("head"),
        P("dp", "ctx", "head"),
        P("dp", None),
    )
    return jax.shard_map(
        local,
        mesh=mesh,
        in_specs=placed,
        out_specs=(
            P("dp", "ctx", "head"),
            P("dp", "ctx", "head"),
            P("dp", "ctx", None),
            P("dp", "ctx", None),
            P("head"),
            P("head"),
            P("head"),
        ),
        check_vma=False,
    )
```
